32 devices in a mesh: blk: 4 (over y, x), ulys: 8 (over z, core).
Axes of the slice: x: 2, y: 2, z: 4, core: 2. Of those that a mesh axis runs over, the one named last changes fastest.
Arguments:
- mamba_input: bfloat16 [8192, 16384], P(('blk', 'ulys')), may hold values from -6 to 6
- gate_input: bfloat16 [8192, 16384], P(('blk', 'ulys')), may hold values from -6 to 6
- delta_low: bfloat16 [8192, 512], P(('blk', 'ulys')), may hold values from -12 to 12
- state_mixers: bfloat16 [8192, 32], P(('blk', 'ulys')), may hold values from -6 to 6
- conv_weight: bfloat16 [4, 16384], P(None, 'ulys'), may hold values from -3 to 3
- conv_bias: float32 [16384], P('ulys'), may hold values from -3 to 3
- delta_weight: bfloat16 [512, 16384], P(None, 'ulys'), may hold values from -0.25 to 0.25
- delta_bias: float32 [16384], P('ulys'), may hold values from -12 to -2.3
- decay_log: float32 [16, 16384], P(None, 'ulys'), may hold values from -1 to 2.7
- skip_gain: float32 [16384], P('ulys'), may hold values from 0.5 to 1.5
- queries: bfloat16 [8192, 4096], P(('blk', 'ulys')), may hold values from -4.5 to 4.5
- key_rows: bfloat16 [8192, 1024], P(('blk', 'ulys')), may hold values from -4.5 to 4.5
- value_rows: bfloat16 [8192, 1024], P(('blk', 'ulys')), may hold values from -6 to 6
- span_order: int32 [8], replicated, may hold values from 0 to 7, as said below
Outputs:
- mamba_output: bfloat16 [8192, 16384], P(('blk', 'ulys'))
- attention_output: bfloat16 [8192, 4096], P(('blk', 'ulys'))
The draws below stay inside these ranges and needn't reach their ends.
Inputs may be any that keep to these rules, and one draw needn't show every extreme that they name: `span_order`: device i of blk holds stored blocks 2i and 2i+1, whose sequence places are p and 7 - p for some p below 4, in either order; every sequence place appears once; the device holding places 0 and 7 and the device holding places 1 and 6 are 2 apart along blk.
All inputs are finite; a program needn't handle non-finite values.
Results may differ from the reference program's by a relative error of at most 0.013.
Values may be sent and summed in bfloat16 or wider, within the bound.
No kernel may reach another device: no remote copies, remote signals or barrier semaphores. Data moves between devices by JAX's collectives and lax.ppermute only.
A program may use at most 192 MiB of HBM per device.

```python
import jax
import jax.numpy as jnp
from jax import lax

INNER = 16384
STATE = 16
DT_RANK = 512
CONV = 4
KVH = 8
HD = 128
QH = 32
SPAN = 1024
NCH = 8
SEQUENCE_TOKENS = 8192


def draw_span_order(key, part):
    pair_count = NCH // 2
    firsts = jax.random.permutation(jax.random.fold_in(key, 21), pair_count).astype(jnp.int32)
    slots = jnp.arange(pair_count, dtype=jnp.int32)
    holder_zero = jnp.sum(jnp.where(firsts == 0, slots, 0)).astype(jnp.int32)
    holder_one = jnp.sum(jnp.where(firsts == 1, slots, 0)).astype(jnp.int32)
    target = ((holder_zero + pair_count // 2) % pair_count).astype(jnp.int32)
    at_target = jnp.sum(jnp.where(slots == target, firsts, 0)).astype(jnp.int32)
    firsts = jnp.where(slots == target, 1, jnp.where(slots == holder_one, at_target, firsts)).astype(jnp.int32)
    flips = jax.random.randint(jax.random.fold_in(key, 22), (pair_count,), 0, 2).astype(jnp.int32)
    lower = jnp.where(flips == 1, NCH - 1 - firsts, firsts)
    upper = NCH - 1 - lower
    return jnp.stack([lower, upper], axis=1).reshape(NCH).astype(jnp.int32)


def draw_delta_low(key, part):
    base_key = jax.random.fold_in(key, 11)
    pick_key = jax.random.fold_in(key, 12)
    starting_rows = jax.random.normal(base_key, (SEQUENCE_TOKENS, DT_RANK), jnp.float32)
    selected_rows = jax.random.randint(pick_key, (8,), 0, SEQUENCE_TOKENS)
    token_group = jnp.any(jnp.arange(SEQUENCE_TOKENS)[:, None] == selected_rows[None, :], axis=1)
    return jnp.clip(jnp.where(token_group[:, None], 5.0 * starting_rows, starting_rows), -12.0, 12.0).astype(jnp.bfloat16)


def draw_delta_bias(key, part):
    return jax.random.uniform(key, (INNER,), jnp.float32, -11.5, -2.3)


def drawn_rows(key, col_count):
    return jnp.clip(jax.random.normal(key, (SEQUENCE_TOKENS, col_count), jnp.float32), -4.5, 4.5)


def draw_queries(key, part):
    starting_rows = drawn_rows(jax.random.fold_in(key, 1), QH * HD)
    return starting_rows.astype(jnp.bfloat16)


def draw_key_rows(key, part):
    starting_rows = drawn_rows(jax.random.fold_in(key, 2), KVH * HD)
    return starting_rows.astype(jnp.bfloat16)


def block_levels(stream_key, extent, pieces, least, top_value):
    gain = 1.0
    for dim, shards_of in pieces:
        draws = jax.random.uniform(jax.random.fold_in(jax.random.fold_in(stream_key, 6), dim), (shards_of,), jnp.float32, least / len(pieces), top_value / len(pieces))
        gain = gain * jnp.repeat(jnp.exp(draws), extent[dim] // shards_of).reshape((-1,) + (1,) * (len(extent) - 1 - dim))
    return gain


def bell_draw(own_key, dims, width, most, shards=(), kind=jnp.bfloat16):
    array = jax.random.normal(own_key, dims, jnp.float32) * width
    if len(shards) > 0:
        array = block_levels(own_key, dims, shards, -0.22, 0.18) * array
    return jnp.clip(array, min=-most, max=most).astype(kind)


def setup_inputs(seed: int = 0) -> dict:
    key_of = jax.random.split(jax.random.key(seed), 15)
    mamba_input = bell_draw(key_of[0], (SEQUENCE_TOKENS, INNER), 1.0, 6.0, ((0, 32),))
    gate_input = bell_draw(key_of[1], (SEQUENCE_TOKENS, INNER), 1.0, 6.0, ((0, 32),))
    delta_low = draw_delta_low(jax.random.fold_in(key_of[14], 71), 0)
    state_mixers = bell_draw(key_of[3], (SEQUENCE_TOKENS, 2 * STATE), 1.0, 6.0, ((0, 32),))
    conv_weight = bell_draw(key_of[4], (CONV, INNER), CONV ** -0.5, 3.0, ((1, 8),))
    conv_bias = bell_draw(key_of[5], (INNER,), 0.5, 3.0, ((0, 8),), jnp.float32)
    delta_weight = bell_draw(key_of[6], (DT_RANK, INNER), DT_RANK ** -0.5, 0.25, ((1, 8),))
    delta_bias = draw_delta_bias(jax.random.fold_in(key_of[14], 71), 0)
    decay_log = jnp.clip(-1.0 + 3.7 * jax.random.uniform(key_of[8], (STATE, INNER), jnp.float32) ** block_levels(key_of[8], (STATE, INNER), ((1, 8),), -0.2, 0.2), -1.0, 2.7)
    skip_gain = jnp.clip(0.5 + 1.0 * jax.random.uniform(key_of[9], (INNER,), jnp.float32) ** block_levels(key_of[9], (INNER,), ((0, 8),), -0.2, 0.2), 0.5, 1.5)
    queries = draw_queries(jax.random.fold_in(key_of[14], 71), 0)
    key_rows = draw_key_rows(jax.random.fold_in(key_of[14], 71), 0)
    value_rows = bell_draw(key_of[12], (SEQUENCE_TOKENS, KVH * HD), 1.0, 6.0, ((0, 32),))
    span_order = draw_span_order(jax.random.fold_in(key_of[14], 71), 0)
    return dict(mamba_input=mamba_input, gate_input=gate_input, delta_low=delta_low, state_mixers=state_mixers, conv_weight=conv_weight, conv_bias=conv_bias, delta_weight=delta_weight, delta_bias=delta_bias, decay_log=decay_log, skip_gain=skip_gain, queries=queries, key_rows=key_rows, value_rows=value_rows, span_order=span_order)


NEG_LARGE = -1.0e30


def block_holder(span_order):
    places = jnp.arange(NCH, dtype=jnp.int32)
    matches = span_order[None, :] == places[:, None]
    return jnp.sum(jnp.where(matches, places[None, :], 0), axis=1).astype(jnp.int32)


def into_sequence(stored, holder):
    blocks = stored.reshape(NCH, SPAN, stored.shape[1])
    return jnp.take(blocks, holder, axis=0).reshape(stored.shape)


def into_storage(ordered, span_order):
    blocks = ordered.reshape(NCH, SPAN, ordered.shape[1])
    return jnp.take(blocks, span_order, axis=0).reshape(ordered.shape)


def split_columns(matrix, block_count):
    return matrix.reshape(matrix.shape[0], block_count, matrix.shape[1] // block_count).transpose(1, 0, 2)


def mamba_columns(columns, low_seq, mixers_seq):
    input_cols, gate_cols, conv_cols, conv_shift, delta_cols, delta_shift, decay_cols, skip_cols = columns
    col_count = input_cols.shape[1]
    padded = jnp.concatenate([jnp.zeros((CONV - 1, col_count), jnp.float32), input_cols.astype(jnp.float32)], axis=0)
    mixed_sum = jnp.broadcast_to(conv_shift[None, :], (SEQUENCE_TOKENS, col_count))
    for offset in range(CONV):
        mixed_sum = mixed_sum + conv_cols[offset].astype(jnp.float32)[None, :] * padded[offset:offset + SEQUENCE_TOKENS]
    driven = jax.nn.silu(mixed_sum)
    delta_step = jax.nn.softplus(jnp.dot(low_seq, delta_cols, preferred_element_type=jnp.float32) + delta_shift[None, :])
    decay_rates = -jnp.exp(decay_cols)
    inject = mixers_seq[:, :STATE].astype(jnp.float32)
    readout_matrix = mixers_seq[:, STATE:].astype(jnp.float32)

    def advance(hidden, inputs):
        delta_now, driven_now, inject_now, readout_now = inputs
        hidden = jnp.exp(delta_now[None, :] * decay_rates) * hidden + (delta_now * driven_now)[None, :] * inject_now[:, None]
        return hidden, jnp.sum(readout_now[:, None] * hidden, axis=0)

    _, scanned = lax.scan(advance, jnp.zeros((STATE, col_count), jnp.float32), (delta_step, driven, inject, readout_matrix))
    ssm_out = (scanned + skip_cols[None, :] * driven).astype(jnp.bfloat16)
    return (lax.optimization_barrier(ssm_out).astype(jnp.float32) * jax.nn.silu(gate_cols.astype(jnp.float32))).astype(jnp.bfloat16)


def attention_sequence(query_seq, key_seq, value_seq):
    group_size = QH // KVH
    query_block = min(SEQUENCE_TOKENS, 1024)
    score_scale = HD ** -0.5
    key_pos = jnp.arange(SEQUENCE_TOKENS, dtype=jnp.int32)

    def one_head(head_index):
        query_head = lax.dynamic_slice_in_dim(query_seq, head_index * HD, HD, 1)
        key_head = lax.dynamic_slice_in_dim(key_seq, (head_index // group_size) * HD, HD, 1)
        value_head = lax.dynamic_slice_in_dim(value_seq, (head_index // group_size) * HD, HD, 1)

        def one_block(block_index):
            query_part = lax.dynamic_slice_in_dim(query_head, block_index * query_block, query_block, 0)
            scores = jnp.dot(query_part, key_head.T, preferred_element_type=jnp.float32) * score_scale
            query_pos = block_index * query_block + jnp.arange(query_block, dtype=jnp.int32)
            allowed = key_pos[None, :] <= query_pos[:, None]
            row_top = jnp.max(jnp.where(allowed, scores, NEG_LARGE), axis=1, keepdims=True)
            weights = jnp.where(allowed, jnp.exp(scores - row_top), 0.0)
            row_total = jnp.sum(weights, axis=1, keepdims=True)
            return jnp.dot(weights.astype(jnp.bfloat16), value_head, preferred_element_type=jnp.float32) / row_total

        return lax.map(one_block, jnp.arange(SEQUENCE_TOKENS // query_block, dtype=jnp.int32))

    heads_out = lax.map(one_head, jnp.arange(QH, dtype=jnp.int32))
    return heads_out.reshape(QH, SEQUENCE_TOKENS, HD).transpose(1, 0, 2).reshape(SEQUENCE_TOKENS, QH * HD).astype(jnp.bfloat16)


def reference(mamba_input, gate_input, delta_low, state_mixers, conv_weight, conv_bias, delta_weight, delta_bias, decay_log, skip_gain, queries, key_rows, value_rows, span_order):
    holder = block_holder(span_order)
    block_cols = min(INNER, 2048)
    block_count = INNER // block_cols
    columns = (
        split_columns(into_sequence(mamba_input, holder), block_count),
        split_columns(into_sequence(gate_input, holder), block_count),
        split_columns(conv_weight, block_count),
        conv_bias.reshape(block_count, block_cols),
        split_columns(delta_weight, block_count),
        delta_bias.reshape(block_count, block_cols),
        split_columns(decay_log, block_count),
        skip_gain.reshape(block_count, block_cols),
    )
    low_seq = into_sequence(delta_low, holder)
    mixers_seq = into_sequence(state_mixers, holder)
    gated = lax.map(lambda part_cols: mamba_columns(part_cols, low_seq, mixers_seq), columns)
    mamba_seq = gated.transpose(1, 0, 2).reshape(SEQUENCE_TOKENS, INNER)
    attention_seq = attention_sequence(into_sequence(queries, holder), into_sequence(key_rows, holder), into_sequence(value_rows, holder))
    return into_storage(mamba_seq, span_order), into_storage(attention_seq, span_order)
```

```python
import functools

import jax
import jax.numpy as jnp
from jax import lax
from jax.experimental import pallas as pl
from jax.experimental.pallas import tpu as pltpu
from jax.sharding import Mesh
from jax.sharding import PartitionSpec as P

STATE = 16
CONV = 4
HD = 128
SPAN = 1024
LANES = 128
PAIR = 2
GROUP = 16
NEG_LARGE = -1e30
LOG2E = 1.4426950408889634
PARAM_ROWS = 24
VMEM_LIMIT = 56 * 1024 * 1024


def softplus(x):
    e = jnp.exp(-jnp.abs(x))
    return jnp.maximum(x, 0.0) + jnp.log1p(e)


def scan_kernel(
    core_ref, own_ref, other_ref, halo_ref, low_ref, weight_ref, param_ref, inject_ref, read_ref,
    delta_ref, y_ref, end_ref, total_ref,
    x_scr, driven_scr, push_scr, hist_scr,
):
    core = core_ref[0]
    tokens, cols = delta_ref.shape
    half = tokens // 2
    depth = low_ref.shape[1]
    x_scr[0:8, :] = halo_ref[...].astype(jnp.float32)
    x_scr[pl.ds(pl.multiple_of(8 + core * half, 8), half), :] = own_ref[...].astype(jnp.float32)
    x_scr[pl.ds(pl.multiple_of(8 + (1 - core) * half, 8), half), :] = other_ref[...].astype(jnp.float32)
    params = param_ref[0]
    weight = weight_ref[...].reshape(depth, cols)
    delta_ref[...] = jnp.dot(low_ref[...], weight, preferred_element_type=jnp.float32)
    rows = 16
    taps = [params[STATE + k : STATE + k + 1, :] for k in range(CONV)]
    conv_bias = params[STATE + CONV : STATE + CONV + 1, :]
    delta_bias = params[STATE + CONV + 1 : STATE + CONV + 2, :]
    skip = params[STATE + CONV + 2 : STATE + CONV + 3, :]

    def prepare(step, carry):
        first = pl.multiple_of(step * rows, rows)
        window = x_scr[pl.ds(first, rows + 8), :]
        mixed = jnp.broadcast_to(conv_bias, (rows, cols))
        for k in range(CONV):
            lo = 8 - (CONV - 1) + k
            mixed = mixed + taps[k] * window[lo : lo + rows, :]
        driven = mixed * jax.nn.sigmoid(mixed)
        delta = softplus(delta_ref[pl.ds(first, rows), :] + delta_bias)
        delta_ref[pl.ds(first, rows), :] = delta
        driven_scr[pl.ds(first, rows), :] = driven * skip
        push_scr[pl.ds(first, rows), :] = driven * delta
        return carry + delta.reshape(rows // 8, 8, cols).sum(axis=0)

    total = lax.fori_loop(0, tokens // rows, prepare, jnp.zeros((8, cols), jnp.float32))
    total_ref[...] = jnp.broadcast_to(jnp.sum(total, axis=0, keepdims=True), (8, cols))
    rates = -LOG2E * jnp.exp(params[:STATE, :])
    reps = cols // LANES

    def step16(group, hidden):
        base = pl.multiple_of(group * GROUP, GROUP)
        for i in range(GROUP):
            delta = delta_ref[pl.ds(base + i, 1), :]
            push = push_scr[pl.ds(base + i, 1), :]
            inject = inject_ref[pl.ds(pl.multiple_of((base + i) * STATE, STATE), STATE), :]
            inject = jnp.concatenate([inject] * reps, axis=1)
            hidden = jnp.exp2(delta * rates) * hidden + push * inject
            hist_scr[i * STATE : (i + 1) * STATE, :] = hidden.astype(jnp.bfloat16)
        read = read_ref[pl.ds(base, GROUP), :]
        out = jnp.dot(read, hist_scr[...], preferred_element_type=jnp.float32)
        y_ref[pl.ds(base, GROUP), :] = (out + driven_scr[pl.ds(base, GROUP), :]).astype(y_ref.dtype)
        return hidden

    end_ref[...] = lax.fori_loop(
        0, tokens // GROUP, step16, jnp.zeros((STATE, cols), jnp.float32)
    )


def correct_kernel(
    core_ref, delta_ref, y_ref, enter_ref, param_ref, read_ref, own_gate_ref, other_gate_ref,
    mine_ref, theirs_ref, hist_scr, out_scr,
):
    core = core_ref[0]
    tokens, cols = delta_ref.shape
    half = tokens // 2
    rates = -LOG2E * jnp.exp(param_ref[0][:STATE, :])
    enter = enter_ref[...].astype(jnp.float32)

    def step16(group, elapsed):
        base = pl.multiple_of(group * GROUP, GROUP)
        for i in range(GROUP):
            elapsed = elapsed + delta_ref[pl.ds(base + i, 1), :]
            carried = jnp.exp2(elapsed * rates) * enter
            hist_scr[i * STATE : (i + 1) * STATE, :] = carried.astype(jnp.bfloat16)
        read = read_ref[pl.ds(base, GROUP), :]
        out = jnp.dot(read, hist_scr[...], preferred_element_type=jnp.float32)
        total = out + y_ref[pl.ds(base, GROUP), :].astype(jnp.float32)
        out_scr[pl.ds(base, GROUP), :] = total.astype(jnp.bfloat16).astype(jnp.float32)
        return elapsed

    lax.fori_loop(0, tokens // GROUP, step16, jnp.zeros((1, cols), jnp.float32))
    rows = 16

    def gated(gate_ref, dest_ref, offset):
        def body(step, carry):
            first = pl.multiple_of(step * rows, rows)
            gate = gate_ref[pl.ds(first, rows), :].astype(jnp.float32)
            value = out_scr[pl.ds(pl.multiple_of(offset + first, 8), rows), :]
            dest_ref[pl.ds(first, rows), :] = (
                value * (gate * jax.nn.sigmoid(gate))
            ).astype(dest_ref.dtype)
            return carry

        lax.fori_loop(0, half // rows, body, 0)

    gated(own_gate_ref, mine_ref, core * half)
    gated(other_gate_ref, theirs_ref, (1 - core) * half)


def combine_kernel(order_ref, end_ref, total_ref, rate_ref, enter_ref):
    chunks = end_ref.shape[0]
    rates = rate_ref[...]

    def body(place, state):
        chunk = order_ref[place]
        enter_ref[chunk] = state.astype(enter_ref.dtype)
        total = total_ref[chunk]
        return jnp.exp2(total[0:1, :] * rates) * state + end_ref[chunk]

    lax.fori_loop(0, chunks, body, jnp.zeros(rates.shape, jnp.float32))


def flash_kernel(
    side_ref, block_ref, diag_ref, first_ref, last_ref, q_ref, kv_ref, out_ref,
    max_scr, acc_scr, value_scr, *, heads, rows,
):
    step = pl.program_id(0)
    scale = LOG2E * HD ** (-0.5)
    span = kv_ref.shape[0]
    value_scr[:, :HD] = kv_ref[:, HD:]
    value_scr[:, HD:] = jnp.ones((span, HD), jnp.bfloat16)

    @pl.when(first_ref[step] == 1)
    def _():
        max_scr[...] = jnp.full(max_scr.shape, NEG_LARGE, jnp.float32)
        acc_scr[...] = jnp.zeros(acc_scr.shape, jnp.float32)

    def absorb(head, row, key_count, masked):
        q = q_ref[row : row + rows, head * HD : (head + 1) * HD]
        scores = lax.dot_general(
            q, kv_ref[:key_count, :HD], (((1,), (1,)), ((), ())),
            preferred_element_type=jnp.float32,
        ) * scale
        if masked:
            query_at = lax.broadcasted_iota(jnp.int32, scores.shape, 0) + row
            key_at = lax.broadcasted_iota(jnp.int32, scores.shape, 1)
            scores = jnp.where(key_at <= query_at, scores, NEG_LARGE)
        at = slice(head * span + row, head * span + row + rows)
        old_max = max_scr[at, :]
        new_max = jnp.maximum(old_max, jnp.max(scores, axis=1, keepdims=True))
        weights = jnp.exp2(scores - new_max[:, :1]).astype(jnp.bfloat16)
        shrink = jnp.exp2(old_max - new_max)
        acc_scr[at, :] = acc_scr[at, :] * shrink[:, :1] + jnp.dot(
            weights, value_scr[:key_count, :], preferred_element_type=jnp.float32
        )
        max_scr[at, :] = new_max

    @pl.when(diag_ref[step] == 0)
    def _():
        for head in range(heads):
            for row in range(0, span, rows):
                absorb(head, row, span, False)

    @pl.when(diag_ref[step] == 1)
    def _():
        for head in range(heads):
            for row in range(0, span, rows):
                absorb(head, row, row + rows, True)

    @pl.when(last_ref[step] == 1)
    def _():
        for head in range(heads):
            for row in range(0, span, rows):
                at = slice(head * span + row, head * span + row + rows)
                out_ref[row : row + rows, head * HD : (head + 1) * HD] = (
                    acc_scr[at, :HD] / acc_scr[at, HD:]
                ).astype(out_ref.dtype)


def run_scan(core, x_own, x_other, halo, low, weight, params, inject, read, col_block):
    half, _ = x_own.shape
    tokens = 2 * half
    cols = x_other.shape[1]
    shard_cols = params.shape[2]
    per_shard = shard_cols // col_block
    parts, _, part_rows, _ = weight.shape
    blocks = cols // col_block

    def own_map(j, core_ref):
        return (0, (PAIR * (j // per_shard) + core_ref[0]) * per_shard + j % per_shard)

    def plain(j, core_ref):
        return (0, j)

    def fixed(j, core_ref):
        return (0, 0)

    grid_spec = pltpu.PrefetchScalarGridSpec(
        num_scalar_prefetch=1,
        grid=(blocks,),
        in_specs=[
            pl.BlockSpec((half, col_block), own_map),
            pl.BlockSpec((half, col_block), plain),
            pl.BlockSpec((8, col_block), plain),
            pl.BlockSpec(low.shape, fixed, pipeline_mode=pl.Buffered(1)),
            pl.BlockSpec(
                (parts, 1, part_rows, col_block),
                lambda j, core_ref: (0, j // per_shard, 0, j % per_shard),
            ),
            pl.BlockSpec(
                (1, PARAM_ROWS, col_block),
                lambda j, core_ref: (j // per_shard, 0, j % per_shard),
            ),
            pl.BlockSpec(inject.shape, fixed, pipeline_mode=pl.Buffered(1)),
            pl.BlockSpec(read.shape, fixed, pipeline_mode=pl.Buffered(1)),
        ],
        out_specs=[
            pl.BlockSpec((tokens, col_block), plain),
            pl.BlockSpec((tokens, col_block), plain),
            pl.BlockSpec((STATE, col_block), plain),
            pl.BlockSpec((8, col_block), plain),
        ],
        scratch_shapes=[
            pltpu.VMEM((tokens + 8, col_block), jnp.float32),
            pltpu.VMEM((tokens, col_block), jnp.float32),
            pltpu.VMEM((tokens, col_block), jnp.float32),
            pltpu.VMEM((GROUP * STATE, col_block), jnp.bfloat16),
        ],
    )
    return pl.pallas_call(
        scan_kernel,
        grid_spec=grid_spec,
        out_shape=[
            jax.ShapeDtypeStruct((tokens, cols), jnp.float32),
            jax.ShapeDtypeStruct((tokens, cols), jnp.bfloat16),
            jax.ShapeDtypeStruct((STATE, cols), jnp.float32),
            jax.ShapeDtypeStruct((8, cols), jnp.float32),
        ],
        compiler_params=pltpu.CompilerParams(vmem_limit_bytes=VMEM_LIMIT),
        name="token_scan",
    )(core, x_own, x_other, halo, low, weight, params, inject, read)


def run_correct(core, delta, y, enter, params, read, gate_own, gate_other, col_block):
    tokens, cols = delta.shape
    half = tokens // 2
    shard_cols = params.shape[2]
    per_shard = shard_cols // col_block
    blocks = cols // col_block

    def own_map(j, core_ref):
        return (0, (PAIR * (j // per_shard) + core_ref[0]) * per_shard + j % per_shard)

    def plain(j, core_ref):
        return (0, j)

    grid_spec = pltpu.PrefetchScalarGridSpec(
        num_scalar_prefetch=1,
        grid=(blocks,),
        in_specs=[
            pl.BlockSpec((tokens, col_block), plain),
            pl.BlockSpec((tokens, col_block), plain),
            pl.BlockSpec((STATE, col_block), plain),
            pl.BlockSpec(
                (1, PARAM_ROWS, col_block),
                lambda j, core_ref: (j // per_shard, 0, j % per_shard),
            ),
            pl.BlockSpec(read.shape, lambda j, core_ref: (0, 0), pipeline_mode=pl.Buffered(1)),
            pl.BlockSpec((half, col_block), own_map),
            pl.BlockSpec((half, col_block), plain),
        ],
        out_specs=[
            pl.BlockSpec((half, col_block), plain),
            pl.BlockSpec((half, col_block), plain),
        ],
        scratch_shapes=[
            pltpu.VMEM((GROUP * STATE, col_block), jnp.bfloat16),
            pltpu.VMEM((tokens, col_block), jnp.float32),
        ],
    )
    return pl.pallas_call(
        correct_kernel,
        grid_spec=grid_spec,
        out_shape=[jax.ShapeDtypeStruct((half, cols), jnp.bfloat16)] * 2,
        compiler_params=pltpu.CompilerParams(vmem_limit_bytes=VMEM_LIMIT),
        name="state_correction",
    )(core, delta, y, enter, params, read, gate_own, gate_other)


def run_combine(order, ends, totals, rates):
    chunks, _, cols = ends.shape
    return pl.pallas_call(
        combine_kernel,
        grid_spec=pltpu.PrefetchScalarGridSpec(
            num_scalar_prefetch=1,
            grid=(1,),
            in_specs=[
                pl.BlockSpec(ends.shape, lambda i, o: (0, 0, 0)),
                pl.BlockSpec(totals.shape, lambda i, o: (0, 0, 0)),
                pl.BlockSpec(rates.shape, lambda i, o: (0, 0)),
            ],
            out_specs=pl.BlockSpec(ends.shape, lambda i, o: (0, 0, 0)),
        ),
        out_shape=jax.ShapeDtypeStruct(ends.shape, jnp.bfloat16),
        compiler_params=pltpu.CompilerParams(vmem_limit_bytes=VMEM_LIMIT),
        name="state_combine",
    )(order, ends, totals, rates)


def run_flash(tables, q, kv, rows=512):
    tokens, width = q.shape
    heads = width // HD
    steps = tables[0].shape[0]

    def q_map(s, side, block, diag, first, last):
        return (side[s], 0)

    def kv_map(s, side, block, diag, first, last):
        return (block[s], 0)

    return pl.pallas_call(
        functools.partial(flash_kernel, heads=heads, rows=rows),
        grid_spec=pltpu.PrefetchScalarGridSpec(
            num_scalar_prefetch=5,
            grid=(steps,),
            in_specs=[pl.BlockSpec((SPAN, width), q_map), pl.BlockSpec((SPAN, 2 * HD), kv_map)],
            out_specs=pl.BlockSpec((SPAN, width), q_map),
            scratch_shapes=[
                pltpu.VMEM((heads * SPAN, HD), jnp.float32),
                pltpu.VMEM((heads * SPAN, 2 * HD), jnp.float32),
                pltpu.VMEM((SPAN, 2 * HD), jnp.bfloat16),
            ],
        ),
        out_shape=jax.ShapeDtypeStruct(q.shape, jnp.bfloat16),
        compiler_params=pltpu.CompilerParams(vmem_limit_bytes=VMEM_LIMIT),
        name="causal_attention",
    )(*tables, q, kv)


def flash_tables(span_order, my_blocks):
    block_total = span_order.shape[0]
    places = jnp.arange(block_total, dtype=jnp.int32)
    holder = jnp.sum(jnp.where(span_order[None, :] == places[:, None], places[None, :], 0), axis=1)
    steps = jnp.arange(block_total + 1, dtype=jnp.int32)
    first_count = my_blocks[0] + 1
    side = (steps >= first_count).astype(jnp.int32)
    place = jnp.where(side == 1, steps - first_count, steps)
    limit = jnp.where(side == 1, my_blocks[1], my_blocks[0])
    block = jnp.sum(jnp.where(places[None, :] == place[:, None], holder[None, :], 0), axis=1)
    last = (place == limit).astype(jnp.int32)
    first = (place == 0).astype(jnp.int32)
    return (side, block.astype(jnp.int32), last, first, last)


def local(
    mamba_input, gate_input, delta_low, state_mixers, conv_weight, conv_bias, delta_weight,
    delta_bias, decay_log, skip_gain, queries, key_rows, value_rows, span_order,
):
    blk = lax.axis_index("blk")
    chip = lax.axis_index("chip")
    core = lax.axis_index("core")
    blk_count = lax.axis_size("blk")
    chip_count = lax.axis_size("chip")
    ulys = ("chip", "core")
    ulys_count = chip_count * PAIR
    chunks = blk_count * chip_count
    block_total = span_order.shape[0]
    half, inner = mamba_input.shape
    tokens = PAIR * half
    shard_cols = delta_weight.shape[1]
    cols = inner // PAIR
    col_block = min(1024, shard_cols)
    swap = [(0, 1), (1, 0)]
    core_arr = core.astype(jnp.int32).reshape(1)
    my_blocks = lax.dynamic_slice_in_dim(span_order, 2 * blk, 2, 0)

    kv_heads = key_rows.shape[1] // HD
    repeat = ulys_count // kv_heads
    kv_rows = jnp.stack(
        [key_rows.reshape(half, kv_heads, HD), value_rows.reshape(half, kv_heads, HD)], axis=2
    )
    kv_rows = jnp.broadcast_to(
        kv_rows[:, :, None], (half, kv_heads, repeat, 2, HD)
    ).reshape(half, ulys_count * 2 * HD)
    kv_local = lax.all_to_all(kv_rows, ulys, split_axis=1, concat_axis=0, tiled=True)
    kv_all = lax.all_gather(kv_local, "blk", axis=0, tiled=True)
    q_local = lax.all_to_all(queries, ulys, split_axis=1, concat_axis=0, tiled=True)

    depth = delta_weight.shape[0]
    part_rows = depth // blk_count
    part = lax.dynamic_slice_in_dim(delta_weight, blk * part_rows, part_rows, 0)
    weight = lax.all_gather(part, ("blk", "chip"), axis=0, tiled=False)
    weight = weight.reshape(blk_count, chip_count, part_rows, shard_cols)
    packed = jnp.concatenate(
        [
            decay_log,
            conv_weight.astype(jnp.float32),
            conv_bias[None],
            delta_bias[None],
            skip_gain[None],
            jnp.zeros((1, shard_cols), jnp.float32),
        ],
        axis=0,
    )
    params = lax.all_gather(packed, "chip", axis=0, tiled=False)

    def other_half(array):
        parts = array.reshape(half, chip_count, PAIR, shard_cols)
        picked = lax.dynamic_index_in_dim(parts, 1 - core, 2, False)
        return picked.reshape(half, cols)

    x_other = lax.ppermute(other_half(mamba_input), "core", swap)
    gate_other = lax.ppermute(other_half(gate_input), "core", swap)
    low = lax.all_gather(delta_low, "core", axis=0, tiled=True)
    mixers = lax.all_gather(state_mixers, "core", axis=0, tiled=True)
    inject = jnp.broadcast_to(
        mixers[:, :STATE].astype(jnp.float32).reshape(tokens * STATE, 1), (tokens * STATE, LANES)
    )
    same = jnp.arange(tokens, dtype=jnp.int32)[:, None] % GROUP == jnp.arange(GROUP, dtype=jnp.int32)
    read = jnp.where(
        same[:, :, None], mixers[:, None, STATE:], jnp.zeros((), jnp.bfloat16)
    ).reshape(tokens, GROUP * STATE)

    per_block = SPAN // tokens
    chunk_ids = jnp.arange(chunks, dtype=jnp.int32)
    stored = chunk_ids // per_block
    block_ids = jnp.arange(block_total, dtype=jnp.int32)
    block_pos = jnp.sum(
        jnp.where(stored[:, None] == block_ids[None, :], span_order[None, :], 0), axis=1
    )
    chunk_pos = block_pos * per_block + chunk_ids % per_block
    order = jnp.sum(
        jnp.where(chunk_pos[None, :] == chunk_ids[:, None], chunk_ids[None, :], 0), axis=1
    ).astype(jnp.int32)
    me = blk * chip_count + chip
    my_pos = jnp.sum(jnp.where(chunk_ids == me, chunk_pos, 0))
    own_cols = lax.dynamic_index_in_dim(
        mamba_input[half - 8 :].reshape(8, chip_count, PAIR, shard_cols), core, 2, False
    ).reshape(8, cols)
    tail = jnp.where(core == 1, own_cols, x_other[half - 8 :])
    tails = lax.all_to_all(
        jnp.broadcast_to(tail[None, 8 - (CONV - 1) :], (chunks, CONV - 1, cols)),
        ("blk", "chip"), split_axis=0, concat_axis=0, tiled=True,
    )
    before = (chunk_pos == my_pos - 1).astype(jnp.bfloat16)
    halo = jnp.einsum("m,mkc->kc", before, tails, preferred_element_type=jnp.float32)
    halo = jnp.concatenate(
        [jnp.zeros((8 - (CONV - 1), cols), jnp.bfloat16), halo.astype(jnp.bfloat16)], axis=0
    )

    delta, y_local, ends, totals = run_scan(
        core_arr, mamba_input, x_other, halo, low, weight, params, inject, read, col_block
    )

    piece = cols // chunks
    top = totals[0:1]
    hi = top.astype(jnp.bfloat16)
    rest = top - hi.astype(jnp.float32)
    mid = rest.astype(jnp.bfloat16)
    tiny = (rest - mid.astype(jnp.float32)).astype(jnp.bfloat16)
    sent = jnp.concatenate([ends.astype(jnp.bfloat16), hi, mid, tiny], axis=0)
    sent_rows = STATE + 3
    got = lax.all_to_all(
        sent.reshape(sent_rows, chunks, piece).transpose(1, 0, 2), ("blk", "chip"),
        split_axis=0, concat_axis=0, tiled=True,
    ).astype(jnp.float32)
    got_totals = jnp.sum(got[:, STATE:], axis=1, keepdims=True)
    rates = -LOG2E * jnp.exp(params[:, :STATE].transpose(1, 0, 2).reshape(STATE, cols))
    my_rates = lax.dynamic_slice_in_dim(rates, me * piece, piece, 1)
    enter = run_combine(order, got[:, :STATE], got_totals, my_rates)
    enter = lax.all_to_all(enter, ("blk", "chip"), split_axis=0, concat_axis=0, tiled=True)
    enter = enter.transpose(1, 0, 2).reshape(STATE, cols)

    attended = run_flash(flash_tables(span_order, my_blocks), q_local, kv_all)
    attention_output = lax.all_to_all(attended, ulys, split_axis=0, concat_axis=1, tiled=True)

    mine, theirs = run_correct(
        core_arr, delta, y_local, enter, params, read, gate_input, gate_other, col_block
    )
    back = lax.ppermute(theirs, "core", swap)
    mine = mine.reshape(half, chip_count, shard_cols)
    back = back.reshape(half, chip_count, shard_cols)
    even = jnp.where(core == 0, mine, back)
    odd = jnp.where(core == 0, back, mine)
    mamba_output = jnp.stack([even, odd], axis=2).reshape(half, inner)
    return (mamba_output, attention_output)


def solution(mesh):
    blk_count = mesh.shape["blk"]
    ulys_count = mesh.shape["ulys"]
    fine = Mesh(
        mesh.devices.reshape(blk_count, ulys_count // PAIR, PAIR), ("blk", "chip", "core")
    )
    rows = P(("blk", "chip", "core"), None)
    col = ("chip", "core")
    placed = (
        rows, rows, rows, rows,
        P(None, col), P(col), P(None, col), P(col), P(None, col), P(col),
        rows, rows, rows,
        P(),
    )
    return jax.shard_map(
        local, mesh=fine, in_specs=placed, out_specs=(rows, rows), check_vma=False
    )
```

```python
import functools

import jax
import jax.numpy as jnp
from jax import lax
from jax.experimental import pallas as pl
from jax.experimental.pallas import tpu as pltpu
from jax.sharding import Mesh
from jax.sharding import PartitionSpec as P

STATE = 16
CONV = 4
HD = 128
SPAN = 1024
LANES = 128
PAIR = 2
GROUP = 16
PIECES = 2
NEG_LARGE = -1e30
LOG2E = 1.4426950408889634
PARAM_ROWS = 24
VMEM_LIMIT = 56 * 1024 * 1024


def softplus(x):
    return jnp.maximum(x, 0.0) + jnp.log1p(jnp.exp(-jnp.abs(x)))


def silu(x):
    half = 0.5 * x
    return half * jnp.tanh(half) + half


def lane_tiles(cols):
    size = min(LANES, cols)
    return [slice(at, at + size) for at in range(0, cols, size)]


def spread(ref, k, row, count):
    return jnp.broadcast_to(ref[k, pl.ds(row, 1), :], (count, ref.shape[2]))


def scan_kernel(
    core_ref, own_ref, other_ref, halo_ref, low_own_ref, low_other_ref, weight_ref, param_ref,
    inject_ref, read_ref,
    delta_ref, y_ref, sent_ref,
    x_scr, driven_scr, push_scr, hist_scr, rate_scr, param_scr,
):
    core = core_ref[0]
    tokens, cols = y_ref.shape
    half = tokens // 2
    depth = low_own_ref.shape[1]
    tiles = lane_tiles(cols)
    mine = pl.multiple_of(core * half, 8)
    theirs = pl.multiple_of((1 - core) * half, 8)
    weight = weight_ref[...].reshape(depth, cols)
    raw_mine = jnp.dot(low_own_ref[...], weight, preferred_element_type=jnp.float32)
    for k, tile in enumerate(tiles):
        delta_ref[k, pl.ds(mine, half), :] = raw_mine[:, tile]
    raw_theirs = jnp.dot(low_other_ref[...], weight, preferred_element_type=jnp.float32)
    for k, tile in enumerate(tiles):
        delta_ref[k, pl.ds(theirs, half), :] = raw_theirs[:, tile]
    for k, tile in enumerate(tiles):
        x_scr[k, 0:8, :] = halo_ref[:, tile].astype(jnp.float32)
        x_scr[k, pl.ds(8 + mine, half), :] = own_ref[:, tile].astype(jnp.float32)
        x_scr[k, pl.ds(8 + theirs, half), :] = other_ref[:, tile].astype(jnp.float32)
    rate_scr[...] = -LOG2E * jnp.exp(param_ref[0, :STATE, :])
    for k in range(CONV + 3):
        param_scr[8 * k : 8 * k + 8, :] = jnp.broadcast_to(
            param_ref[0, STATE + k : STATE + k + 1, :], (8, cols)
        )

    def prepare(step, total):
        first = pl.multiple_of(step * 8, 8)
        total = list(total)
        for k, tile in enumerate(tiles):
            mixed = param_scr[8 * CONV : 8 * CONV + 8, tile]
            for j in range(CONV):
                shifted = x_scr[k, pl.ds(first + 8 - (CONV - 1) + j, 8), :]
                mixed = mixed + param_scr[8 * j : 8 * j + 8, tile] * shifted
            driven = silu(mixed)
            delta = softplus(
                delta_ref[k, pl.ds(first, 8), :] + param_scr[8 * CONV + 8 : 8 * CONV + 16, tile]
            )
            delta_ref[k, pl.ds(first, 8), :] = delta
            driven_scr[pl.ds(first, 8), tile] = driven * param_scr[8 * CONV + 16 : 8 * CONV + 24, tile]
            push_scr[k, pl.ds(first, 8), :] = driven * delta
            total[k] = total[k] + delta
        return tuple(total)

    zero = jnp.zeros((8, tiles[0].stop), jnp.float32)
    total = lax.fori_loop(0, tokens // 8, prepare, (zero,) * len(tiles))
    total = jnp.sum(jnp.concatenate(total, axis=1), axis=0, keepdims=True)

    def step16(group, hidden):
        base = pl.multiple_of(group * GROUP, GROUP)
        hidden = list(hidden)
        for i in range(GROUP):
            inject = inject_ref[pl.ds(pl.multiple_of((base + i) * STATE, STATE), STATE), :]
            for k, tile in enumerate(tiles):
                decay = jnp.exp2(spread(delta_ref, k, base + i, STATE) * rate_scr[:, tile])
                push = spread(push_scr, k, base + i, STATE)
                hidden[k] = decay * hidden[k] + push * inject
            hist_scr[i * STATE : (i + 1) * STATE, :] = jnp.concatenate(hidden, axis=1).astype(
                jnp.bfloat16
            )
        read = read_ref[pl.ds(base, GROUP), :]
        out = jnp.dot(read, hist_scr[...], preferred_element_type=jnp.float32)
        y_ref[pl.ds(base, GROUP), :] = (out + driven_scr[pl.ds(base, GROUP), :]).astype(y_ref.dtype)
        return tuple(hidden)

    zero = jnp.zeros((STATE, tiles[0].stop), jnp.float32)
    end = lax.fori_loop(0, tokens // GROUP, step16, (zero,) * len(tiles))
    end = jnp.concatenate(end, axis=1)
    top = total.astype(jnp.bfloat16).astype(jnp.float32)
    mid = (total - top).astype(jnp.bfloat16).astype(jnp.float32)
    low = total - top - mid
    row = lax.broadcasted_iota(jnp.int32, (STATE, cols), 0)
    rows = jnp.where(row == 0, top, jnp.where(row == 1, mid, jnp.where(row == 2, low, 0.0)))
    sent_ref[:STATE, :] = end.astype(sent_ref.dtype)
    sent_ref[STATE:, :] = rows.astype(sent_ref.dtype)


def correct_body(
    core_ref, delta_ref, y_ref, enter_ref, param_ref, read_ref, own_gate_ref, other_gate_ref,
    mine_ref, theirs_ref, hist_scr, out_scr, rate_scr,
):
    core = core_ref[0]
    tokens, cols = y_ref.shape
    half = tokens // 2
    rate_scr[...] = -LOG2E * jnp.exp(param_ref[0, :STATE, :])

    tiles = lane_tiles(cols)

    def step16(group, elapsed):
        base = pl.multiple_of(group * GROUP, GROUP)
        elapsed = list(elapsed)
        for i in range(GROUP):
            carried = []
            for k, tile in enumerate(tiles):
                elapsed[k] = elapsed[k] + spread(delta_ref, k, base + i, 8)
                twice = jnp.concatenate([elapsed[k], elapsed[k]], axis=0)
                carried.append(jnp.exp2(twice * rate_scr[:, tile]))
            carried = jnp.concatenate(carried, axis=1).astype(jnp.bfloat16)
            hist_scr[i * STATE : (i + 1) * STATE, :] = carried * enter_ref[...]
        read = read_ref[pl.ds(base, GROUP), :]
        out = jnp.dot(read, hist_scr[...], preferred_element_type=jnp.float32)
        total = out + y_ref[pl.ds(base, GROUP), :].astype(jnp.float32)
        out_scr[pl.ds(base, GROUP), :] = total.astype(jnp.bfloat16).astype(jnp.float32)
        return tuple(elapsed)

    zero = jnp.zeros((8, tiles[0].stop), jnp.float32)
    lax.fori_loop(0, tokens // GROUP, step16, (zero,) * len(tiles))
    rows = 16

    def gated(gate_ref, dest_ref, offset):
        def body(step, carry):
            first = pl.multiple_of(step * rows, rows)
            gate = gate_ref[pl.ds(first, rows), :].astype(jnp.float32)
            value = out_scr[pl.ds(pl.multiple_of(offset + first, 8), rows), :]
            dest_ref[pl.ds(first, rows), :] = (value * silu(gate)).astype(dest_ref.dtype)
            return carry

        lax.fori_loop(0, half // rows, body, 0)

    gated(own_gate_ref, mine_ref, core * half)
    gated(other_gate_ref, theirs_ref, (1 - core) * half)


def correct_kernel(core_ref, *refs, resumed):
    correct_body(core_ref, *(refs[1:] if resumed else refs))


def combine_kernel(order_ref, got_ref, rate_ref, enter_ref):
    chunks = got_ref.shape[0]
    rates = rate_ref[...]

    def body(place, state):
        chunk = order_ref[place]
        enter_ref[chunk] = state.astype(enter_ref.dtype)
        got = got_ref[chunk].astype(jnp.float32)
        total = got[STATE : STATE + 1] + got[STATE + 1 : STATE + 2] + got[STATE + 2 : STATE + 3]
        return jnp.exp2(total * rates) * state + got[:STATE]

    lax.fori_loop(0, chunks, body, jnp.zeros(rates.shape, jnp.float32))


def copy_kernel(core_ref, in_ref, out_ref):
    out_ref[...] = in_ref[...]


def place_kernel(core_ref, buffer_ref, in_ref, out_ref):
    out_ref[...] = in_ref[...]


def flash_kernel(
    side_ref, block_ref, diag_ref, first_ref, last_ref, q_ref, kv_ref, out_ref,
    max_scr, acc_scr, value_scr, *, heads, rows,
):
    step = pl.program_id(0)
    scale = LOG2E * HD ** (-0.5)
    span = kv_ref.shape[0]
    value_scr[:, :HD] = kv_ref[:, HD:]
    value_scr[:, HD:] = jnp.ones((span, HD), jnp.bfloat16)

    @pl.when(first_ref[step] == 1)
    def _():
        max_scr[...] = jnp.full(max_scr.shape, NEG_LARGE, jnp.float32)
        acc_scr[...] = jnp.zeros(acc_scr.shape, jnp.float32)

    def absorb(head, row, key_count, masked):
        q = q_ref[row : row + rows, head * HD : (head + 1) * HD]
        scores = lax.dot_general(
            q, kv_ref[:key_count, :HD], (((1,), (1,)), ((), ())),
            preferred_element_type=jnp.float32,
        ) * scale
        if masked:
            query_at = lax.broadcasted_iota(jnp.int32, scores.shape, 0) + row
            key_at = lax.broadcasted_iota(jnp.int32, scores.shape, 1)
            scores = jnp.where(key_at <= query_at, scores, NEG_LARGE)
        at = slice(head * span + row, head * span + row + rows)
        old_max = max_scr[at, :]
        new_max = jnp.maximum(old_max, jnp.max(scores, axis=1, keepdims=True))
        weights = jnp.exp2(scores - new_max[:, :1]).astype(jnp.bfloat16)
        shrink = jnp.exp2(old_max - new_max)
        acc_scr[at, :] = acc_scr[at, :] * shrink[:, :1] + jnp.dot(
            weights, value_scr[:key_count, :], preferred_element_type=jnp.float32
        )
        max_scr[at, :] = new_max

    @pl.when(diag_ref[step] == 0)
    def _():
        for head in range(heads):
            for row in range(0, span, rows):
                absorb(head, row, span, False)

    @pl.when(diag_ref[step] == 1)
    def _():
        for head in range(heads):
            for row in range(0, span, rows):
                absorb(head, row, row + rows, True)

    @pl.when(last_ref[step] == 1)
    def _():
        for head in range(heads):
            for row in range(0, span, rows):
                at = slice(head * span + row, head * span + row + rows)
                out_ref[row : row + rows, head * HD : (head + 1) * HD] = (
                    acc_scr[at, :HD] / acc_scr[at, HD:]
                ).astype(out_ref.dtype)


def whole(shape):
    return pl.BlockSpec(
        shape, lambda j, core_ref: (0,) * len(shape), pipeline_mode=pl.Buffered(1)
    )


def shard_map_of(side, piece):
    return lambda j, core_ref: (0, (PAIR * j + (core_ref[0] + side) % PAIR) * PIECES + piece)


def plain(j, core_ref):
    return (0, j)


def run_pick(core, full, piece, width):
    half, inner = full.shape
    blocks = inner // (width * PIECES * PAIR)
    return pl.pallas_call(
        copy_kernel,
        grid_spec=pltpu.PrefetchScalarGridSpec(
            num_scalar_prefetch=1,
            grid=(blocks,),
            in_specs=[pl.BlockSpec((half, width), shard_map_of(1, piece))],
            out_specs=pl.BlockSpec((half, width), plain),
        ),
        out_shape=jax.ShapeDtypeStruct((half, blocks * width), full.dtype),
        name="pick_channels",
    )(core, full)


def run_place(core, full, part, piece, width):
    half, _ = full.shape
    blocks = part.shape[1] // width
    return pl.pallas_call(
        place_kernel,
        grid_spec=pltpu.PrefetchScalarGridSpec(
            num_scalar_prefetch=1,
            grid=(blocks,),
            in_specs=[pl.BlockSpec(memory_space=pl.ANY), pl.BlockSpec((half, width), plain)],
            out_specs=pl.BlockSpec((half, width), shard_map_of(1, piece)),
        ),
        out_shape=jax.ShapeDtypeStruct(full.shape, full.dtype),
        input_output_aliases={1: 0},
        name="place_channels",
    )(core, full, part)


def run_scan(core, x_own, x_other, halo, low_own, low_other, weight, params, inject, read, piece):
    half, cols = x_other.shape
    tokens = 2 * half
    parts, blocks, part_rows, width = weight.shape
    lanes = min(LANES, width)
    tiles = width // lanes
    return pl.pallas_call(
        scan_kernel,
        grid_spec=pltpu.PrefetchScalarGridSpec(
            num_scalar_prefetch=1,
            grid=(blocks,),
            in_specs=[
                pl.BlockSpec((half, width), shard_map_of(0, piece)),
                pl.BlockSpec((half, width), plain),
                pl.BlockSpec((8, width), plain),
                whole(low_own.shape),
                whole(low_other.shape),
                pl.BlockSpec((parts, 1, part_rows, width), lambda j, core_ref: (0, j, 0, 0)),
                pl.BlockSpec((1, PARAM_ROWS, width), lambda j, core_ref: (j, 0, piece)),
                whole(inject.shape),
                whole(read.shape),
            ],
            out_specs=[
                pl.BlockSpec((tiles, tokens, lanes), lambda j, core_ref: (j, 0, 0)),
                pl.BlockSpec((tokens, width), plain),
                pl.BlockSpec((2 * STATE, width), plain),
            ],
            scratch_shapes=[
                pltpu.VMEM((tiles, tokens + 8, lanes), jnp.float32),
                pltpu.VMEM((tokens, width), jnp.float32),
                pltpu.VMEM((tiles, tokens, lanes), jnp.float32),
                pltpu.VMEM((GROUP * STATE, width), jnp.bfloat16),
                pltpu.VMEM((STATE, width), jnp.float32),
                pltpu.VMEM((8 * (CONV + 3), width), jnp.float32),
            ],
        ),
        out_shape=[
            jax.ShapeDtypeStruct((cols // lanes, tokens, lanes), jnp.float32),
            jax.ShapeDtypeStruct((tokens, cols), jnp.bfloat16),
            jax.ShapeDtypeStruct((2 * STATE, cols), jnp.bfloat16),
        ],
        compiler_params=pltpu.CompilerParams(vmem_limit_bytes=VMEM_LIMIT),
        name="token_scan",
    )(core, x_own, x_other, halo, low_own, low_other, weight, params, inject, read)


def run_correct(core, full, delta, y, enter, params, read, gate_own, gate_other, piece, width):
    tokens, cols = y.shape
    half, inner = gate_own.shape
    blocks = cols // width
    lanes = delta.shape[2]
    tiles = width // lanes
    resumed = full is not None
    first_spec = [pl.BlockSpec(memory_space=pl.ANY)] if resumed else []
    first_arg = (full,) if resumed else ()
    return pl.pallas_call(
        functools.partial(correct_kernel, resumed=resumed),
        grid_spec=pltpu.PrefetchScalarGridSpec(
            num_scalar_prefetch=1,
            grid=(blocks,),
            in_specs=first_spec
            + [
                pl.BlockSpec((tiles, tokens, lanes), lambda j, core_ref: (j, 0, 0)),
                pl.BlockSpec((tokens, width), plain),
                pl.BlockSpec((STATE, width), plain),
                pl.BlockSpec((1, PARAM_ROWS, width), lambda j, core_ref: (j, 0, piece)),
                whole(read.shape),
                pl.BlockSpec((half, width), shard_map_of(0, piece)),
                pl.BlockSpec((half, width), plain),
            ],
            out_specs=[
                pl.BlockSpec((half, width), shard_map_of(0, piece)),
                pl.BlockSpec((half, width), plain),
            ],
            scratch_shapes=[
                pltpu.VMEM((GROUP * STATE, width), jnp.bfloat16),
                pltpu.VMEM((tokens, width), jnp.float32),
                pltpu.VMEM((STATE, width), jnp.float32),
            ],
        ),
        out_shape=[
            jax.ShapeDtypeStruct((half, inner), jnp.bfloat16),
            jax.ShapeDtypeStruct((half, cols), jnp.bfloat16),
        ],
        input_output_aliases={1: 0} if resumed else {},
        compiler_params=pltpu.CompilerParams(vmem_limit_bytes=VMEM_LIMIT),
        name="state_correction",
    )(core, *first_arg, delta, y, enter, params, read, gate_own, gate_other)


def run_combine(order, got, rates):
    chunks, _, cols = got.shape
    return pl.pallas_call(
        combine_kernel,
        grid_spec=pltpu.PrefetchScalarGridSpec(
            num_scalar_prefetch=1,
            grid=(1,),
            in_specs=[
                pl.BlockSpec(got.shape, lambda i, o: (0, 0, 0)),
                pl.BlockSpec(rates.shape, lambda i, o: (0, 0)),
            ],
            out_specs=pl.BlockSpec((chunks, STATE, cols), lambda i, o: (0, 0, 0)),
        ),
        out_shape=jax.ShapeDtypeStruct((chunks, STATE, cols), jnp.bfloat16),
        compiler_params=pltpu.CompilerParams(vmem_limit_bytes=VMEM_LIMIT),
        name="state_combine",
    )(order, got, rates)


def run_flash(tables, q, kv, rows=512):
    tokens, width = q.shape
    heads = width // HD
    steps = tables[0].shape[0]

    def q_map(s, side, block, diag, first, last):
        return (side[s], 0)

    def kv_map(s, side, block, diag, first, last):
        return (block[s], 0)

    return pl.pallas_call(
        functools.partial(flash_kernel, heads=heads, rows=rows),
        grid_spec=pltpu.PrefetchScalarGridSpec(
            num_scalar_prefetch=5,
            grid=(steps,),
            in_specs=[pl.BlockSpec((SPAN, width), q_map), pl.BlockSpec((SPAN, 2 * HD), kv_map)],
            out_specs=pl.BlockSpec((SPAN, width), q_map),
            scratch_shapes=[
                pltpu.VMEM((heads * SPAN, HD), jnp.float32),
                pltpu.VMEM((heads * SPAN, 2 * HD), jnp.float32),
                pltpu.VMEM((SPAN, 2 * HD), jnp.bfloat16),
            ],
        ),
        out_shape=jax.ShapeDtypeStruct(q.shape, jnp.bfloat16),
        compiler_params=pltpu.CompilerParams(vmem_limit_bytes=VMEM_LIMIT),
        name="causal_attention",
    )(*tables, q, kv)


def flash_tables(span_order, my_blocks):
    block_total = span_order.shape[0]
    places = jnp.arange(block_total, dtype=jnp.int32)
    holder = jnp.sum(jnp.where(span_order[None, :] == places[:, None], places[None, :], 0), axis=1)
    steps = jnp.arange(block_total + 1, dtype=jnp.int32)
    first_count = my_blocks[0] + 1
    side = (steps >= first_count).astype(jnp.int32)
    place = jnp.where(side == 1, steps - first_count, steps)
    limit = jnp.where(side == 1, my_blocks[1], my_blocks[0])
    block = jnp.sum(jnp.where(places[None, :] == place[:, None], holder[None, :], 0), axis=1)
    last = (place == limit).astype(jnp.int32)
    first = (place == 0).astype(jnp.int32)
    return (side, block.astype(jnp.int32), last, first, last)


def local(
    mamba_input, gate_input, delta_low, state_mixers, conv_weight, conv_bias, delta_weight,
    delta_bias, decay_log, skip_gain, queries, key_rows, value_rows, span_order,
):
    blk = lax.axis_index("blk")
    chip = lax.axis_index("chip")
    core = lax.axis_index("core")
    blk_count = lax.axis_size("blk")
    chip_count = lax.axis_size("chip")
    ulys = ("chip", "core")
    chips = ("blk", "chip")
    ulys_count = chip_count * PAIR
    chunks = blk_count * chip_count
    block_total = span_order.shape[0]
    half, inner = mamba_input.shape
    tokens = PAIR * half
    shard_cols = delta_weight.shape[1]
    width = shard_cols // PIECES
    cols = chip_count * width
    swap = [(0, 1), (1, 0)]
    core_arr = core.astype(jnp.int32).reshape(1)
    my_blocks = lax.dynamic_slice_in_dim(span_order, 2 * blk, 2, 0)

    depth = delta_weight.shape[0]
    part_rows = depth // blk_count
    part = lax.dynamic_slice_in_dim(delta_weight, blk * part_rows, part_rows, 0)
    weights = []
    for piece in range(PIECES):
        gathered = lax.all_gather(
            part[:, piece * width : (piece + 1) * width], chips, axis=0, tiled=False
        )
        weights.append(gathered.reshape(blk_count, chip_count, part_rows, width))
    packed = jnp.concatenate(
        [
            decay_log,
            conv_weight.astype(jnp.float32),
            conv_bias[None],
            delta_bias[None],
            skip_gain[None],
            jnp.zeros((1, shard_cols), jnp.float32),
        ],
        axis=0,
    )
    params = lax.all_to_all(
        jnp.broadcast_to(packed[None], (chip_count, PARAM_ROWS, shard_cols)), "chip",
        split_axis=0, concat_axis=0, tiled=True,
    )
    rates = -LOG2E * jnp.exp(params[:, :STATE])

    x_other = [
        lax.ppermute(run_pick(core_arr, mamba_input, piece, width), "core", swap)
        for piece in range(PIECES)
    ]
    low_other = lax.ppermute(delta_low, "core", swap)
    mixers_other = lax.ppermute(state_mixers, "core", swap)
    mixers = jnp.where(
        core == 0,
        jnp.concatenate([state_mixers, mixers_other], axis=0),
        jnp.concatenate([mixers_other, state_mixers], axis=0),
    )
    inject = jnp.broadcast_to(
        mixers[:, :STATE].astype(jnp.float32).reshape(tokens * STATE, 1), (tokens * STATE, LANES)
    )
    same = jnp.arange(tokens, dtype=jnp.int32)[:, None] % GROUP == jnp.arange(GROUP, dtype=jnp.int32)
    read = jnp.where(
        same[:, :, None], mixers[:, None, STATE:], jnp.zeros((), jnp.bfloat16)
    ).reshape(tokens, GROUP * STATE)

    per_block = SPAN // tokens
    chunk_ids = jnp.arange(chunks, dtype=jnp.int32)
    stored = chunk_ids // per_block
    block_ids = jnp.arange(block_total, dtype=jnp.int32)
    block_pos = jnp.sum(
        jnp.where(stored[:, None] == block_ids[None, :], span_order[None, :], 0), axis=1
    )
    chunk_pos = block_pos * per_block + chunk_ids % per_block
    order = jnp.sum(
        jnp.where(chunk_pos[None, :] == chunk_ids[:, None], chunk_ids[None, :], 0), axis=1
    ).astype(jnp.int32)
    me = blk * chip_count + chip
    my_pos = jnp.sum(jnp.where(chunk_ids == me, chunk_pos, 0))
    own_tail = lax.dynamic_index_in_dim(
        mamba_input[half - (CONV - 1) :].reshape(CONV - 1, chip_count, PAIR, PIECES, width),
        core, 2, False,
    )
    other_tail = jnp.stack(
        [x[half - (CONV - 1) :].reshape(CONV - 1, chip_count, width) for x in x_other], axis=2
    )
    tail = jnp.where(core == 1, own_tail, other_tail).reshape(CONV - 1, PIECES * cols)
    tails = lax.all_to_all(
        jnp.broadcast_to(tail[None], (chunks, CONV - 1, PIECES * cols)), chips,
        split_axis=0, concat_axis=0, tiled=True,
    )
    before = (chunk_pos == my_pos - 1).astype(jnp.bfloat16)
    halo = jnp.einsum("m,mkc->kc", before, tails, preferred_element_type=jnp.float32)
    halo = jnp.concatenate(
        [jnp.zeros((8 - (CONV - 1), PIECES * cols), jnp.bfloat16), halo.astype(jnp.bfloat16)],
        axis=0,
    ).reshape(8, chip_count, PIECES, width)

    kv_heads = key_rows.shape[1] // HD
    repeat = ulys_count // kv_heads
    kv_rows = jnp.stack(
        [key_rows.reshape(half, kv_heads, HD), value_rows.reshape(half, kv_heads, HD)], axis=2
    )
    kv_rows = jnp.broadcast_to(
        kv_rows[:, :, None], (half, kv_heads, repeat, 2, HD)
    ).reshape(half, ulys_count * 2 * HD)
    kv_local = lax.all_to_all(kv_rows, ulys, split_axis=1, concat_axis=0, tiled=True)
    kv_all = gather_blocks(kv_local, blk, blk_count)
    q_local = lax.all_to_all(queries, ulys, split_axis=1, concat_axis=0, tiled=True)

    def scan_piece(piece, x_piece):
        return run_scan(
            core_arr, mamba_input, x_piece, halo[:, :, piece].reshape(8, cols), delta_low,
            low_other, weights[piece], params, inject, read, piece,
        )

    share = cols // chunks

    def exchange(sent, piece):
        got = lax.all_to_all(
            sent.reshape(2 * STATE, chunks, share).transpose(1, 0, 2), chips,
            split_axis=0, concat_axis=0, tiled=True,
        )
        piece_rates = rates[:, :, piece * width : (piece + 1) * width]
        piece_rates = piece_rates.transpose(1, 0, 2).reshape(STATE, cols)
        my_rates = lax.dynamic_slice_in_dim(piece_rates, me * share, share, 1)
        enter = run_combine(order, got, my_rates)
        enter = lax.all_to_all(enter, chips, split_axis=0, concat_axis=0, tiled=True)
        return enter.transpose(1, 0, 2).reshape(STATE, cols)

    delta_0, y_0, sent_0 = scan_piece(0, x_other[0])
    q_local, sent_0 = lax.optimization_barrier((q_local, sent_0))
    attended = run_flash(flash_tables(span_order, my_blocks), q_local, kv_all)
    x_later, attended = lax.optimization_barrier((x_other[1], attended))
    attention_output = lax.all_to_all(attended, ulys, split_axis=0, concat_axis=1, tiled=True)
    enter_0 = exchange(sent_0, 0)
    delta_1, y_1, sent_1 = scan_piece(1, x_later)
    gate_other = [
        lax.ppermute(run_pick(core_arr, gate_input, piece, width), "core", swap)
        for piece in range(PIECES)
    ]
    enter_0, sent_1 = lax.optimization_barrier((enter_0, sent_1))
    enter_1 = exchange(sent_1, 1)
    full, theirs_0 = run_correct(
        core_arr, None, delta_0, y_0, enter_0, params, read, gate_input, gate_other[0], 0, width
    )
    back_0 = lax.ppermute(theirs_0, "core", swap)
    full, theirs_1 = run_correct(
        core_arr, full, delta_1, y_1, enter_1, params, read, gate_input, gate_other[1], 1, width
    )
    back_1 = lax.ppermute(theirs_1, "core", swap)
    full = run_place(core_arr, full, back_0, 0, width)
    mamba_output = run_place(core_arr, full, back_1, 1, width)
    return (mamba_output, attention_output)


def gather_blocks(rows, blk, blk_count):
    count = rows.shape[0]
    total = jnp.zeros((blk_count * count, rows.shape[1]), rows.dtype)
    total = lax.dynamic_update_slice_in_dim(total, rows, blk * count, 0)
    for flip in range(1, blk_count):
        pairs = [(i, i ^ flip) for i in range(blk_count)]
        got = lax.ppermute(rows, "blk", pairs)
        total = lax.dynamic_update_slice_in_dim(total, got, (blk ^ flip) * count, 0)
    return total


def solution(mesh):
    blk_count = mesh.shape["blk"]
    ulys_count = mesh.shape["ulys"]
    fine = Mesh(
        mesh.devices.reshape(blk_count, ulys_count // PAIR, PAIR), ("blk", "chip", "core")
    )
    rows = P(("blk", "chip", "core"), None)
    col = ("chip", "core")
    placed = (
        rows, rows, rows, rows,
        P(None, col), P(col), P(None, col), P(col), P(None, col), P(col),
        rows, rows, rows,
        P(),
    )
    return jax.shard_map(
        local, mesh=fine, in_specs=placed, out_specs=(rows, rows), check_vma=False
    )
```

```python
import functools

import jax
import jax.numpy as jnp
from jax import lax
from jax.experimental import pallas as pl
from jax.experimental.pallas import tpu as pltpu
from jax.sharding import Mesh
from jax.sharding import PartitionSpec as P

STATE = 16
CONV = 4
HD = 128
SPAN = 1024
LANES = 128
PAIR = 2
GROUP = 16
PIECES = 2
ONES = 16
NEG_LARGE = -1e30
LOG2E = 1.4426950408889634
PARAM_ROWS = 24
VMEM_LIMIT = 56 * 1024 * 1024


def softplus(x):
    return jnp.maximum(x, 0.0) + jnp.log1p(jnp.exp(-jnp.abs(x)))


def silu(x):
    half = 0.5 * x
    return half * jnp.tanh(half) + half


def lane_tiles(cols):
    size = min(LANES, cols)
    return [slice(at, at + size) for at in range(0, cols, size)]


def spread(ref, k, row, count):
    return jnp.broadcast_to(ref[k, pl.ds(row, 1), :], (count, ref.shape[2]))


def scan_kernel(
    core_ref, own_ref, other_ref, halo_ref, low_own_ref, low_other_ref, weight_ref, param_ref,
    inject_ref, read_ref,
    delta_ref, y_ref, sent_ref,
    x_scr, driven_scr, push_scr, hist_scr, rate_scr, param_scr,
):
    core = core_ref[0]
    tokens, cols = y_ref.shape
    half = tokens // 2
    depth = low_own_ref.shape[1]
    tiles = lane_tiles(cols)
    mine = pl.multiple_of(core * half, 8)
    theirs = pl.multiple_of((1 - core) * half, 8)
    weight = weight_ref[...].reshape(depth, cols)
    raw_mine = jnp.dot(low_own_ref[...], weight, preferred_element_type=jnp.float32)
    for k, tile in enumerate(tiles):
        delta_ref[k, pl.ds(mine, half), :] = raw_mine[:, tile]
    raw_theirs = jnp.dot(low_other_ref[...], weight, preferred_element_type=jnp.float32)
    for k, tile in enumerate(tiles):
        delta_ref[k, pl.ds(theirs, half), :] = raw_theirs[:, tile]
    for k, tile in enumerate(tiles):
        x_scr[k, 0:8, :] = halo_ref[:, tile].astype(jnp.float32)
        x_scr[k, pl.ds(8 + mine, half), :] = own_ref[:, tile].astype(jnp.float32)
        x_scr[k, pl.ds(8 + theirs, half), :] = other_ref[:, tile].astype(jnp.float32)
    rate_scr[...] = -LOG2E * jnp.exp(param_ref[0, :STATE, :])
    for k in range(CONV + 3):
        param_scr[8 * k : 8 * k + 8, :] = jnp.broadcast_to(
            param_ref[0, STATE + k : STATE + k + 1, :], (8, cols)
        )

    def prepare(step, total):
        first = pl.multiple_of(step * 8, 8)
        total = list(total)
        for k, tile in enumerate(tiles):
            mixed = param_scr[8 * CONV : 8 * CONV + 8, tile]
            for j in range(CONV):
                shifted = x_scr[k, pl.ds(first + 8 - (CONV - 1) + j, 8), :]
                mixed = mixed + param_scr[8 * j : 8 * j + 8, tile] * shifted
            driven = silu(mixed)
            delta = softplus(
                delta_ref[k, pl.ds(first, 8), :] + param_scr[8 * CONV + 8 : 8 * CONV + 16, tile]
            )
            delta_ref[k, pl.ds(first, 8), :] = delta
            driven_scr[pl.ds(first, 8), tile] = driven * param_scr[8 * CONV + 16 : 8 * CONV + 24, tile]
            push_scr[k, pl.ds(first, 8), :] = driven * delta
            total[k] = total[k] + delta
        return tuple(total)

    zero = jnp.zeros((8, tiles[0].stop), jnp.float32)
    total = lax.fori_loop(0, tokens // 8, prepare, (zero,) * len(tiles))
    total = jnp.sum(jnp.concatenate(total, axis=1), axis=0, keepdims=True)

    def step16(group, hidden):
        base = pl.multiple_of(group * GROUP, GROUP)
        hidden = list(hidden)
        for i in range(GROUP):
            inject = inject_ref[pl.ds(pl.multiple_of((base + i) * STATE, STATE), STATE), :]
            for k, tile in enumerate(tiles):
                decay = jnp.exp2(spread(delta_ref, k, base + i, STATE) * rate_scr[:, tile])
                push = spread(push_scr, k, base + i, STATE)
                hidden[k] = decay * hidden[k] + push * inject
            hist_scr[i * STATE : (i + 1) * STATE, :] = jnp.concatenate(hidden, axis=1).astype(
                jnp.bfloat16
            )
        read = read_ref[pl.ds(base, GROUP), :]
        out = jnp.dot(read, hist_scr[...], preferred_element_type=jnp.float32)
        y_ref[pl.ds(base, GROUP), :] = (out + driven_scr[pl.ds(base, GROUP), :]).astype(y_ref.dtype)
        return tuple(hidden)

    zero = jnp.zeros((STATE, tiles[0].stop), jnp.float32)
    end = lax.fori_loop(0, tokens // GROUP, step16, (zero,) * len(tiles))
    end = jnp.concatenate(end, axis=1)
    top = total.astype(jnp.bfloat16).astype(jnp.float32)
    mid = (total - top).astype(jnp.bfloat16).astype(jnp.float32)
    low = total - top - mid
    row = lax.broadcasted_iota(jnp.int32, (STATE, cols), 0)
    rows = jnp.where(row == 0, top, jnp.where(row == 1, mid, jnp.where(row == 2, low, 0.0)))
    share = sent_ref.shape[2]
    for k in range(sent_ref.shape[0]):
        at = slice(k * share, (k + 1) * share)
        sent_ref[k, :STATE, :] = end[:, at].astype(sent_ref.dtype)
        sent_ref[k, STATE:, :] = rows[:, at].astype(sent_ref.dtype)


def correct_body(
    core_ref, delta_ref, y_ref, enter_ref, param_ref, read_ref, own_gate_ref, other_gate_ref,
    mine_ref, theirs_ref, hist_scr, out_scr, rate_scr, enter_scr,
):
    core = core_ref[0]
    enter_scr[...] = jnp.concatenate([enter_ref[k] for k in range(enter_ref.shape[0])], axis=1)
    tokens, cols = y_ref.shape
    half = tokens // 2
    rate_scr[...] = -LOG2E * jnp.exp(param_ref[0, :STATE, :])

    tiles = lane_tiles(cols)

    def step16(group, elapsed):
        base = pl.multiple_of(group * GROUP, GROUP)
        elapsed = list(elapsed)
        for i in range(GROUP):
            carried = []
            for k, tile in enumerate(tiles):
                elapsed[k] = elapsed[k] + spread(delta_ref, k, base + i, 8)
                twice = jnp.concatenate([elapsed[k], elapsed[k]], axis=0)
                carried.append(jnp.exp2(twice * rate_scr[:, tile]))
            carried = jnp.concatenate(carried, axis=1).astype(jnp.bfloat16)
            hist_scr[i * STATE : (i + 1) * STATE, :] = carried * enter_scr[...]
        read = read_ref[pl.ds(base, GROUP), :]
        out = jnp.dot(read, hist_scr[...], preferred_element_type=jnp.float32)
        total = out + y_ref[pl.ds(base, GROUP), :].astype(jnp.float32)
        out_scr[pl.ds(base, GROUP), :] = total.astype(jnp.bfloat16).astype(jnp.float32)
        return tuple(elapsed)

    zero = jnp.zeros((8, tiles[0].stop), jnp.float32)
    lax.fori_loop(0, tokens // GROUP, step16, (zero,) * len(tiles))
    rows = 16

    def gated(gate_ref, dest_ref, offset):
        def body(step, carry):
            first = pl.multiple_of(step * rows, rows)
            gate = gate_ref[pl.ds(first, rows), :].astype(jnp.float32)
            value = out_scr[pl.ds(pl.multiple_of(offset + first, 8), rows), :]
            dest_ref[pl.ds(first, rows), :] = (value * silu(gate)).astype(dest_ref.dtype)
            return carry

        lax.fori_loop(0, half // rows, body, 0)

    gated(own_gate_ref, mine_ref, core * half)
    gated(other_gate_ref, theirs_ref, (1 - core) * half)


def correct_kernel(core_ref, *refs, resumed):
    correct_body(core_ref, *(refs[1:] if resumed else refs))


def combine_kernel(order_ref, got_ref, rate_ref, enter_ref):
    chunks = got_ref.shape[0]
    rates = rate_ref[...]

    def body(place, state):
        chunk = order_ref[place]
        enter_ref[chunk] = state.astype(enter_ref.dtype)
        got = got_ref[chunk].astype(jnp.float32)
        total = got[STATE : STATE + 1] + got[STATE + 1 : STATE + 2] + got[STATE + 2 : STATE + 3]
        return jnp.exp2(total * rates) * state + got[:STATE]

    lax.fori_loop(0, chunks, body, jnp.zeros(rates.shape, jnp.float32))


def copy_kernel(core_ref, in_ref, out_ref):
    out_ref[...] = in_ref[...]


def place_kernel(core_ref, buffer_ref, in_ref, out_ref):
    out_ref[...] = in_ref[...]


def flash_kernel(
    side_ref, flip_ref, half_ref, diag_ref, first_ref, last_ref, q_ref, *refs, heads, rows, sources,
):
    kv_refs = refs[:sources]
    out_ref, query_scr, key_scr, value_scr, max_scr, acc_scr = refs[sources:]
    step = pl.program_id(0)
    scale = LOG2E * HD ** (-0.5)
    wide = 2 * HD
    span = q_ref.shape[0]

    for source in range(sources):

        @pl.when(flip_ref[step] == source)
        def _(kv_ref=kv_refs[source]):
            key_scr[:, :HD] = kv_ref[:, :HD]
            key_scr[:, HD:] = kv_ref[:, :HD]
            value_scr[:HD, :] = kv_ref[:, HD:].T

    value_scr[HD:, :] = jnp.ones((ONES, span), jnp.bfloat16)

    @pl.when(first_ref[step] == 1)
    def _():
        max_scr[...] = jnp.full(max_scr.shape, NEG_LARGE, jnp.float32)
        acc_scr[...] = jnp.zeros(acc_scr.shape, jnp.float32)
        for head in range(heads):
            scaled = q_ref[:, head * HD : (head + 1) * HD].astype(jnp.float32) * scale
            coarse = scaled.astype(jnp.bfloat16)
            query_scr[:, head * wide : head * wide + HD] = coarse
            query_scr[:, head * wide + HD : (head + 1) * wide] = (
                scaled - coarse.astype(jnp.float32)
            ).astype(jnp.bfloat16)

    def score(head, row, key_count, masked):
        q = query_scr[row : row + rows, head * wide : (head + 1) * wide]
        scores = lax.dot_general(
            key_scr[:key_count, :], q, (((1,), (1,)), ((), ())),
            preferred_element_type=jnp.float32,
        )
        if masked:
            last = scores[row:, :]
            key_at = lax.broadcasted_iota(jnp.int32, last.shape, 0)
            query_at = lax.broadcasted_iota(jnp.int32, last.shape, 1)
            last = jnp.where(key_at <= query_at, last, NEG_LARGE)
            scores = jnp.concatenate([scores[:row, :], last], axis=0) if row else last
        return scores

    def absorb(head, row, key_count, scores):
        at = slice(row, row + rows)
        old_max = max_scr[head, 0:1, at]
        new_max = jnp.maximum(old_max, jnp.max(scores, axis=0, keepdims=True))
        weights = jnp.exp2(scores - new_max).astype(jnp.bfloat16)
        shrink = jnp.exp2(old_max - new_max)
        acc_scr[head, :, at] = acc_scr[head, :, at] * shrink + jnp.dot(
            value_scr[:, :key_count], weights, preferred_element_type=jnp.float32
        )
        max_scr[head, :, at] = jnp.broadcast_to(new_max, (8, rows))

    def sweep(masked):
        work = [(head, row) for head in range(heads) for row in range(0, span, rows)]
        count = [row + rows if masked else span for _, row in work]
        ahead = score(*work[0], count[0], masked)
        for i, (head, row) in enumerate(work):
            scores = ahead
            if i + 1 < len(work):
                ahead = score(*work[i + 1], count[i + 1], masked)
            absorb(head, row, count[i], scores)

    @pl.when(diag_ref[step] == 0)
    def _():
        sweep(False)

    @pl.when(diag_ref[step] == 1)
    def _():
        sweep(True)

    @pl.when(last_ref[step] == 1)
    def _():
        for head in range(heads):
            for row in range(0, span, rows):
                at = slice(row, row + rows)
                ratio = acc_scr[head, :HD, at] / acc_scr[head, HD : HD + 1, at]
                out_ref[at, head * HD : (head + 1) * HD] = ratio.T.astype(out_ref.dtype)


def whole(shape):
    return pl.BlockSpec(
        shape, lambda j, core_ref: (0,) * len(shape), pipeline_mode=pl.Buffered(1)
    )


def shard_map_of(side, piece, first=0):
    return lambda j, core_ref: (
        0, (PAIR * (j + first) + (core_ref[0] + side) % PAIR) * PIECES + piece,
    )


def param_spec(count, width, piece, first):
    return pl.BlockSpec(
        (1, PARAM_ROWS, width),
        lambda j, core_ref: (lax.rem(core_ref[1] + count - (j + first), count), 0, piece),
    )


def plain(j, core_ref):
    return (0, j)


def run_pick(core, full, piece, width):
    half, inner = full.shape
    blocks = inner // (width * PIECES * PAIR)
    return pl.pallas_call(
        copy_kernel,
        grid_spec=pltpu.PrefetchScalarGridSpec(
            num_scalar_prefetch=1,
            grid=(blocks,),
            in_specs=[pl.BlockSpec((half, width), shard_map_of(1, piece))],
            out_specs=pl.BlockSpec((half, width), plain),
        ),
        out_shape=jax.ShapeDtypeStruct((half, blocks * width), full.dtype),
        name="pick_channels",
    )(core, full)


def run_place(core, full, part, piece, width, first):
    half, _ = full.shape
    blocks = part.shape[1] // width
    return pl.pallas_call(
        place_kernel,
        grid_spec=pltpu.PrefetchScalarGridSpec(
            num_scalar_prefetch=1,
            grid=(blocks,),
            in_specs=[pl.BlockSpec(memory_space=pl.ANY), pl.BlockSpec((half, width), plain)],
            out_specs=pl.BlockSpec((half, width), shard_map_of(1, piece, first)),
        ),
        out_shape=jax.ShapeDtypeStruct(full.shape, full.dtype),
        input_output_aliases={1: 0},
        name="place_channels",
    )(core, full, part)


def run_scan(
    core, x_own, x_other, halo, low_own, low_other, weight, params, inject, read, piece, width, share,
    first, blocks,
):
    half = x_other.shape[0]
    cols = blocks * width
    tokens = 2 * half
    parts, shards, part_rows, _ = weight.shape

    def shifted(j, core_ref):
        return (0, j + first)

    lanes = min(LANES, width)
    tiles = width // lanes
    return pl.pallas_call(
        scan_kernel,
        grid_spec=pltpu.PrefetchScalarGridSpec(
            num_scalar_prefetch=1,
            grid=(blocks,),
            in_specs=[
                pl.BlockSpec((half, width), shard_map_of(0, piece, first)),
                pl.BlockSpec((half, width), shifted),
                pl.BlockSpec((8, width), lambda j, core_ref: (0, piece * shards + j + first)),
                whole(low_own.shape),
                whole(low_other.shape),
                pl.BlockSpec((parts, 1, part_rows, width), lambda j, core_ref: (0, j + first, 0, piece)),
                param_spec(shards, width, piece, first),
                whole(inject.shape),
                whole(read.shape),
            ],
            out_specs=[
                pl.BlockSpec((tiles, tokens, lanes), lambda j, core_ref: (j, 0, 0)),
                pl.BlockSpec((tokens, width), plain),
                pl.BlockSpec((width // share, 2 * STATE, share), lambda j, core_ref: (j, 0, 0)),
            ],
            scratch_shapes=[
                pltpu.VMEM((tiles, tokens + 8, lanes), jnp.float32),
                pltpu.VMEM((tokens, width), jnp.float32),
                pltpu.VMEM((tiles, tokens, lanes), jnp.float32),
                pltpu.VMEM((GROUP * STATE, width), jnp.bfloat16),
                pltpu.VMEM((STATE, width), jnp.float32),
                pltpu.VMEM((8 * (CONV + 3), width), jnp.float32),
            ],
        ),
        out_shape=[
            jax.ShapeDtypeStruct((cols // lanes, tokens, lanes), jnp.float32),
            jax.ShapeDtypeStruct((tokens, cols), jnp.bfloat16),
            jax.ShapeDtypeStruct((cols // share, 2 * STATE, share), jnp.bfloat16),
        ],
        compiler_params=pltpu.CompilerParams(vmem_limit_bytes=VMEM_LIMIT),
        name="token_scan",
    )(core, x_own, x_other, halo, low_own, low_other, weight, params, inject, read)


def run_correct(
    core, full, delta, y, enter, params, read, gate_own, gate_other, piece, width, first, inside, blocks
):
    tokens = y.shape[0]
    half, inner = gate_own.shape
    cols = blocks * width
    lanes = delta.shape[2]
    tiles = width // lanes
    share = enter.shape[2]
    resumed = full is not None
    first_spec = [pl.BlockSpec(memory_space=pl.ANY)] if resumed else []
    first_arg = (full,) if resumed else ()
    return pl.pallas_call(
        functools.partial(correct_kernel, resumed=resumed),
        grid_spec=pltpu.PrefetchScalarGridSpec(
            num_scalar_prefetch=1,
            grid=(blocks,),
            in_specs=first_spec
            + [
                pl.BlockSpec((tiles, tokens, lanes), lambda j, core_ref: (j + inside, 0, 0)),
                pl.BlockSpec((tokens, width), lambda j, core_ref: (0, j + inside)),
                pl.BlockSpec((width // share, STATE, share), lambda j, core_ref: (j + first, 0, 0)),
                param_spec(params.shape[0], width, piece, first),
                whole(read.shape),
                pl.BlockSpec((half, width), shard_map_of(0, piece, first)),
                pl.BlockSpec((half, width), lambda j, core_ref: (0, j + first)),
            ],
            out_specs=[
                pl.BlockSpec((half, width), shard_map_of(0, piece, first)),
                pl.BlockSpec((half, width), plain),
            ],
            scratch_shapes=[
                pltpu.VMEM((GROUP * STATE, width), jnp.bfloat16),
                pltpu.VMEM((tokens, width), jnp.float32),
                pltpu.VMEM((STATE, width), jnp.float32),
                pltpu.VMEM((STATE, width), jnp.bfloat16),
            ],
        ),
        out_shape=[
            jax.ShapeDtypeStruct((half, inner), jnp.bfloat16),
            jax.ShapeDtypeStruct((half, cols), jnp.bfloat16),
        ],
        input_output_aliases={1: 0} if resumed else {},
        compiler_params=pltpu.CompilerParams(vmem_limit_bytes=VMEM_LIMIT),
        name="state_correction",
    )(core, *first_arg, delta, y, enter, params, read, gate_own, gate_other)


def run_combine(order, got, rates):
    chunks, _, cols = got.shape
    return pl.pallas_call(
        combine_kernel,
        grid_spec=pltpu.PrefetchScalarGridSpec(
            num_scalar_prefetch=1,
            grid=(1,),
            in_specs=[
                pl.BlockSpec(got.shape, lambda i, o: (0, 0, 0)),
                pl.BlockSpec(rates.shape, lambda i, o: (0, 0)),
            ],
            out_specs=pl.BlockSpec((chunks, STATE, cols), lambda i, o: (0, 0, 0)),
        ),
        out_shape=jax.ShapeDtypeStruct((chunks, STATE, cols), jnp.bfloat16),
        compiler_params=pltpu.CompilerParams(vmem_limit_bytes=VMEM_LIMIT),
        name="state_combine",
    )(order, got, rates)


def run_flash(tables, q, kv_parts, rows=512):
    tokens, width = q.shape
    heads = width // HD
    steps = tables[0].shape[0]
    sources = len(kv_parts)

    def q_map(s, side, flip, half, diag, first, last):
        return (side[s], 0)

    def kv_map(s, side, flip, half, diag, first, last):
        return (half[s], 0)

    return pl.pallas_call(
        functools.partial(flash_kernel, heads=heads, rows=rows, sources=sources),
        grid_spec=pltpu.PrefetchScalarGridSpec(
            num_scalar_prefetch=6,
            grid=(steps,),
            in_specs=[pl.BlockSpec((SPAN, width), q_map)]
            + [pl.BlockSpec((SPAN, 2 * HD), kv_map)] * sources,
            out_specs=pl.BlockSpec((SPAN, width), q_map),
            scratch_shapes=[
                pltpu.VMEM((SPAN, 2 * width), jnp.bfloat16),
                pltpu.VMEM((SPAN, 2 * HD), jnp.bfloat16),
                pltpu.VMEM((HD + ONES, SPAN), jnp.bfloat16),
                pltpu.VMEM((heads, 8, SPAN), jnp.float32),
                pltpu.VMEM((heads, HD + ONES, SPAN), jnp.float32),
            ],
        ),
        out_shape=jax.ShapeDtypeStruct(q.shape, jnp.bfloat16),
        compiler_params=pltpu.CompilerParams(vmem_limit_bytes=VMEM_LIMIT),
        name="causal_attention",
    )(*tables, q, *kv_parts)


def flash_tables(span_order, my_blocks, blk):
    block_total = span_order.shape[0]
    places = jnp.arange(block_total, dtype=jnp.int32)
    holder = jnp.sum(jnp.where(span_order[None, :] == places[:, None], places[None, :], 0), axis=1)
    steps = jnp.arange(block_total + 1, dtype=jnp.int32)
    first_count = my_blocks[0] + 1
    side = (steps >= first_count).astype(jnp.int32)
    place = jnp.where(side == 1, steps - first_count, steps)
    limit = jnp.where(side == 1, my_blocks[1], my_blocks[0])
    block = jnp.sum(jnp.where(places[None, :] == place[:, None], holder[None, :], 0), axis=1)
    block = block.astype(jnp.int32)
    last = (place == limit).astype(jnp.int32)
    first = (place == 0).astype(jnp.int32)
    return (side, (block // 2) ^ blk.astype(jnp.int32), block % 2, last, first, last)


def local(
    mamba_input, gate_input, delta_low, state_mixers, conv_weight, conv_bias, delta_weight,
    delta_bias, decay_log, skip_gain, queries, key_rows, value_rows, span_order,
):
    blk = lax.axis_index("blk")
    chip = lax.axis_index("chip")
    core = lax.axis_index("core")
    blk_count = lax.axis_size("blk")
    chip_count = lax.axis_size("chip")
    ulys = ("chip", "core")
    chips = ("blk", "chip")
    ulys_count = chip_count * PAIR
    chunks = blk_count * chip_count
    block_total = span_order.shape[0]
    half, inner = mamba_input.shape
    tokens = PAIR * half
    shard_cols = delta_weight.shape[1]
    width = shard_cols // PIECES
    cols = chip_count * width
    swap = [(0, 1), (1, 0)]
    core_arr = jnp.stack([core, chip]).astype(jnp.int32)
    my_blocks = lax.dynamic_slice_in_dim(span_order, 2 * blk, 2, 0)

    depth = delta_weight.shape[0]
    part_rows = depth // blk_count
    part = lax.dynamic_slice_in_dim(delta_weight, blk * part_rows, part_rows, 0)
    weight = lax.all_gather(part, chips, axis=0, tiled=False)
    weight = weight.reshape(blk_count, chip_count, part_rows, shard_cols)

    kv_heads = key_rows.shape[1] // HD
    repeat = ulys_count // kv_heads
    kv_rows = jnp.stack(
        [key_rows.reshape(half, kv_heads, HD), value_rows.reshape(half, kv_heads, HD)], axis=2
    )
    kv_rows = jnp.broadcast_to(
        kv_rows[:, :, None], (half, kv_heads, repeat, 2, HD)
    ).reshape(half, ulys_count * 2 * HD)
    kv_local = lax.all_to_all(kv_rows, ulys, split_axis=1, concat_axis=0, tiled=True)

    packed = jnp.concatenate(
        [
            decay_log,
            conv_weight.astype(jnp.float32),
            conv_bias[None],
            delta_bias[None],
            skip_gain[None],
            jnp.zeros((1, shard_cols), jnp.float32),
        ],
        axis=0,
    )
    x_other = [
        lax.ppermute(run_pick(core_arr, mamba_input, piece, width), "core", swap)
        for piece in range(PIECES)
    ]
    low_other = lax.ppermute(delta_low, "core", swap)
    mixers_other = lax.ppermute(state_mixers, "core", swap)
    mixers = jnp.where(
        core == 0,
        jnp.concatenate([state_mixers, mixers_other], axis=0),
        jnp.concatenate([mixers_other, state_mixers], axis=0),
    )
    inject = jnp.broadcast_to(
        mixers[:, :STATE].astype(jnp.float32).reshape(tokens * STATE, 1), (tokens * STATE, LANES)
    )
    same = jnp.arange(tokens, dtype=jnp.int32)[:, None] % GROUP == jnp.arange(GROUP, dtype=jnp.int32)
    read = jnp.where(
        same[:, :, None], mixers[:, None, STATE:], jnp.zeros((), jnp.bfloat16)
    ).reshape(tokens, GROUP * STATE)

    per_block = SPAN // tokens
    chunk_ids = jnp.arange(chunks, dtype=jnp.int32)
    stored = chunk_ids // per_block
    block_ids = jnp.arange(block_total, dtype=jnp.int32)
    block_pos = jnp.sum(
        jnp.where(stored[:, None] == block_ids[None, :], span_order[None, :], 0), axis=1
    )
    chunk_pos = block_pos * per_block + chunk_ids % per_block
    order = jnp.sum(
        jnp.where(chunk_pos[None, :] == chunk_ids[:, None], chunk_ids[None, :], 0), axis=1
    ).astype(jnp.int32)
    me = blk * chip_count + chip
    my_pos = jnp.sum(jnp.where(chunk_ids == me, chunk_pos, 0))
    own_tail = lax.dynamic_index_in_dim(
        mamba_input[half - (CONV - 1) :].reshape(CONV - 1, chip_count, PAIR, PIECES, width),
        core, 2, False,
    ).swapaxes(1, 2).reshape(CONV - 1, PIECES * cols)
    other_tail = jnp.concatenate([x[half - (CONV - 1) :] for x in x_other], axis=1)
    tail = jnp.where(core == 1, own_tail, other_tail)
    gate_other = [
        lax.ppermute(run_pick(core_arr, gate_input, piece, width), "core", swap)
        for piece in range(PIECES)
    ]

    params = jnp.stack(
        [packed]
        + [
            lax.ppermute(packed, "chip", [(i, (i + far) % chip_count) for i in range(chip_count)])
            for far in range(1, chip_count)
        ]
    )

    kv_local, queries = lax.optimization_barrier((kv_local, queries))
    kv_parts = [kv_local] + [
        lax.ppermute(kv_local, "blk", [(i, i ^ flip) for i in range(blk_count)])
        for flip in range(1, blk_count)
    ]
    q_local = lax.all_to_all(queries, ulys, split_axis=1, concat_axis=0, tiled=True)
    q_local, kv_parts, tail = lax.optimization_barrier((q_local, kv_parts, tail))
    tails = lax.all_to_all(
        jnp.broadcast_to(tail[None], (chunks, CONV - 1, PIECES * cols)), chips,
        split_axis=0, concat_axis=0, tiled=True,
    )
    before = (chunk_pos == my_pos - 1).astype(jnp.bfloat16)
    halo = jnp.einsum("m,mkc->kc", before, tails, preferred_element_type=jnp.float32)
    halo = jnp.concatenate(
        [jnp.zeros((8 - (CONV - 1), PIECES * cols), jnp.bfloat16), halo.astype(jnp.bfloat16)],
        axis=0,
    )

    share = cols // chunks
    split = chip_count // 2

    def scan_part(piece, x_piece, first, blocks):
        return run_scan(
            core_arr, mamba_input, x_piece, halo, delta_low,
            low_other, weight, params, inject, read, piece, width, share, first, blocks,
        )

    def rates_of(piece):
        at = me * share
        shard = at // width
        far = (chip + chip_count - shard) % chip_count
        mine = lax.dynamic_slice(
            params, (far, 0, piece * width + at % width), (1, STATE, share)
        )
        return -LOG2E * jnp.exp(mine[0])

    my_rates = [rates_of(piece) for piece in range(PIECES)]

    def to_owners(array):
        return lax.all_to_all(array, chips, split_axis=0, concat_axis=0, tiled=True)

    def correct_part(full, made, enter, piece, first, inside, blocks):
        delta, y = made[:2]
        return run_correct(
            core_arr, full, delta, y, enter, params, read, gate_input, gate_other[piece], piece,
            width, first, inside, blocks,
        )

    q_local, gate_other, inject, read, my_rates, x_other, low_other = lax.optimization_barrier(
        (q_local, gate_other, inject, read, my_rates, x_other, low_other)
    )
    attended = run_flash(flash_tables(span_order, my_blocks, blk), q_local, kv_parts)
    x_now, attended = lax.optimization_barrier((x_other[0], attended))
    made_0 = scan_part(0, x_now, 0, chip_count)
    x_now, sent_0 = lax.optimization_barrier((x_other[1], made_0[2]))
    got_0 = to_owners(sent_0)
    made_1a = scan_part(1, x_now, 0, split)
    x_now, got_0, sent_1a = lax.optimization_barrier((x_now, got_0, made_1a[2]))
    enter_0 = to_owners(run_combine(order, got_0, my_rates[0]))
    made_1b = scan_part(1, x_now, split, chip_count - split)
    enter_0, sent_1 = lax.optimization_barrier(
        (enter_0, jnp.concatenate([sent_1a, made_1b[2]], axis=0))
    )
    got_1 = to_owners(sent_1)
    full, theirs_0a = correct_part(None, made_0, enter_0, 0, 0, 0, split)
    full, got_1 = lax.optimization_barrier((full, got_1))
    enter_1 = to_owners(run_combine(order, got_1, my_rates[1]))
    back_0a = lax.ppermute(theirs_0a, "core", swap)
    full, theirs_0b = correct_part(full, made_0, enter_0, 0, split, split, chip_count - split)
    back_0b = lax.ppermute(theirs_0b, "core", swap)
    full, enter_1, attended = lax.optimization_barrier((full, enter_1, attended))
    attention_output = lax.all_to_all(attended, ulys, split_axis=0, concat_axis=1, tiled=True)
    full, theirs_1a = correct_part(full, made_1a, enter_1, 1, 0, 0, split)
    back_1a = lax.ppermute(theirs_1a, "core", swap)
    full, theirs_1b = correct_part(full, made_1b, enter_1, 1, split, 0, chip_count - split)
    back_1b = lax.ppermute(theirs_1b, "core", swap)
    full = run_place(core_arr, full, back_0a, 0, width, 0)
    full = run_place(core_arr, full, back_0b, 0, width, split)
    full = run_place(core_arr, full, back_1a, 1, width, 0)
    mamba_output = run_place(core_arr, full, back_1b, 1, width, split)
    return (mamba_output, attention_output)


def solution(mesh):
    blk_count = mesh.shape["blk"]
    ulys_count = mesh.shape["ulys"]
    fine = Mesh(
        mesh.devices.reshape(blk_count, ulys_count // PAIR, PAIR), ("blk", "chip", "core")
    )
    rows = P(("blk", "chip", "core"), None)
    col = ("chip", "core")
    placed = (
        rows, rows, rows, rows,
        P(None, col), P(col), P(None, col), P(col), P(None, col), P(col),
        rows, rows, rows,
        P(),
    )
    return jax.shard_map(
        local, mesh=fine, in_specs=placed, out_specs=(rows, rows), check_vma=False
    )
```

```python
import functools

import jax
import jax.numpy as jnp
from jax import lax
from jax.experimental import pallas as pl
from jax.experimental.pallas import tpu as pltpu
from jax.sharding import Mesh
from jax.sharding import PartitionSpec as P


STATE = 16
CONV = 4
HD = 128
SPAN = 1024
LANES = 128
PAIR = 2
GROUP = 16
PIECES = 2
ONES = 16
NEG_LARGE = -1e30
LOG2E = 1.4426950408889634
PARAM_ROWS = 24
VMEM_LIMIT = 56 * 1024 * 1024


def softplus(x):
    return jnp.maximum(x, 0.0) + jnp.log1p(jnp.exp(-jnp.abs(x)))


def silu(x):
    half = 0.5 * x
    return half * jnp.tanh(half) + half


def lane_tiles(cols):
    size = min(LANES, cols)
    return [slice(at, at + size) for at in range(0, cols, size)]


def spread(ref, k, row, count):
    return jnp.broadcast_to(ref[k, pl.ds(row, 1), :], (count, ref.shape[2]))


def scan_kernel(
    core_ref, own_ref, other_ref, halo_ref, low_own_ref, low_other_ref, param_ref, inject_ref,
    read_ref, *refs, sources,
):
    weight_refs = refs[:sources]
    delta_ref, y_ref, sent_ref = refs[sources : sources + 3]
    x_scr, driven_scr, push_scr, hist_scr, rate_scr, param_scr = refs[sources + 3 :]
    core = core_ref[0]
    tokens, cols = y_ref.shape
    half = tokens // 2
    depth = low_own_ref.shape[1]
    tiles = lane_tiles(cols)
    mine = pl.multiple_of(core * half, 8)
    theirs = pl.multiple_of((1 - core) * half, 8)
    weight = jnp.concatenate(
        [ref[...].reshape(depth // sources, cols) for ref in weight_refs], axis=0
    )
    raw_mine = jnp.dot(low_own_ref[...], weight, preferred_element_type=jnp.float32)
    for k, tile in enumerate(tiles):
        delta_ref[k, pl.ds(mine, half), :] = raw_mine[:, tile]
    raw_theirs = jnp.dot(low_other_ref[...], weight, preferred_element_type=jnp.float32)
    for k, tile in enumerate(tiles):
        delta_ref[k, pl.ds(theirs, half), :] = raw_theirs[:, tile]
    for k, tile in enumerate(tiles):
        x_scr[k, 0:8, :] = halo_ref[:, tile].astype(jnp.float32)
        x_scr[k, pl.ds(8 + mine, half), :] = own_ref[:, tile].astype(jnp.float32)
        x_scr[k, pl.ds(8 + theirs, half), :] = other_ref[:, tile].astype(jnp.float32)
    rate_scr[...] = -LOG2E * jnp.exp(param_ref[0, :STATE, :])
    for k in range(CONV + 3):
        param_scr[8 * k : 8 * k + 8, :] = jnp.broadcast_to(
            param_ref[0, STATE + k : STATE + k + 1, :], (8, cols)
        )

    def prepare(step, total):
        first = pl.multiple_of(step * 8, 8)
        total = list(total)
        for k, tile in enumerate(tiles):
            mixed = param_scr[8 * CONV : 8 * CONV + 8, tile]
            for j in range(CONV):
                shifted = x_scr[k, pl.ds(first + 8 - (CONV - 1) + j, 8), :]
                mixed = mixed + param_scr[8 * j : 8 * j + 8, tile] * shifted
            driven = silu(mixed)
            delta = softplus(
                delta_ref[k, pl.ds(first, 8), :] + param_scr[8 * CONV + 8 : 8 * CONV + 16, tile]
            )
            delta_ref[k, pl.ds(first, 8), :] = delta
            driven_scr[pl.ds(first, 8), tile] = driven * param_scr[8 * CONV + 16 : 8 * CONV + 24, tile]
            push_scr[k, pl.ds(first, 8), :] = driven * delta
            total[k] = total[k] + delta
        return tuple(total)

    zero = jnp.zeros((8, tiles[0].stop), jnp.float32)
    total = lax.fori_loop(0, tokens // 8, prepare, (zero,) * len(tiles))
    total = jnp.sum(jnp.concatenate(total, axis=1), axis=0, keepdims=True)

    def step16(group, hidden):
        base = pl.multiple_of(group * GROUP, GROUP)
        hidden = list(hidden)
        for i in range(GROUP):
            inject = inject_ref[pl.ds(pl.multiple_of((base + i) * STATE, STATE), STATE), :]
            for k, tile in enumerate(tiles):
                decay = jnp.exp2(spread(delta_ref, k, base + i, STATE) * rate_scr[:, tile])
                push = spread(push_scr, k, base + i, STATE)
                hidden[k] = decay * hidden[k] + push * inject
            hist_scr[i * STATE : (i + 1) * STATE, :] = jnp.concatenate(hidden, axis=1).astype(
                jnp.bfloat16
            )
        read = read_ref[pl.ds(base, GROUP), :]
        out = jnp.dot(read, hist_scr[...], preferred_element_type=jnp.float32)
        y_ref[pl.ds(base, GROUP), :] = (out + driven_scr[pl.ds(base, GROUP), :]).astype(y_ref.dtype)
        return tuple(hidden)

    zero = jnp.zeros((STATE, tiles[0].stop), jnp.float32)
    end = lax.fori_loop(0, tokens // GROUP, step16, (zero,) * len(tiles))
    end = jnp.concatenate(end, axis=1)
    top = total.astype(jnp.bfloat16).astype(jnp.float32)
    mid = (total - top).astype(jnp.bfloat16).astype(jnp.float32)
    low = total - top - mid
    row = lax.broadcasted_iota(jnp.int32, (STATE, cols), 0)
    rows = jnp.where(row == 0, top, jnp.where(row == 1, mid, jnp.where(row == 2, low, 0.0)))
    share = sent_ref.shape[2]
    for k in range(sent_ref.shape[0]):
        at = slice(k * share, (k + 1) * share)
        sent_ref[k, :STATE, :] = end[:, at].astype(sent_ref.dtype)
        sent_ref[k, STATE:, :] = rows[:, at].astype(sent_ref.dtype)


def correct_body(
    core_ref, delta_ref, y_ref, enter_ref, param_ref, read_ref, own_gate_ref, other_gate_ref,
    mine_ref, theirs_ref, hist_scr, out_scr, rate_scr, enter_scr,
):
    core = core_ref[0]
    enter_scr[...] = jnp.concatenate([enter_ref[k] for k in range(enter_ref.shape[0])], axis=1)
    tokens, cols = y_ref.shape
    half = tokens // 2
    rate_scr[...] = -LOG2E * jnp.exp(param_ref[0, :STATE, :])

    tiles = lane_tiles(cols)

    def step16(group, elapsed):
        base = pl.multiple_of(group * GROUP, GROUP)
        elapsed = list(elapsed)
        for i in range(GROUP):
            carried = []
            for k, tile in enumerate(tiles):
                elapsed[k] = elapsed[k] + spread(delta_ref, k, base + i, 8)
                twice = jnp.concatenate([elapsed[k], elapsed[k]], axis=0)
                carried.append(jnp.exp2(twice * rate_scr[:, tile]))
            carried = jnp.concatenate(carried, axis=1).astype(jnp.bfloat16)
            hist_scr[i * STATE : (i + 1) * STATE, :] = carried * enter_scr[...]
        read = read_ref[pl.ds(base, GROUP), :]
        out = jnp.dot(read, hist_scr[...], preferred_element_type=jnp.float32)
        total = out + y_ref[pl.ds(base, GROUP), :].astype(jnp.float32)
        out_scr[pl.ds(base, GROUP), :] = total.astype(jnp.bfloat16).astype(jnp.float32)
        return tuple(elapsed)

    zero = jnp.zeros((8, tiles[0].stop), jnp.float32)
    lax.fori_loop(0, tokens // GROUP, step16, (zero,) * len(tiles))
    rows = 16

    def gated(gate_ref, dest_ref, offset):
        def body(step, carry):
            first = pl.multiple_of(step * rows, rows)
            gate = gate_ref[pl.ds(first, rows), :].astype(jnp.float32)
            value = out_scr[pl.ds(pl.multiple_of(offset + first, 8), rows), :]
            dest_ref[pl.ds(first, rows), :] = (value * silu(gate)).astype(dest_ref.dtype)
            return carry

        lax.fori_loop(0, half // rows, body, 0)

    gated(own_gate_ref, mine_ref, core * half)
    gated(other_gate_ref, theirs_ref, (1 - core) * half)


def correct_kernel(core_ref, *refs, resumed):
    correct_body(core_ref, *(refs[1:] if resumed else refs))


def combine_kernel(order_ref, got_ref, rate_ref, enter_ref):
    chunks = got_ref.shape[0]
    rates = rate_ref[...]

    def body(place, state):
        chunk = order_ref[place]
        enter_ref[chunk] = state.astype(enter_ref.dtype)
        got = got_ref[chunk].astype(jnp.float32)
        total = got[STATE : STATE + 1] + got[STATE + 1 : STATE + 2] + got[STATE + 2 : STATE + 3]
        return jnp.exp2(total * rates) * state + got[:STATE]

    lax.fori_loop(0, chunks, body, jnp.zeros(rates.shape, jnp.float32))


def copy_kernel(core_ref, in_ref, out_ref):
    out_ref[...] = in_ref[...]


def place_kernel(core_ref, buffer_ref, in_ref, out_ref):
    out_ref[...] = in_ref[...]


def flash_kernel(
    side_ref, flip_ref, half_ref, diag_ref, first_ref, last_ref, q_ref, *refs, heads, rows, sources,
):
    kv_refs = refs[:sources]
    out_ref, query_scr, key_scr, value_scr, max_scr, acc_scr = refs[sources:]
    step = pl.program_id(0)
    scale = LOG2E * HD ** (-0.5)
    wide = 2 * HD
    span = q_ref.shape[0]

    for source in range(sources):

        @pl.when(flip_ref[step] == source)
        def _(kv_ref=kv_refs[source]):
            key_scr[:, :HD] = kv_ref[:, :HD]
            key_scr[:, HD:] = kv_ref[:, :HD]
            value_scr[:HD, :] = kv_ref[:, HD:].T

    value_scr[HD:, :] = jnp.ones((ONES, span), jnp.bfloat16)

    @pl.when(first_ref[step] == 1)
    def _():
        max_scr[...] = jnp.full(max_scr.shape, NEG_LARGE, jnp.float32)
        acc_scr[...] = jnp.zeros(acc_scr.shape, jnp.float32)
        for head in range(heads):
            scaled = q_ref[:, head * HD : (head + 1) * HD].astype(jnp.float32) * scale
            coarse = scaled.astype(jnp.bfloat16)
            query_scr[:, head * wide : head * wide + HD] = coarse
            query_scr[:, head * wide + HD : (head + 1) * wide] = (
                scaled - coarse.astype(jnp.float32)
            ).astype(jnp.bfloat16)

    def score(head, row, key_count, masked):
        q = query_scr[row : row + rows, head * wide : (head + 1) * wide]
        scores = lax.dot_general(
            key_scr[:key_count, :], q, (((1,), (1,)), ((), ())),
            preferred_element_type=jnp.float32,
        )
        if masked:
            last = scores[row:, :]
            key_at = lax.broadcasted_iota(jnp.int32, last.shape, 0)
            query_at = lax.broadcasted_iota(jnp.int32, last.shape, 1)
            last = jnp.where(key_at <= query_at, last, NEG_LARGE)
            scores = jnp.concatenate([scores[:row, :], last], axis=0) if row else last
        return scores

    def absorb(head, row, key_count, scores):
        at = slice(row, row + rows)
        old_max = max_scr[head, 0:1, at]
        new_max = jnp.maximum(old_max, jnp.max(scores, axis=0, keepdims=True))
        weights = jnp.exp2(scores - new_max).astype(jnp.bfloat16)
        shrink = jnp.exp2(old_max - new_max)
        acc_scr[head, :, at] = acc_scr[head, :, at] * shrink + jnp.dot(
            value_scr[:, :key_count], weights, preferred_element_type=jnp.float32
        )
        max_scr[head, :, at] = jnp.broadcast_to(new_max, (8, rows))

    def sweep(masked):
        work = [(head, row) for head in range(heads) for row in range(0, span, rows)]
        count = [row + rows if masked else span for _, row in work]
        ahead = score(*work[0], count[0], masked)
        for i, (head, row) in enumerate(work):
            scores = ahead
            if i + 1 < len(work):
                ahead = score(*work[i + 1], count[i + 1], masked)
            absorb(head, row, count[i], scores)

    @pl.when(diag_ref[step] == 0)
    def _():
        sweep(False)

    @pl.when(diag_ref[step] == 1)
    def _():
        sweep(True)

    @pl.when(last_ref[step] == 1)
    def _():
        for head in range(heads):
            for row in range(0, span, rows):
                at = slice(row, row + rows)
                ratio = acc_scr[head, :HD, at] / acc_scr[head, HD : HD + 1, at]
                out_ref[at, head * HD : (head + 1) * HD] = ratio.T.astype(out_ref.dtype)


def whole(shape):
    return pl.BlockSpec(
        shape, lambda j, core_ref: (0,) * len(shape), pipeline_mode=pl.Buffered(1)
    )


def shard_map_of(side, piece, first=0):
    return lambda j, core_ref: (
        0, (PAIR * (j + first) + (core_ref[0] + side) % PAIR) * PIECES + piece,
    )


def param_spec(count, width, piece, first):
    return pl.BlockSpec(
        (1, PARAM_ROWS, width),
        lambda j, core_ref: (lax.rem(core_ref[1] + count - (j + first), count), 0, piece),
    )


def plain(j, core_ref):
    return (0, j)


def run_pick(core, full, piece, width):
    half, inner = full.shape
    blocks = inner // (width * PIECES * PAIR)
    return pl.pallas_call(
        copy_kernel,
        grid_spec=pltpu.PrefetchScalarGridSpec(
            num_scalar_prefetch=1,
            grid=(blocks,),
            in_specs=[pl.BlockSpec((half, width), shard_map_of(1, piece))],
            out_specs=pl.BlockSpec((half, width), plain),
        ),
        out_shape=jax.ShapeDtypeStruct((half, blocks * width), full.dtype),
        name="pick_channels",
    )(core, full)


def run_place(core, full, part, piece, width, first):
    half, _ = full.shape
    blocks = part.shape[1] // width
    return pl.pallas_call(
        place_kernel,
        grid_spec=pltpu.PrefetchScalarGridSpec(
            num_scalar_prefetch=1,
            grid=(blocks,),
            in_specs=[pl.BlockSpec(memory_space=pl.ANY), pl.BlockSpec((half, width), plain)],
            out_specs=pl.BlockSpec((half, width), shard_map_of(1, piece, first)),
        ),
        out_shape=jax.ShapeDtypeStruct(full.shape, full.dtype),
        input_output_aliases={1: 0},
        name="place_channels",
    )(core, full, part)


def weight_spec(weight, width, shards, first):
    if weight.ndim == 4:
        parts, _, rows, _ = weight.shape
        return pl.BlockSpec((parts, 1, rows, width), lambda j, core_ref: (0, j + first, 0, 0))
    return pl.BlockSpec(
        (1, weight.shape[1], width),
        lambda j, core_ref: (lax.rem(core_ref[1] + shards - (j + first), shards), 0, 0),
    )


def run_scan(
    core, x_own, x_other, halo, low_own, low_other, weights, params, inject, read, piece, width, share,
    first, blocks,
):
    half = x_other.shape[0]
    cols = blocks * width
    tokens = 2 * half
    shards = params.shape[0]
    sources = len(weights)

    def shifted(j, core_ref):
        return (0, j + first)

    lanes = min(LANES, width)
    tiles = width // lanes
    return pl.pallas_call(
        functools.partial(scan_kernel, sources=sources),
        grid_spec=pltpu.PrefetchScalarGridSpec(
            num_scalar_prefetch=1,
            grid=(blocks,),
            in_specs=[
                pl.BlockSpec((half, width), shard_map_of(0, piece, first)),
                pl.BlockSpec((half, width), shifted),
                pl.BlockSpec((8, width), lambda j, core_ref: (0, piece * shards + j + first)),
                whole(low_own.shape),
                whole(low_other.shape),
                param_spec(shards, width, piece, first),
                whole(inject.shape),
                whole(read.shape),
            ]
            + [weight_spec(weight, width, shards, first) for weight in weights],
            out_specs=[
                pl.BlockSpec((tiles, tokens, lanes), lambda j, core_ref: (j, 0, 0)),
                pl.BlockSpec((tokens, width), plain),
                pl.BlockSpec((width // share, 2 * STATE, share), lambda j, core_ref: (j, 0, 0)),
            ],
            scratch_shapes=[
                pltpu.VMEM((tiles, tokens + 8, lanes), jnp.float32),
                pltpu.VMEM((tokens, width), jnp.float32),
                pltpu.VMEM((tiles, tokens, lanes), jnp.float32),
                pltpu.VMEM((GROUP * STATE, width), jnp.bfloat16),
                pltpu.VMEM((STATE, width), jnp.float32),
                pltpu.VMEM((8 * (CONV + 3), width), jnp.float32),
            ],
        ),
        out_shape=[
            jax.ShapeDtypeStruct((cols // lanes, tokens, lanes), jnp.float32),
            jax.ShapeDtypeStruct((tokens, cols), jnp.bfloat16),
            jax.ShapeDtypeStruct((cols // share, 2 * STATE, share), jnp.bfloat16),
        ],
        compiler_params=pltpu.CompilerParams(vmem_limit_bytes=VMEM_LIMIT),
        name="token_scan",
    )(core, x_own, x_other, halo, low_own, low_other, params, inject, read, *weights)


def run_correct(
    core, full, delta, y, enter, params, read, gate_own, gate_other, piece, width, first, inside, blocks
):
    tokens = y.shape[0]
    half, inner = gate_own.shape
    cols = blocks * width
    lanes = delta.shape[2]
    tiles = width // lanes
    share = enter.shape[2]
    resumed = full is not None
    first_spec = [pl.BlockSpec(memory_space=pl.ANY)] if resumed else []
    first_arg = (full,) if resumed else ()
    return pl.pallas_call(
        functools.partial(correct_kernel, resumed=resumed),
        grid_spec=pltpu.PrefetchScalarGridSpec(
            num_scalar_prefetch=1,
            grid=(blocks,),
            in_specs=first_spec
            + [
                pl.BlockSpec((tiles, tokens, lanes), lambda j, core_ref: (j + inside, 0, 0)),
                pl.BlockSpec((tokens, width), lambda j, core_ref: (0, j + inside)),
                pl.BlockSpec((width // share, STATE, share), lambda j, core_ref: (j + first, 0, 0)),
                param_spec(params.shape[0], width, piece, first),
                whole(read.shape),
                pl.BlockSpec((half, width), shard_map_of(0, piece, first)),
                pl.BlockSpec((half, width), lambda j, core_ref: (0, j + first)),
            ],
            out_specs=[
                pl.BlockSpec((half, width), shard_map_of(0, piece, first)),
                pl.BlockSpec((half, width), plain),
            ],
            scratch_shapes=[
                pltpu.VMEM((GROUP * STATE, width), jnp.bfloat16),
                pltpu.VMEM((tokens, width), jnp.float32),
                pltpu.VMEM((STATE, width), jnp.float32),
                pltpu.VMEM((STATE, width), jnp.bfloat16),
            ],
        ),
        out_shape=[
            jax.ShapeDtypeStruct((half, inner), jnp.bfloat16),
            jax.ShapeDtypeStruct((half, cols), jnp.bfloat16),
        ],
        input_output_aliases={1: 0} if resumed else {},
        compiler_params=pltpu.CompilerParams(vmem_limit_bytes=VMEM_LIMIT),
        name="state_correction",
    )(core, *first_arg, delta, y, enter, params, read, gate_own, gate_other)


def run_combine(order, got, rates):
    chunks, _, cols = got.shape
    return pl.pallas_call(
        combine_kernel,
        grid_spec=pltpu.PrefetchScalarGridSpec(
            num_scalar_prefetch=1,
            grid=(1,),
            in_specs=[
                pl.BlockSpec(got.shape, lambda i, o: (0, 0, 0)),
                pl.BlockSpec(rates.shape, lambda i, o: (0, 0)),
            ],
            out_specs=pl.BlockSpec((chunks, STATE, cols), lambda i, o: (0, 0, 0)),
        ),
        out_shape=jax.ShapeDtypeStruct((chunks, STATE, cols), jnp.bfloat16),
        compiler_params=pltpu.CompilerParams(vmem_limit_bytes=VMEM_LIMIT),
        name="state_combine",
    )(order, got, rates)


def run_flash(tables, q, kv_parts, rows=512):
    _, width = q.shape
    heads = width // HD
    steps = tables[0].shape[0]
    sources = len(kv_parts)

    def q_map(s, side, flip, half, diag, first, last):
        return (side[s], 0)

    def kv_map(s, side, flip, half, diag, first, last):
        return (half[s], 0)

    return pl.pallas_call(
        functools.partial(flash_kernel, heads=heads, rows=rows, sources=sources),
        grid_spec=pltpu.PrefetchScalarGridSpec(
            num_scalar_prefetch=6,
            grid=(steps,),
            in_specs=[pl.BlockSpec((SPAN, width), q_map)]
            + [pl.BlockSpec((SPAN, 2 * HD), kv_map)] * sources,
            out_specs=pl.BlockSpec((SPAN, width), q_map),
            scratch_shapes=[
                pltpu.VMEM((SPAN, 2 * width), jnp.bfloat16),
                pltpu.VMEM((SPAN, 2 * HD), jnp.bfloat16),
                pltpu.VMEM((HD + ONES, SPAN), jnp.bfloat16),
                pltpu.VMEM((heads, 8, SPAN), jnp.float32),
                pltpu.VMEM((heads, HD + ONES, SPAN), jnp.float32),
            ],
        ),
        out_shape=jax.ShapeDtypeStruct(q.shape, jnp.bfloat16),
        compiler_params=pltpu.CompilerParams(vmem_limit_bytes=VMEM_LIMIT),
        name="causal_attention",
    )(*tables, q, *kv_parts)


def flash_tables(span_order, my_blocks, blk):
    block_total = span_order.shape[0]
    places = jnp.arange(block_total, dtype=jnp.int32)
    holder = jnp.sum(jnp.where(span_order[None, :] == places[:, None], places[None, :], 0), axis=1)
    steps = jnp.arange(block_total + 1, dtype=jnp.int32)
    first_count = my_blocks[0] + 1
    side = (steps >= first_count).astype(jnp.int32)
    place = jnp.where(side == 1, steps - first_count, steps)
    limit = jnp.where(side == 1, my_blocks[1], my_blocks[0])
    block = jnp.sum(jnp.where(places[None, :] == place[:, None], holder[None, :], 0), axis=1)
    block = block.astype(jnp.int32)
    last = (place == limit).astype(jnp.int32)
    first = (place == 0).astype(jnp.int32)
    return (side, (block // 2) ^ blk.astype(jnp.int32), block % 2, last, first, last)


def local(
    mamba_input, gate_input, delta_low, state_mixers, conv_weight, conv_bias, delta_weight,
    delta_bias, decay_log, skip_gain, queries, key_rows, value_rows, span_order,
):
    blk = lax.axis_index("blk")
    chip = lax.axis_index("chip")
    core = lax.axis_index("core")
    blk_count = lax.axis_size("blk")
    chip_count = lax.axis_size("chip")
    ulys = ("chip", "core")
    chips = ("blk", "chip")
    ulys_count = chip_count * PAIR
    chunks = blk_count * chip_count
    block_total = span_order.shape[0]
    half, _ = mamba_input.shape
    tokens = PAIR * half
    shard_cols = delta_weight.shape[1]
    width = shard_cols // PIECES
    cols = chip_count * width
    swap = [(0, 1), (1, 0)]
    core_arr = jnp.stack([core, chip]).astype(jnp.int32)
    my_blocks = lax.dynamic_slice_in_dim(span_order, 2 * blk, 2, 0)

    depth = delta_weight.shape[0]
    part_rows = depth // blk_count
    part = lax.dynamic_slice_in_dim(delta_weight, blk * part_rows, part_rows, 0)
    far_moves = [
        [(i, (i + far) % chip_count) for i in range(chip_count)] for far in range(1, chip_count)
    ]
    flips = [[(i, i ^ flip) for i in range(blk_count)] for flip in range(1, blk_count)]
    part_first, part_later = part[:, :width], part[:, width:]
    shards_first = jnp.stack(
        [part_first] + [lax.ppermute(part_first, "chip", move) for move in far_moves]
    )
    weights_first = [shards_first] + [
        lax.ppermute(shards_first, "blk", move) for move in flips
    ]
    weights_later = lax.all_gather(part_later, chips, axis=0, tiled=False)
    weights_later = [weights_later.reshape(blk_count, chip_count, part_rows, width)]

    def by_flip(low):
        return jnp.concatenate(
            [
                lax.dynamic_slice_in_dim(low, (blk ^ flip) * part_rows, part_rows, 1)
                for flip in range(blk_count)
            ],
            axis=1,
        )

    kv_heads = key_rows.shape[1] // HD
    repeat = ulys_count // kv_heads
    kv_rows = jnp.stack(
        [key_rows.reshape(half, kv_heads, HD), value_rows.reshape(half, kv_heads, HD)], axis=2
    )
    kv_rows = jnp.broadcast_to(
        kv_rows[:, :, None], (half, kv_heads, repeat, 2, HD)
    ).reshape(half, ulys_count * 2 * HD)
    kv_rows, _ = lax.optimization_barrier((kv_rows, shards_first))
    kv_local = lax.all_to_all(kv_rows, ulys, split_axis=1, concat_axis=0, tiled=True)

    packed = jnp.concatenate(
        [
            decay_log,
            conv_weight.astype(jnp.float32),
            conv_bias[None],
            delta_bias[None],
            skip_gain[None],
            jnp.zeros((1, shard_cols), jnp.float32),
        ],
        axis=0,
    )
    x_other = [
        lax.ppermute(run_pick(core_arr, mamba_input, piece, width), "core", swap)
        for piece in range(PIECES)
    ]
    low_other = lax.ppermute(delta_low, "core", swap)
    mixers_other = lax.ppermute(state_mixers, "core", swap)
    mixers = jnp.where(
        core == 0,
        jnp.concatenate([state_mixers, mixers_other], axis=0),
        jnp.concatenate([mixers_other, state_mixers], axis=0),
    )
    inject = jnp.broadcast_to(
        mixers[:, :STATE].astype(jnp.float32).reshape(tokens * STATE, 1), (tokens * STATE, LANES)
    )
    same = jnp.arange(tokens, dtype=jnp.int32)[:, None] % GROUP == jnp.arange(GROUP, dtype=jnp.int32)
    read = jnp.where(
        same[:, :, None], mixers[:, None, STATE:], jnp.zeros((), jnp.bfloat16)
    ).reshape(tokens, GROUP * STATE)

    per_block = SPAN // tokens
    chunk_ids = jnp.arange(chunks, dtype=jnp.int32)
    stored = chunk_ids // per_block
    block_ids = jnp.arange(block_total, dtype=jnp.int32)
    block_pos = jnp.sum(
        jnp.where(stored[:, None] == block_ids[None, :], span_order[None, :], 0), axis=1
    )
    chunk_pos = block_pos * per_block + chunk_ids % per_block
    order = jnp.sum(
        jnp.where(chunk_pos[None, :] == chunk_ids[:, None], chunk_ids[None, :], 0), axis=1
    ).astype(jnp.int32)
    me = blk * chip_count + chip
    my_pos = jnp.sum(jnp.where(chunk_ids == me, chunk_pos, 0))
    own_tail = lax.dynamic_index_in_dim(
        mamba_input[half - (CONV - 1) :].reshape(CONV - 1, chip_count, PAIR, PIECES, width),
        core, 2, False,
    ).swapaxes(1, 2).reshape(CONV - 1, PIECES * cols)
    other_tail = jnp.concatenate([x[half - (CONV - 1) :] for x in x_other], axis=1)
    tail = jnp.where(core == 1, own_tail, other_tail)
    gate_other = [
        lax.ppermute(run_pick(core_arr, gate_input, piece, width), "core", swap)
        for piece in range(PIECES)
    ]

    params = jnp.stack([packed] + [lax.ppermute(packed, "chip", move) for move in far_moves])

    kv_local, tail = lax.optimization_barrier((kv_local, tail))
    tails = lax.all_to_all(
        jnp.broadcast_to(tail[None], (chunks, CONV - 1, PIECES * cols)), chips,
        split_axis=0, concat_axis=0, tiled=True,
    )
    before = (chunk_pos == my_pos - 1).astype(jnp.bfloat16)
    halo = jnp.einsum("m,mkc->kc", before, tails, preferred_element_type=jnp.float32)
    halo = jnp.concatenate(
        [jnp.zeros((8 - (CONV - 1), PIECES * cols), jnp.bfloat16), halo.astype(jnp.bfloat16)],
        axis=0,
    )

    share = cols // chunks
    split = chip_count // 2

    def scan_part(piece, x_piece, lows, weights, first, blocks):
        return run_scan(
            core_arr, mamba_input, x_piece, halo, *lows, weights, params, inject, read, piece,
            width, share, first, blocks,
        )

    def rates_of(piece):
        at = me * share
        shard = at // width
        far = (chip + chip_count - shard) % chip_count
        mine = lax.dynamic_slice(
            params, (far, 0, piece * width + at % width), (1, STATE, share)
        )
        return -LOG2E * jnp.exp(mine[0])

    my_rates = [rates_of(piece) for piece in range(PIECES)]

    def to_owners(array):
        return lax.all_to_all(array, chips, split_axis=0, concat_axis=0, tiled=True)

    def correct_part(full, made, enter, piece, first, inside, blocks):
        delta, y = made[:2]
        return run_correct(
            core_arr, full, delta, y, enter, params, read, gate_input, gate_other[piece], piece,
            width, first, inside, blocks,
        )

    lows_first = (by_flip(delta_low), by_flip(low_other))
    lows_later = (delta_low, low_other)
    tables = flash_tables(span_order, my_blocks, blk)
    x_now, gate_other, my_rates, tables, order = lax.optimization_barrier(
        (x_other[0], gate_other, my_rates, tables, order)
    )
    made_0 = scan_part(0, x_now, lows_first, weights_first, 0, chip_count)
    halo, queries, kv_local = lax.optimization_barrier((halo, queries, kv_local))
    q_local = lax.all_to_all(queries, ulys, split_axis=1, concat_axis=0, tiled=True)
    kv_parts = [kv_local] + [lax.ppermute(kv_local, "blk", move) for move in flips]
    x_now, sent_0, q_local, kv_parts, my_rates = lax.optimization_barrier(
        (x_other[1], made_0[2], q_local, kv_parts, my_rates)
    )
    got_0 = to_owners(sent_0)
    made_1a = scan_part(1, x_now, lows_later, weights_later, 0, split)
    x_now, got_0, sent_1a = lax.optimization_barrier((x_now, got_0, made_1a[2]))
    enter_0 = to_owners(run_combine(order, got_0, my_rates[0]))
    made_1b = scan_part(1, x_now, lows_later, weights_later, split, chip_count - split)
    enter_0, sent_1, q_local = lax.optimization_barrier(
        (enter_0, jnp.concatenate([sent_1a, made_1b[2]], axis=0), q_local)
    )
    got_1 = to_owners(sent_1)
    attended = run_flash(tables, q_local, kv_parts)
    enter_0, got_1, attended = lax.optimization_barrier((enter_0, got_1, attended))
    enter_1 = to_owners(run_combine(order, got_1, my_rates[1]))
    full, theirs_0 = correct_part(None, made_0, enter_0, 0, 0, 0, chip_count)
    full, enter_1, attended = lax.optimization_barrier((full, enter_1, attended))
    back_0 = lax.ppermute(theirs_0, "core", swap)
    attention_output = lax.all_to_all(attended, ulys, split_axis=0, concat_axis=1, tiled=True)
    full, theirs_1a = correct_part(full, made_1a, enter_1, 1, 0, 0, split)
    back_1a = lax.ppermute(theirs_1a, "core", swap)
    full, theirs_1b = correct_part(full, made_1b, enter_1, 1, split, 0, chip_count - split)
    back_1b = lax.ppermute(theirs_1b, "core", swap)
    full = run_place(core_arr, full, back_0, 0, width, 0)
    full = run_place(core_arr, full, back_1a, 1, width, 0)
    mamba_output = run_place(core_arr, full, back_1b, 1, width, split)
    return (mamba_output, attention_output)


def solution(mesh):
    blk_count = mesh.shape["blk"]
    ulys_count = mesh.shape["ulys"]
    fine = Mesh(
        mesh.devices.reshape(blk_count, ulys_count // PAIR, PAIR), ("blk", "chip", "core")
    )
    rows = P(("blk", "chip", "core"), None)
    col = ("chip", "core")
    placed = (
        rows, rows, rows, rows,
        P(None, col), P(col), P(None, col), P(col), P(None, col), P(col),
        rows, rows, rows,
        P(),
    )

    return jax.shard_map(local, mesh=fine, in_specs=placed, out_specs=(rows, rows), check_vma=False)
```

```python
import functools

import jax
import jax.numpy as jnp
from jax import lax
from jax.experimental import pallas as pl
from jax.experimental.pallas import tpu as pltpu
from jax.sharding import Mesh
from jax.sharding import PartitionSpec as P


STATE = 16
CONV = 4
HD = 128
SPAN = 1024
LANES = 128
PAIR = 2
GROUP = 16
PIECES = 2
ONES = 16
NEG_LARGE = -1e30
LOG2E = 1.4426950408889634
PARAM_ROWS = 24
VMEM_LIMIT = 56 * 1024 * 1024


def softplus(x):
    return jnp.maximum(x, 0.0) + jnp.log1p(jnp.exp(-jnp.abs(x)))


def silu(x):
    half = 0.5 * x
    return half * jnp.tanh(half) + half


def lane_tiles(cols):
    size = min(LANES, cols)
    return [slice(at, at + size) for at in range(0, cols, size)]


def spread(ref, k, row, count):
    return jnp.broadcast_to(ref[k, pl.ds(row, 1), :], (count, ref.shape[2]))


def scan_kernel(
    core_ref, own_ref, other_ref, halo_ref, low_own_ref, low_other_ref, param_ref, inject_ref,
    read_ref, *refs, sources,
):
    weight_refs = refs[:sources]
    delta_ref, y_ref, sent_ref = refs[sources : sources + 3]
    x_scr, driven_scr, push_scr, hist_scr, rate_scr, param_scr = refs[sources + 3 :]
    core = core_ref[0]
    tokens, cols = y_ref.shape
    half = tokens // 2
    depth = low_own_ref.shape[1]
    tiles = lane_tiles(cols)
    mine = pl.multiple_of(core * half, 8)
    theirs = pl.multiple_of((1 - core) * half, 8)
    weight = jnp.concatenate(
        [ref[...].reshape(depth // sources, cols) for ref in weight_refs], axis=0
    )
    raw_mine = jnp.dot(low_own_ref[...], weight, preferred_element_type=jnp.float32)
    for k, tile in enumerate(tiles):
        delta_ref[k, pl.ds(mine, half), :] = raw_mine[:, tile]
    raw_theirs = jnp.dot(low_other_ref[...], weight, preferred_element_type=jnp.float32)
    for k, tile in enumerate(tiles):
        delta_ref[k, pl.ds(theirs, half), :] = raw_theirs[:, tile]
    for k, tile in enumerate(tiles):
        x_scr[k, 0:8, :] = halo_ref[:, tile].astype(jnp.float32)
        x_scr[k, pl.ds(8 + mine, half), :] = own_ref[:, tile].astype(jnp.float32)
        x_scr[k, pl.ds(8 + theirs, half), :] = other_ref[:, tile].astype(jnp.float32)
    rate_scr[...] = -LOG2E * jnp.exp(param_ref[0, :STATE, :])
    for k in range(CONV + 3):
        param_scr[8 * k : 8 * k + 8, :] = jnp.broadcast_to(
            param_ref[0, STATE + k : STATE + k + 1, :], (8, cols)
        )

    def prepare(step, total):
        first = pl.multiple_of(step * 8, 8)
        total = list(total)
        for k, tile in enumerate(tiles):
            mixed = param_scr[8 * CONV : 8 * CONV + 8, tile]
            for j in range(CONV):
                shifted = x_scr[k, pl.ds(first + 8 - (CONV - 1) + j, 8), :]
                mixed = mixed + param_scr[8 * j : 8 * j + 8, tile] * shifted
            driven = silu(mixed)
            delta = softplus(
                delta_ref[k, pl.ds(first, 8), :] + param_scr[8 * CONV + 8 : 8 * CONV + 16, tile]
            )
            delta_ref[k, pl.ds(first, 8), :] = delta
            driven_scr[pl.ds(first, 8), tile] = driven * param_scr[8 * CONV + 16 : 8 * CONV + 24, tile]
            push_scr[k, pl.ds(first, 8), :] = driven * delta
            total[k] = total[k] + delta
        return tuple(total)

    zero = jnp.zeros((8, tiles[0].stop), jnp.float32)
    total = lax.fori_loop(0, tokens // 8, prepare, (zero,) * len(tiles))
    total = jnp.sum(jnp.concatenate(total, axis=1), axis=0, keepdims=True)

    def step16(group, hidden):
        base = pl.multiple_of(group * GROUP, GROUP)
        hidden = list(hidden)
        for i in range(GROUP):
            inject = inject_ref[pl.ds(pl.multiple_of((base + i) * STATE, STATE), STATE), :]
            for k, tile in enumerate(tiles):
                decay = jnp.exp2(spread(delta_ref, k, base + i, STATE) * rate_scr[:, tile])
                push = spread(push_scr, k, base + i, STATE)
                hidden[k] = decay * hidden[k] + push * inject
            hist_scr[i * STATE : (i + 1) * STATE, :] = jnp.concatenate(hidden, axis=1).astype(
                jnp.bfloat16
            )
        read = read_ref[pl.ds(base, GROUP), :]
        out = jnp.dot(read, hist_scr[...], preferred_element_type=jnp.float32)
        y_ref[pl.ds(base, GROUP), :] = (out + driven_scr[pl.ds(base, GROUP), :]).astype(y_ref.dtype)
        return tuple(hidden)

    zero = jnp.zeros((STATE, tiles[0].stop), jnp.float32)
    end = lax.fori_loop(0, tokens // GROUP, step16, (zero,) * len(tiles))
    end = jnp.concatenate(end, axis=1)
    top = total.astype(jnp.bfloat16).astype(jnp.float32)
    mid = (total - top).astype(jnp.bfloat16).astype(jnp.float32)
    low = total - top - mid
    row = lax.broadcasted_iota(jnp.int32, (STATE, cols), 0)
    rows = jnp.where(row == 0, top, jnp.where(row == 1, mid, jnp.where(row == 2, low, 0.0)))
    share = sent_ref.shape[2]
    for k in range(sent_ref.shape[0]):
        at = slice(k * share, (k + 1) * share)
        sent_ref[k, :STATE, :] = end[:, at].astype(sent_ref.dtype)
        sent_ref[k, STATE:, :] = rows[:, at].astype(sent_ref.dtype)


def correct_body(
    core_ref, delta_ref, y_ref, enter_ref, param_ref, read_ref, own_gate_ref, other_gate_ref,
    mine_ref, theirs_ref, hist_scr, out_scr, rate_scr, enter_scr,
):
    core = core_ref[0]
    enter_scr[...] = jnp.concatenate([enter_ref[k] for k in range(enter_ref.shape[0])], axis=1)
    tokens, cols = y_ref.shape
    half = tokens // 2
    rate_scr[...] = -LOG2E * jnp.exp(param_ref[0, :STATE, :])

    tiles = lane_tiles(cols)

    def step16(group, elapsed):
        base = pl.multiple_of(group * GROUP, GROUP)
        elapsed = list(elapsed)
        for i in range(GROUP):
            carried = []
            for k, tile in enumerate(tiles):
                elapsed[k] = elapsed[k] + spread(delta_ref, k, base + i, 8)
                twice = jnp.concatenate([elapsed[k], elapsed[k]], axis=0)
                carried.append(jnp.exp2(twice * rate_scr[:, tile]))
            carried = jnp.concatenate(carried, axis=1).astype(jnp.bfloat16)
            hist_scr[i * STATE : (i + 1) * STATE, :] = carried * enter_scr[...]
        read = read_ref[pl.ds(base, GROUP), :]
        out = jnp.dot(read, hist_scr[...], preferred_element_type=jnp.float32)
        total = out + y_ref[pl.ds(base, GROUP), :].astype(jnp.float32)
        out_scr[pl.ds(base, GROUP), :] = total.astype(jnp.bfloat16).astype(jnp.float32)
        return tuple(elapsed)

    zero = jnp.zeros((8, tiles[0].stop), jnp.float32)
    lax.fori_loop(0, tokens // GROUP, step16, (zero,) * len(tiles))
    rows = 16

    def gated(gate_ref, dest_ref, offset):
        def body(step, carry):
            first = pl.multiple_of(step * rows, rows)
            gate = gate_ref[pl.ds(first, rows), :].astype(jnp.float32)
            value = out_scr[pl.ds(pl.multiple_of(offset + first, 8), rows), :]
            dest_ref[pl.ds(first, rows), :] = (value * silu(gate)).astype(dest_ref.dtype)
            return carry

        lax.fori_loop(0, half // rows, body, 0)

    gated(own_gate_ref, mine_ref, core * half)
    gated(other_gate_ref, theirs_ref, (1 - core) * half)


def correct_kernel(core_ref, *refs, resumed):
    correct_body(core_ref, *(refs[1:] if resumed else refs))


def combine_kernel(order_ref, got_ref, rate_ref, enter_ref):
    chunks = got_ref.shape[0]
    rates = rate_ref[...]

    def body(place, state):
        chunk = order_ref[place]
        enter_ref[chunk] = state.astype(enter_ref.dtype)
        got = got_ref[chunk].astype(jnp.float32)
        total = got[STATE : STATE + 1] + got[STATE + 1 : STATE + 2] + got[STATE + 2 : STATE + 3]
        return jnp.exp2(total * rates) * state + got[:STATE]

    lax.fori_loop(0, chunks, body, jnp.zeros(rates.shape, jnp.float32))


def copy_kernel(core_ref, in_ref, out_ref):
    out_ref[...] = in_ref[...]


def place_kernel(core_ref, buffer_ref, in_ref, out_ref):
    out_ref[...] = in_ref[...]


def flash_kernel(
    side_ref, flip_ref, half_ref, diag_ref, first_ref, last_ref, q_ref, *refs, heads, rows, sources,
):
    kv_refs = refs[:sources]
    out_ref, query_scr, key_scr, value_scr, max_scr, acc_scr = refs[sources:]
    step = pl.program_id(0)
    scale = LOG2E * HD ** (-0.5)
    wide = 2 * HD
    span = q_ref.shape[0]

    for source in range(sources):

        @pl.when(flip_ref[step] == source)
        def _(kv_ref=kv_refs[source]):
            key_scr[:, :HD] = kv_ref[:, :HD]
            key_scr[:, HD:] = kv_ref[:, :HD]
            value_scr[:HD, :] = kv_ref[:, HD:].T

    value_scr[HD:, :] = jnp.ones((ONES, span), jnp.bfloat16)

    @pl.when(first_ref[step] == 1)
    def _():
        max_scr[...] = jnp.full(max_scr.shape, NEG_LARGE, jnp.float32)
        acc_scr[...] = jnp.zeros(acc_scr.shape, jnp.float32)
        for head in range(heads):
            scaled = q_ref[:, head * HD : (head + 1) * HD].astype(jnp.float32) * scale
            coarse = scaled.astype(jnp.bfloat16)
            query_scr[:, head * wide : head * wide + HD] = coarse
            query_scr[:, head * wide + HD : (head + 1) * wide] = (
                scaled - coarse.astype(jnp.float32)
            ).astype(jnp.bfloat16)

    def score(head, row, key_count, masked):
        q = query_scr[row : row + rows, head * wide : (head + 1) * wide]
        scores = lax.dot_general(
            key_scr[:key_count, :], q, (((1,), (1,)), ((), ())),
            preferred_element_type=jnp.float32,
        )
        if masked:
            last = scores[row:, :]
            key_at = lax.broadcasted_iota(jnp.int32, last.shape, 0)
            query_at = lax.broadcasted_iota(jnp.int32, last.shape, 1)
            last = jnp.where(key_at <= query_at, last, NEG_LARGE)
            scores = jnp.concatenate([scores[:row, :], last], axis=0) if row else last
        return scores

    def absorb(head, row, key_count, scores):
        at = slice(row, row + rows)
        old_max = max_scr[head, 0:1, at]
        new_max = jnp.maximum(old_max, jnp.max(scores, axis=0, keepdims=True))
        weights = jnp.exp2(scores - new_max).astype(jnp.bfloat16)
        shrink = jnp.exp2(old_max - new_max)
        acc_scr[head, :, at] = acc_scr[head, :, at] * shrink + jnp.dot(
            value_scr[:, :key_count], weights, preferred_element_type=jnp.float32
        )
        max_scr[head, :, at] = jnp.broadcast_to(new_max, (8, rows))

    def sweep(masked):
        work = [(head, row) for head in range(heads) for row in range(0, span, rows)]
        count = [row + rows if masked else span for _, row in work]
        ahead = score(*work[0], count[0], masked)
        for i, (head, row) in enumerate(work):
            scores = ahead
            if i + 1 < len(work):
                ahead = score(*work[i + 1], count[i + 1], masked)
            absorb(head, row, count[i], scores)

    @pl.when(diag_ref[step] == 0)
    def _():
        sweep(False)

    @pl.when(diag_ref[step] == 1)
    def _():
        sweep(True)

    @pl.when(last_ref[step] == 1)
    def _():
        for head in range(heads):
            for row in range(0, span, rows):
                at = slice(row, row + rows)
                ratio = acc_scr[head, :HD, at] / acc_scr[head, HD : HD + 1, at]
                out_ref[at, head * HD : (head + 1) * HD] = ratio.T.astype(out_ref.dtype)


def whole(shape):
    return pl.BlockSpec(
        shape, lambda j, core_ref: (0,) * len(shape), pipeline_mode=pl.Buffered(1)
    )


def shard_map_of(side, piece, first=0):
    return lambda j, core_ref: (
        0, (PAIR * (j + first) + (core_ref[0] + side) % PAIR) * PIECES + piece,
    )


def param_spec(count, width, piece, first):
    return pl.BlockSpec(
        (1, PARAM_ROWS, width),
        lambda j, core_ref: (lax.rem(core_ref[1] + count - (j + first), count), 0, piece),
    )


def plain(j, core_ref):
    return (0, j)


def run_pick(core, full, piece, width):
    half, inner = full.shape
    blocks = inner // (width * PIECES * PAIR)
    return pl.pallas_call(
        copy_kernel,
        grid_spec=pltpu.PrefetchScalarGridSpec(
            num_scalar_prefetch=1,
            grid=(blocks,),
            in_specs=[pl.BlockSpec((half, width), shard_map_of(1, piece))],
            out_specs=pl.BlockSpec((half, width), plain),
        ),
        out_shape=jax.ShapeDtypeStruct((half, blocks * width), full.dtype),
        name="pick_channels",
    )(core, full)


def run_place(core, full, part, piece, width, first):
    half, _ = full.shape
    blocks = part.shape[1] // width
    return pl.pallas_call(
        place_kernel,
        grid_spec=pltpu.PrefetchScalarGridSpec(
            num_scalar_prefetch=1,
            grid=(blocks,),
            in_specs=[pl.BlockSpec(memory_space=pl.ANY), pl.BlockSpec((half, width), plain)],
            out_specs=pl.BlockSpec((half, width), shard_map_of(1, piece, first)),
        ),
        out_shape=jax.ShapeDtypeStruct(full.shape, full.dtype),
        input_output_aliases={1: 0},
        name="place_channels",
    )(core, full, part)


def weight_spec(weight, width, shards, first):
    if weight.ndim == 4:
        parts, _, rows, _ = weight.shape
        return pl.BlockSpec((parts, 1, rows, width), lambda j, core_ref: (0, j + first, 0, 0))
    return pl.BlockSpec(
        (1, weight.shape[1], width),
        lambda j, core_ref: (lax.rem(core_ref[1] + shards - (j + first), shards), 0, 0),
    )


def run_scan(
    core, x_own, x_other, halo, low_own, low_other, weights, params, inject, read, piece, width, share,
    first, blocks,
):
    half = x_other.shape[0]
    cols = blocks * width
    tokens = 2 * half
    shards = params.shape[0]
    sources = len(weights)

    def shifted(j, core_ref):
        return (0, j + first)

    lanes = min(LANES, width)
    tiles = width // lanes
    return pl.pallas_call(
        functools.partial(scan_kernel, sources=sources),
        grid_spec=pltpu.PrefetchScalarGridSpec(
            num_scalar_prefetch=1,
            grid=(blocks,),
            in_specs=[
                pl.BlockSpec((half, width), shard_map_of(0, piece, first)),
                pl.BlockSpec((half, width), shifted),
                pl.BlockSpec((8, width), lambda j, core_ref: (0, piece * shards + j + first)),
                whole(low_own.shape),
                whole(low_other.shape),
                param_spec(shards, width, piece, first),
                whole(inject.shape),
                whole(read.shape),
            ]
            + [weight_spec(weight, width, shards, first) for weight in weights],
            out_specs=[
                pl.BlockSpec((tiles, tokens, lanes), lambda j, core_ref: (j, 0, 0)),
                pl.BlockSpec((tokens, width), plain),
                pl.BlockSpec((width // share, 2 * STATE, share), lambda j, core_ref: (j, 0, 0)),
            ],
            scratch_shapes=[
                pltpu.VMEM((tiles, tokens + 8, lanes), jnp.float32),
                pltpu.VMEM((tokens, width), jnp.float32),
                pltpu.VMEM((tiles, tokens, lanes), jnp.float32),
                pltpu.VMEM((GROUP * STATE, width), jnp.bfloat16),
                pltpu.VMEM((STATE, width), jnp.float32),
                pltpu.VMEM((8 * (CONV + 3), width), jnp.float32),
            ],
        ),
        out_shape=[
            jax.ShapeDtypeStruct((cols // lanes, tokens, lanes), jnp.float32),
            jax.ShapeDtypeStruct((tokens, cols), jnp.bfloat16),
            jax.ShapeDtypeStruct((cols // share, 2 * STATE, share), jnp.bfloat16),
        ],
        compiler_params=pltpu.CompilerParams(vmem_limit_bytes=VMEM_LIMIT),
        name="token_scan",
    )(core, x_own, x_other, halo, low_own, low_other, params, inject, read, *weights)


def run_correct(
    core, full, delta, y, enter, params, read, gate_own, gate_other, piece, width, first, inside, blocks
):
    tokens = y.shape[0]
    half, inner = gate_own.shape
    cols = blocks * width
    lanes = delta.shape[2]
    tiles = width // lanes
    share = enter.shape[2]
    resumed = full is not None
    first_spec = [pl.BlockSpec(memory_space=pl.ANY)] if resumed else []
    first_arg = (full,) if resumed else ()
    return pl.pallas_call(
        functools.partial(correct_kernel, resumed=resumed),
        grid_spec=pltpu.PrefetchScalarGridSpec(
            num_scalar_prefetch=1,
            grid=(blocks,),
            in_specs=first_spec
            + [
                pl.BlockSpec((tiles, tokens, lanes), lambda j, core_ref: (j + inside, 0, 0)),
                pl.BlockSpec((tokens, width), lambda j, core_ref: (0, j + inside)),
                pl.BlockSpec((width // share, STATE, share), lambda j, core_ref: (j + first, 0, 0)),
                param_spec(params.shape[0], width, piece, first),
                whole(read.shape),
                pl.BlockSpec((half, width), shard_map_of(0, piece, first)),
                pl.BlockSpec((half, width), lambda j, core_ref: (0, j + first)),
            ],
            out_specs=[
                pl.BlockSpec((half, width), shard_map_of(0, piece, first)),
                pl.BlockSpec((half, width), plain),
            ],
            scratch_shapes=[
                pltpu.VMEM((GROUP * STATE, width), jnp.bfloat16),
                pltpu.VMEM((tokens, width), jnp.float32),
                pltpu.VMEM((STATE, width), jnp.float32),
                pltpu.VMEM((STATE, width), jnp.bfloat16),
            ],
        ),
        out_shape=[
            jax.ShapeDtypeStruct((half, inner), jnp.bfloat16),
            jax.ShapeDtypeStruct((half, cols), jnp.bfloat16),
        ],
        input_output_aliases={1: 0} if resumed else {},
        compiler_params=pltpu.CompilerParams(vmem_limit_bytes=VMEM_LIMIT),
        name="state_correction",
    )(core, *first_arg, delta, y, enter, params, read, gate_own, gate_other)


def run_combine(order, got, rates):
    chunks, _, cols = got.shape
    return pl.pallas_call(
        combine_kernel,
        grid_spec=pltpu.PrefetchScalarGridSpec(
            num_scalar_prefetch=1,
            grid=(1,),
            in_specs=[
                pl.BlockSpec(got.shape, lambda i, o: (0, 0, 0)),
                pl.BlockSpec(rates.shape, lambda i, o: (0, 0)),
            ],
            out_specs=pl.BlockSpec((chunks, STATE, cols), lambda i, o: (0, 0, 0)),
        ),
        out_shape=jax.ShapeDtypeStruct((chunks, STATE, cols), jnp.bfloat16),
        compiler_params=pltpu.CompilerParams(vmem_limit_bytes=VMEM_LIMIT),
        name="state_combine",
    )(order, got, rates)


def run_flash(tables, q, kv_parts, rows=512):
    _, width = q.shape
    heads = width // HD
    steps = tables[0].shape[0]
    sources = len(kv_parts)

    def q_map(s, side, flip, half, diag, first, last):
        return (side[s], 0)

    def kv_map(s, side, flip, half, diag, first, last):
        return (half[s], 0)

    return pl.pallas_call(
        functools.partial(flash_kernel, heads=heads, rows=rows, sources=sources),
        grid_spec=pltpu.PrefetchScalarGridSpec(
            num_scalar_prefetch=6,
            grid=(steps,),
            in_specs=[pl.BlockSpec((SPAN, width), q_map)]
            + [pl.BlockSpec((SPAN, 2 * HD), kv_map)] * sources,
            out_specs=pl.BlockSpec((SPAN, width), q_map),
            scratch_shapes=[
                pltpu.VMEM((SPAN, 2 * width), jnp.bfloat16),
                pltpu.VMEM((SPAN, 2 * HD), jnp.bfloat16),
                pltpu.VMEM((HD + ONES, SPAN), jnp.bfloat16),
                pltpu.VMEM((heads, 8, SPAN), jnp.float32),
                pltpu.VMEM((heads, HD + ONES, SPAN), jnp.float32),
            ],
        ),
        out_shape=jax.ShapeDtypeStruct(q.shape, jnp.bfloat16),
        compiler_params=pltpu.CompilerParams(vmem_limit_bytes=VMEM_LIMIT),
        name="causal_attention",
    )(*tables, q, *kv_parts)


def flash_tables(span_order, my_blocks, blk):
    block_total = span_order.shape[0]
    places = jnp.arange(block_total, dtype=jnp.int32)
    holder = jnp.sum(jnp.where(span_order[None, :] == places[:, None], places[None, :], 0), axis=1)
    steps = jnp.arange(block_total + 1, dtype=jnp.int32)
    first_count = my_blocks[0] + 1
    side = (steps >= first_count).astype(jnp.int32)
    place = jnp.where(side == 1, steps - first_count, steps)
    limit = jnp.where(side == 1, my_blocks[1], my_blocks[0])
    block = jnp.sum(jnp.where(places[None, :] == place[:, None], holder[None, :], 0), axis=1)
    block = block.astype(jnp.int32)
    last = (place == limit).astype(jnp.int32)
    first = (place == 0).astype(jnp.int32)
    return (side, (block // 2) ^ blk.astype(jnp.int32), block % 2, last, first, last)


def local(
    mamba_input, gate_input, delta_low, state_mixers, conv_weight, conv_bias, delta_weight,
    delta_bias, decay_log, skip_gain, queries, key_rows, value_rows, span_order,
):
    blk = lax.axis_index("blk")
    chip = lax.axis_index("chip")
    core = lax.axis_index("core")
    blk_count = lax.axis_size("blk")
    chip_count = lax.axis_size("chip")
    ulys = ("chip", "core")
    chips = ("blk", "chip")
    ulys_count = chip_count * PAIR
    chunks = blk_count * chip_count
    block_total = span_order.shape[0]
    half, _ = mamba_input.shape
    tokens = PAIR * half
    shard_cols = delta_weight.shape[1]
    width = shard_cols // PIECES
    cols = chip_count * width
    swap = [(0, 1), (1, 0)]
    core_arr = jnp.stack([core, chip]).astype(jnp.int32)
    my_blocks = lax.dynamic_slice_in_dim(span_order, 2 * blk, 2, 0)

    depth = delta_weight.shape[0]
    part_rows = depth // blk_count
    part = lax.dynamic_slice_in_dim(delta_weight, blk * part_rows, part_rows, 0)
    far_moves = [
        [(i, (i + far) % chip_count) for i in range(chip_count)] for far in range(1, chip_count)
    ]
    flips = [[(i, i ^ flip) for i in range(blk_count)] for flip in range(1, blk_count)]
    part_first, part_later = part[:, :width], part[:, width:]
    shards_first = jnp.stack(
        [part_first] + [lax.ppermute(part_first, "chip", move) for move in far_moves]
    )
    weights_later = lax.all_gather(part_later, chips, axis=0, tiled=False)
    weights_later = [weights_later.reshape(blk_count, chip_count, part_rows, width)]

    def by_flip(low):
        return jnp.concatenate(
            [
                lax.dynamic_slice_in_dim(low, (blk ^ flip) * part_rows, part_rows, 1)
                for flip in range(blk_count)
            ],
            axis=1,
        )

    per_block = SPAN // tokens
    chunk_ids = jnp.arange(chunks, dtype=jnp.int32)
    stored = chunk_ids // per_block
    block_ids = jnp.arange(block_total, dtype=jnp.int32)
    block_pos = jnp.sum(
        jnp.where(stored[:, None] == block_ids[None, :], span_order[None, :], 0), axis=1
    )
    chunk_pos = block_pos * per_block + chunk_ids % per_block
    order = jnp.sum(
        jnp.where(chunk_pos[None, :] == chunk_ids[:, None], chunk_ids[None, :], 0), axis=1
    ).astype(jnp.int32)
    me = blk * chip_count + chip
    my_pos = jnp.sum(jnp.where(chunk_ids == me, chunk_pos, 0))
    last_rows = mamba_input[half - (CONV - 1) :].reshape(
        CONV - 1, chip_count, PAIR, PIECES, width
    )

    def columns_of(side):
        mine = lax.dynamic_index_in_dim(last_rows, side, 2, False)
        return mine.swapaxes(1, 2).reshape(CONV - 1, PIECES * cols)

    tail = jnp.where(
        core == 1, columns_of(core), lax.ppermute(columns_of(1 - core), "core", swap)
    )
    tails = lax.all_to_all(
        jnp.broadcast_to(tail[None], (chunks, CONV - 1, PIECES * cols)), chips,
        split_axis=0, concat_axis=0, tiled=True,
    )
    before = (chunk_pos == my_pos - 1).astype(jnp.bfloat16)
    halo = jnp.einsum("m,mkc->kc", before, tails, preferred_element_type=jnp.float32)
    halo = jnp.concatenate(
        [jnp.zeros((8 - (CONV - 1), PIECES * cols), jnp.bfloat16), halo.astype(jnp.bfloat16)],
        axis=0,
    )

    kv_heads = key_rows.shape[1] // HD
    repeat = ulys_count // kv_heads
    kv_rows = jnp.stack(
        [key_rows.reshape(half, kv_heads, HD), value_rows.reshape(half, kv_heads, HD)], axis=2
    )
    kv_rows = jnp.broadcast_to(
        kv_rows[:, :, None], (half, kv_heads, repeat, 2, HD)
    ).reshape(half, ulys_count * 2 * HD)
    kv_rows, shards_first, halo = lax.optimization_barrier((kv_rows, shards_first, halo))
    weights_first = [shards_first] + [
        lax.ppermute(shards_first, "blk", move) for move in flips
    ]
    kv_local = lax.all_to_all(kv_rows, ulys, split_axis=1, concat_axis=0, tiled=True)

    packed = jnp.concatenate(
        [
            decay_log,
            conv_weight.astype(jnp.float32),
            conv_bias[None],
            delta_bias[None],
            skip_gain[None],
            jnp.zeros((1, shard_cols), jnp.float32),
        ],
        axis=0,
    )
    x_other = [
        lax.ppermute(run_pick(core_arr, mamba_input, piece, width), "core", swap)
        for piece in range(PIECES)
    ]
    low_other = lax.ppermute(delta_low, "core", swap)
    mixers_other = lax.ppermute(state_mixers, "core", swap)
    mixers = jnp.where(
        core == 0,
        jnp.concatenate([state_mixers, mixers_other], axis=0),
        jnp.concatenate([mixers_other, state_mixers], axis=0),
    )
    inject = jnp.broadcast_to(
        mixers[:, :STATE].astype(jnp.float32).reshape(tokens * STATE, 1), (tokens * STATE, LANES)
    )
    same = jnp.arange(tokens, dtype=jnp.int32)[:, None] % GROUP == jnp.arange(GROUP, dtype=jnp.int32)
    read = jnp.where(
        same[:, :, None], mixers[:, None, STATE:], jnp.zeros((), jnp.bfloat16)
    ).reshape(tokens, GROUP * STATE)

    gate_other = [
        lax.ppermute(run_pick(core_arr, gate_input, piece, width), "core", swap)
        for piece in range(PIECES)
    ]

    params = jnp.stack([packed] + [lax.ppermute(packed, "chip", move) for move in far_moves])

    share = cols // chunks
    split = chip_count // 2

    def scan_part(piece, x_piece, lows, weights, first, blocks):
        return run_scan(
            core_arr, mamba_input, x_piece, halo, *lows, weights, params, inject, read, piece,
            width, share, first, blocks,
        )

    def rates_of(piece):
        at = me * share
        shard = at // width
        far = (chip + chip_count - shard) % chip_count
        mine = lax.dynamic_slice(
            params, (far, 0, piece * width + at % width), (1, STATE, share)
        )
        return -LOG2E * jnp.exp(mine[0])

    my_rates = [rates_of(piece) for piece in range(PIECES)]

    def to_owners(array):
        return lax.all_to_all(array, chips, split_axis=0, concat_axis=0, tiled=True)

    def correct_part(full, made, enter, piece, first, inside, blocks):
        delta, y = made[:2]
        return run_correct(
            core_arr, full, delta, y, enter, params, read, gate_input, gate_other[piece], piece,
            width, first, inside, blocks,
        )

    lows_first = (by_flip(delta_low), by_flip(low_other))
    lows_later = (delta_low, low_other)
    tables = flash_tables(span_order, my_blocks, blk)
    (
        queries, kv_local, gate_other, inject, read, params, my_rates, tables, order, lows_first,
        x_other,
    ) = lax.optimization_barrier(
        (
            queries, kv_local, gate_other, inject, read, params, my_rates, tables, order,
            lows_first, x_other,
        )
    )
    q_local = lax.all_to_all(queries, ulys, split_axis=1, concat_axis=0, tiled=True)
    kv_parts = [kv_local] + [lax.ppermute(kv_local, "blk", move) for move in flips]
    made_0 = scan_part(0, x_other[0], lows_first, weights_first, 0, chip_count)
    x_now, sent_0, q_local, kv_parts, my_rates = lax.optimization_barrier(
        (x_other[1], made_0[2], q_local, kv_parts, my_rates)
    )
    got_0 = to_owners(sent_0)
    made_1a = scan_part(1, x_now, lows_later, weights_later, 0, split)
    x_now, got_0, sent_1a = lax.optimization_barrier((x_now, got_0, made_1a[2]))
    enter_0 = to_owners(run_combine(order, got_0, my_rates[0]))
    made_1b = scan_part(1, x_now, lows_later, weights_later, split, chip_count - split)
    enter_0, sent_1, q_local = lax.optimization_barrier(
        (enter_0, jnp.concatenate([sent_1a, made_1b[2]], axis=0), q_local)
    )
    got_1 = to_owners(sent_1)
    attended = run_flash(tables, q_local, kv_parts)
    enter_0, got_1, attended = lax.optimization_barrier((enter_0, got_1, attended))
    enter_1 = to_owners(run_combine(order, got_1, my_rates[1]))
    full, theirs_0 = correct_part(None, made_0, enter_0, 0, 0, 0, chip_count)
    full, enter_1, attended = lax.optimization_barrier((full, enter_1, attended))
    back_0 = lax.ppermute(theirs_0, "core", swap)
    attention_output = lax.all_to_all(attended, ulys, split_axis=0, concat_axis=1, tiled=True)
    full, theirs_1a = correct_part(full, made_1a, enter_1, 1, 0, 0, split)
    back_1a = lax.ppermute(theirs_1a, "core", swap)
    full, theirs_1b = correct_part(full, made_1b, enter_1, 1, split, 0, chip_count - split)
    back_1b = lax.ppermute(theirs_1b, "core", swap)
    full = run_place(core_arr, full, back_0, 0, width, 0)
    full = run_place(core_arr, full, back_1a, 1, width, 0)
    mamba_output = run_place(core_arr, full, back_1b, 1, width, split)
    return (mamba_output, attention_output)


def solution(mesh):
    blk_count = mesh.shape["blk"]
    ulys_count = mesh.shape["ulys"]
    fine = Mesh(
        mesh.devices.reshape(blk_count, ulys_count // PAIR, PAIR), ("blk", "chip", "core")
    )
    rows = P(("blk", "chip", "core"), None)
    col = ("chip", "core")
    placed = (
        rows, rows, rows, rows,
        P(None, col), P(col), P(None, col), P(col), P(None, col), P(col),
        rows, rows, rows,
        P(),
    )

    return jax.shard_map(local, mesh=fine, in_specs=placed, out_specs=(rows, rows), check_vma=False)
```

```python
import functools

import jax
import jax.numpy as jnp
from jax import lax
from jax.experimental import pallas as pl
from jax.experimental.pallas import tpu as pltpu
from jax.sharding import Mesh
from jax.sharding import PartitionSpec as P


STATE = 16
CONV = 4
HD = 128
SPAN = 1024
LANES = 128
PAIR = 2
GROUP = 16
PIECES = 2
ONES = 16
NEG_LARGE = -1e30
LOG2E = 1.4426950408889634
PARAM_ROWS = 24
VMEM_LIMIT = 56 * 1024 * 1024


def softplus(x):
    return jnp.maximum(x, 0.0) + jnp.log1p(jnp.exp(-jnp.abs(x)))


def silu(x):
    half = 0.5 * x
    return half * jnp.tanh(half) + half


def lane_tiles(cols):
    size = min(LANES, cols)
    return [slice(at, at + size) for at in range(0, cols, size)]


def spread(ref, k, row, count):
    return jnp.broadcast_to(ref[k, pl.ds(row, 1), :], (count, ref.shape[2]))


def scan_kernel(
    core_ref, own_ref, other_ref, halo_ref, low_own_ref, low_other_ref, param_ref, inject_ref,
    read_ref, *refs, sources,
):
    weight_refs = refs[:sources]
    delta_ref, y_ref, sent_ref = refs[sources : sources + 3]
    x_scr, driven_scr, push_scr, hist_scr, rate_scr, param_scr = refs[sources + 3 :]
    core = core_ref[0]
    tokens, cols = y_ref.shape
    half = tokens // 2
    depth = low_own_ref.shape[1]
    tiles = lane_tiles(cols)
    mine = pl.multiple_of(core * half, 8)
    theirs = pl.multiple_of((1 - core) * half, 8)
    weight = jnp.concatenate(
        [ref[...].reshape(depth // sources, cols) for ref in weight_refs], axis=0
    )
    raw_mine = jnp.dot(low_own_ref[...], weight, preferred_element_type=jnp.float32)
    for k, tile in enumerate(tiles):
        delta_ref[k, pl.ds(mine, half), :] = raw_mine[:, tile]
    raw_theirs = jnp.dot(low_other_ref[...], weight, preferred_element_type=jnp.float32)
    for k, tile in enumerate(tiles):
        delta_ref[k, pl.ds(theirs, half), :] = raw_theirs[:, tile]
    for k, tile in enumerate(tiles):
        x_scr[k, 0:8, :] = halo_ref[:, tile].astype(jnp.float32)
        x_scr[k, pl.ds(8 + mine, half), :] = own_ref[:, tile].astype(jnp.float32)
        x_scr[k, pl.ds(8 + theirs, half), :] = other_ref[:, tile].astype(jnp.float32)
    rate_scr[...] = -LOG2E * jnp.exp(param_ref[0, :STATE, :])
    for k in range(CONV + 3):
        param_scr[8 * k : 8 * k + 8, :] = jnp.broadcast_to(
            param_ref[0, STATE + k : STATE + k + 1, :], (8, cols)
        )

    def prepare(step, total):
        first = pl.multiple_of(step * 8, 8)
        total = list(total)
        for k, tile in enumerate(tiles):
            mixed = param_scr[8 * CONV : 8 * CONV + 8, tile]
            for j in range(CONV):
                shifted = x_scr[k, pl.ds(first + 8 - (CONV - 1) + j, 8), :]
                mixed = mixed + param_scr[8 * j : 8 * j + 8, tile] * shifted
            driven = silu(mixed)
            delta = softplus(
                delta_ref[k, pl.ds(first, 8), :] + param_scr[8 * CONV + 8 : 8 * CONV + 16, tile]
            )
            delta_ref[k, pl.ds(first, 8), :] = delta
            driven_scr[pl.ds(first, 8), tile] = driven * param_scr[8 * CONV + 16 : 8 * CONV + 24, tile]
            push_scr[k, pl.ds(first, 8), :] = driven * delta
            total[k] = total[k] + delta
        return tuple(total)

    zero = jnp.zeros((8, tiles[0].stop), jnp.float32)
    total = lax.fori_loop(0, tokens // 8, prepare, (zero,) * len(tiles))
    total = jnp.sum(jnp.concatenate(total, axis=1), axis=0, keepdims=True)

    def step16(group, hidden):
        base = pl.multiple_of(group * GROUP, GROUP)
        hidden = list(hidden)
        for i in range(GROUP):
            inject = inject_ref[pl.ds(pl.multiple_of((base + i) * STATE, STATE), STATE), :]
            for k, tile in enumerate(tiles):
                decay = jnp.exp2(spread(delta_ref, k, base + i, STATE) * rate_scr[:, tile])
                push = spread(push_scr, k, base + i, STATE)
                hidden[k] = decay * hidden[k] + push * inject
            hist_scr[i * STATE : (i + 1) * STATE, :] = jnp.concatenate(hidden, axis=1).astype(
                jnp.bfloat16
            )
        read = read_ref[pl.ds(base, GROUP), :]
        out = jnp.dot(read, hist_scr[...], preferred_element_type=jnp.float32)
        y_ref[pl.ds(base, GROUP), :] = (out + driven_scr[pl.ds(base, GROUP), :]).astype(y_ref.dtype)
        return tuple(hidden)

    zero = jnp.zeros((STATE, tiles[0].stop), jnp.float32)
    end = lax.fori_loop(0, tokens // GROUP, step16, (zero,) * len(tiles))
    end = jnp.concatenate(end, axis=1)
    top = total.astype(jnp.bfloat16).astype(jnp.float32)
    mid = (total - top).astype(jnp.bfloat16).astype(jnp.float32)
    low = total - top - mid
    row = lax.broadcasted_iota(jnp.int32, (STATE, cols), 0)
    rows = jnp.where(row == 0, top, jnp.where(row == 1, mid, jnp.where(row == 2, low, 0.0)))
    share = sent_ref.shape[2]
    for k in range(sent_ref.shape[0]):
        at = slice(k * share, (k + 1) * share)
        sent_ref[k, :STATE, :] = end[:, at].astype(sent_ref.dtype)
        sent_ref[k, STATE:, :] = rows[:, at].astype(sent_ref.dtype)


def correct_body(
    core_ref, delta_ref, y_ref, enter_ref, param_ref, read_ref, own_gate_ref, other_gate_ref,
    mine_ref, theirs_ref, hist_scr, out_scr, rate_scr, enter_scr,
):
    core = core_ref[0]
    enter_scr[...] = jnp.concatenate([enter_ref[k] for k in range(enter_ref.shape[0])], axis=1)
    tokens, cols = y_ref.shape
    half = tokens // 2
    rate_scr[...] = -LOG2E * jnp.exp(param_ref[0, :STATE, :])

    tiles = lane_tiles(cols)

    def step16(group, elapsed):
        base = pl.multiple_of(group * GROUP, GROUP)
        elapsed = list(elapsed)
        for i in range(GROUP):
            carried = []
            for k, tile in enumerate(tiles):
                elapsed[k] = elapsed[k] + spread(delta_ref, k, base + i, 8)
                twice = jnp.concatenate([elapsed[k], elapsed[k]], axis=0)
                carried.append(jnp.exp2(twice * rate_scr[:, tile]))
            carried = jnp.concatenate(carried, axis=1).astype(jnp.bfloat16)
            hist_scr[i * STATE : (i + 1) * STATE, :] = carried * enter_scr[...]
        read = read_ref[pl.ds(base, GROUP), :]
        out = jnp.dot(read, hist_scr[...], preferred_element_type=jnp.float32)
        total = out + y_ref[pl.ds(base, GROUP), :].astype(jnp.float32)
        out_scr[pl.ds(base, GROUP), :] = total.astype(jnp.bfloat16).astype(jnp.float32)
        return tuple(elapsed)

    zero = jnp.zeros((8, tiles[0].stop), jnp.float32)
    lax.fori_loop(0, tokens // GROUP, step16, (zero,) * len(tiles))
    rows = 32

    def gated(gate_ref, dest_ref, offset):
        def body(step, carry):
            first = pl.multiple_of(step * rows, rows)
            gate = gate_ref[pl.ds(first, rows), :].astype(jnp.float32)
            value = out_scr[pl.ds(pl.multiple_of(offset + first, 8), rows), :]
            dest_ref[pl.ds(first, rows), :] = (value * silu(gate)).astype(dest_ref.dtype)
            return carry

        lax.fori_loop(0, half // rows, body, 0)

    gated(own_gate_ref, mine_ref, core * half)
    gated(other_gate_ref, theirs_ref, (1 - core) * half)


def correct_kernel(core_ref, *refs, resumed):
    correct_body(core_ref, *(refs[1:] if resumed else refs))


def combine_kernel(order_ref, got_ref, rate_ref, enter_ref):
    chunks = got_ref.shape[0]
    rates = rate_ref[...]

    def body(place, state):
        chunk = order_ref[place]
        enter_ref[chunk] = state.astype(enter_ref.dtype)
        got = got_ref[chunk].astype(jnp.float32)
        total = got[STATE : STATE + 1] + got[STATE + 1 : STATE + 2] + got[STATE + 2 : STATE + 3]
        return jnp.exp2(total * rates) * state + got[:STATE]

    lax.fori_loop(0, chunks, body, jnp.zeros(rates.shape, jnp.float32))


def copy_kernel(core_ref, in_ref, out_ref):
    out_ref[...] = in_ref[...]


def place_kernel(core_ref, buffer_ref, in_ref, out_ref):
    out_ref[...] = in_ref[...]


def flash_kernel(
    side_ref, flip_ref, half_ref, diag_ref, first_ref, last_ref, q_ref, *refs, heads, rows, sources,
):
    kv_refs = refs[:sources]
    out_ref, query_scr, key_scr, value_scr, max_scr, acc_scr = refs[sources:]
    step = pl.program_id(0)
    scale = LOG2E * HD ** (-0.5)
    wide = 2 * HD
    span = q_ref.shape[0]

    for source in range(sources):

        @pl.when(flip_ref[step] == source)
        def _(kv_ref=kv_refs[source]):
            key_scr[:, :HD] = kv_ref[:, :HD]
            key_scr[:, HD:] = kv_ref[:, :HD]
            value_scr[:HD, :] = kv_ref[:, HD:].T

    value_scr[HD:, :] = jnp.ones((ONES, span), jnp.bfloat16)

    @pl.when(first_ref[step] == 1)
    def _():
        max_scr[...] = jnp.full(max_scr.shape, NEG_LARGE, jnp.float32)
        acc_scr[...] = jnp.zeros(acc_scr.shape, jnp.float32)
        for head in range(heads):
            scaled = q_ref[:, head * HD : (head + 1) * HD].astype(jnp.float32) * scale
            coarse = scaled.astype(jnp.bfloat16)
            query_scr[:, head * wide : head * wide + HD] = coarse
            query_scr[:, head * wide + HD : (head + 1) * wide] = (
                scaled - coarse.astype(jnp.float32)
            ).astype(jnp.bfloat16)

    def score(head, row, key_count, masked):
        q = query_scr[row : row + rows, head * wide : (head + 1) * wide]
        scores = lax.dot_general(
            key_scr[:key_count, :], q, (((1,), (1,)), ((), ())),
            preferred_element_type=jnp.float32,
        )
        if masked:
            last = scores[row:, :]
            key_at = lax.broadcasted_iota(jnp.int32, last.shape, 0)
            query_at = lax.broadcasted_iota(jnp.int32, last.shape, 1)
            last = jnp.where(key_at <= query_at, last, NEG_LARGE)
            scores = jnp.concatenate([scores[:row, :], last], axis=0) if row else last
        return scores

    def absorb(head, row, key_count, scores):
        at = slice(row, row + rows)
        old_max = max_scr[head, 0:1, at]
        new_max = jnp.maximum(old_max, jnp.max(scores, axis=0, keepdims=True))
        weights = jnp.exp2(scores - new_max).astype(jnp.bfloat16)
        shrink = jnp.exp2(old_max - new_max)
        acc_scr[head, :, at] = acc_scr[head, :, at] * shrink + jnp.dot(
            value_scr[:, :key_count], weights, preferred_element_type=jnp.float32
        )
        max_scr[head, :, at] = jnp.broadcast_to(new_max, (8, rows))

    def sweep(masked):
        work = [(head, row) for head in range(heads) for row in range(0, span, rows)]
        count = [row + rows if masked else span for _, row in work]
        ahead = score(*work[0], count[0], masked)
        for i, (head, row) in enumerate(work):
            scores = ahead
            if i + 1 < len(work):
                ahead = score(*work[i + 1], count[i + 1], masked)
            absorb(head, row, count[i], scores)

    @pl.when(diag_ref[step] == 0)
    def _():
        sweep(False)

    @pl.when(diag_ref[step] == 1)
    def _():
        sweep(True)

    @pl.when(last_ref[step] == 1)
    def _():
        for head in range(heads):
            for row in range(0, span, rows):
                at = slice(row, row + rows)
                ratio = acc_scr[head, :HD, at] / acc_scr[head, HD : HD + 1, at]
                out_ref[at, head * HD : (head + 1) * HD] = ratio.T.astype(out_ref.dtype)


def whole(shape):
    return pl.BlockSpec(
        shape, lambda j, core_ref: (0,) * len(shape), pipeline_mode=pl.Buffered(1)
    )


def shard_map_of(side, piece, first=0):
    return lambda j, core_ref: (
        0, (PAIR * (j + first) + (core_ref[0] + side) % PAIR) * PIECES + piece,
    )


def param_spec(count, width, piece, first):
    return pl.BlockSpec(
        (1, PARAM_ROWS, width),
        lambda j, core_ref: (lax.rem(core_ref[1] + count - (j + first), count), 0, piece),
    )


def plain(j, core_ref):
    return (0, j)


def run_pick(core, full, piece, width):
    half, inner = full.shape
    blocks = inner // (width * PIECES * PAIR)
    return pl.pallas_call(
        copy_kernel,
        grid_spec=pltpu.PrefetchScalarGridSpec(
            num_scalar_prefetch=1,
            grid=(blocks,),
            in_specs=[pl.BlockSpec((half, width), shard_map_of(1, piece))],
            out_specs=pl.BlockSpec((half, width), plain),
        ),
        out_shape=jax.ShapeDtypeStruct((half, blocks * width), full.dtype),
        name="pick_channels",
    )(core, full)


def run_place(core, full, part, piece, width, first):
    half, _ = full.shape
    blocks = part.shape[1] // width
    return pl.pallas_call(
        place_kernel,
        grid_spec=pltpu.PrefetchScalarGridSpec(
            num_scalar_prefetch=1,
            grid=(blocks,),
            in_specs=[pl.BlockSpec(memory_space=pl.ANY), pl.BlockSpec((half, width), plain)],
            out_specs=pl.BlockSpec((half, width), shard_map_of(1, piece, first)),
        ),
        out_shape=jax.ShapeDtypeStruct(full.shape, full.dtype),
        input_output_aliases={1: 0},
        name="place_channels",
    )(core, full, part)


def weight_spec(weight, width, shards, first):
    if weight.ndim == 4:
        parts, _, rows, _ = weight.shape
        return pl.BlockSpec((parts, 1, rows, width), lambda j, core_ref: (0, j + first, 0, 0))
    return pl.BlockSpec(
        (1, weight.shape[1], width),
        lambda j, core_ref: (lax.rem(core_ref[1] + shards - (j + first), shards), 0, 0),
    )


def run_scan(
    core, x_own, x_other, halo, low_own, low_other, weights, params, inject, read, piece, width, share,
    first, blocks,
):
    half = x_other.shape[0]
    cols = blocks * width
    tokens = 2 * half
    shards = params.shape[0]
    sources = len(weights)

    def shifted(j, core_ref):
        return (0, j + first)

    lanes = min(LANES, width)
    tiles = width // lanes
    return pl.pallas_call(
        functools.partial(scan_kernel, sources=sources),
        grid_spec=pltpu.PrefetchScalarGridSpec(
            num_scalar_prefetch=1,
            grid=(blocks,),
            in_specs=[
                pl.BlockSpec((half, width), shard_map_of(0, piece, first)),
                pl.BlockSpec((half, width), shifted),
                pl.BlockSpec((8, width), lambda j, core_ref: (0, piece * shards + j + first)),
                whole(low_own.shape),
                whole(low_other.shape),
                param_spec(shards, width, piece, first),
                whole(inject.shape),
                whole(read.shape),
            ]
            + [weight_spec(weight, width, shards, first) for weight in weights],
            out_specs=[
                pl.BlockSpec((tiles, tokens, lanes), lambda j, core_ref: (j, 0, 0)),
                pl.BlockSpec((tokens, width), plain),
                pl.BlockSpec((width // share, 2 * STATE, share), lambda j, core_ref: (j, 0, 0)),
            ],
            scratch_shapes=[
                pltpu.VMEM((tiles, tokens + 8, lanes), jnp.float32),
                pltpu.VMEM((tokens, width), jnp.float32),
                pltpu.VMEM((tiles, tokens, lanes), jnp.float32),
                pltpu.VMEM((GROUP * STATE, width), jnp.bfloat16),
                pltpu.VMEM((STATE, width), jnp.float32),
                pltpu.VMEM((8 * (CONV + 3), width), jnp.float32),
            ],
        ),
        out_shape=[
            jax.ShapeDtypeStruct((cols // lanes, tokens, lanes), jnp.float32),
            jax.ShapeDtypeStruct((tokens, cols), jnp.bfloat16),
            jax.ShapeDtypeStruct((cols // share, 2 * STATE, share), jnp.bfloat16),
        ],
        compiler_params=pltpu.CompilerParams(vmem_limit_bytes=VMEM_LIMIT),
        name="token_scan",
    )(core, x_own, x_other, halo, low_own, low_other, params, inject, read, *weights)


def run_correct(
    core, full, delta, y, enter, params, read, gate_own, gate_other, piece, width, first, inside, blocks
):
    tokens = y.shape[0]
    half, inner = gate_own.shape
    cols = blocks * width
    lanes = delta.shape[2]
    tiles = width // lanes
    share = enter.shape[2]
    resumed = full is not None
    first_spec = [pl.BlockSpec(memory_space=pl.ANY)] if resumed else []
    first_arg = (full,) if resumed else ()
    return pl.pallas_call(
        functools.partial(correct_kernel, resumed=resumed),
        grid_spec=pltpu.PrefetchScalarGridSpec(
            num_scalar_prefetch=1,
            grid=(blocks,),
            in_specs=first_spec
            + [
                pl.BlockSpec((tiles, tokens, lanes), lambda j, core_ref: (j + inside, 0, 0)),
                pl.BlockSpec((tokens, width), lambda j, core_ref: (0, j + inside)),
                pl.BlockSpec((width // share, STATE, share), lambda j, core_ref: (j + first, 0, 0)),
                param_spec(params.shape[0], width, piece, first),
                whole(read.shape),
                pl.BlockSpec((half, width), shard_map_of(0, piece, first)),
                pl.BlockSpec((half, width), lambda j, core_ref: (0, j + first)),
            ],
            out_specs=[
                pl.BlockSpec((half, width), shard_map_of(0, piece, first)),
                pl.BlockSpec((half, width), plain),
            ],
            scratch_shapes=[
                pltpu.VMEM((GROUP * STATE, width), jnp.bfloat16),
                pltpu.VMEM((tokens, width), jnp.float32),
                pltpu.VMEM((STATE, width), jnp.float32),
                pltpu.VMEM((STATE, width), jnp.bfloat16),
            ],
        ),
        out_shape=[
            jax.ShapeDtypeStruct((half, inner), jnp.bfloat16),
            jax.ShapeDtypeStruct((half, cols), jnp.bfloat16),
        ],
        input_output_aliases={1: 0} if resumed else {},
        compiler_params=pltpu.CompilerParams(vmem_limit_bytes=VMEM_LIMIT),
        name="state_correction",
    )(core, *first_arg, delta, y, enter, params, read, gate_own, gate_other)


def run_combine(order, got, rates):
    chunks, _, cols = got.shape
    return pl.pallas_call(
        combine_kernel,
        grid_spec=pltpu.PrefetchScalarGridSpec(
            num_scalar_prefetch=1,
            grid=(1,),
            in_specs=[
                pl.BlockSpec(got.shape, lambda i, o: (0, 0, 0)),
                pl.BlockSpec(rates.shape, lambda i, o: (0, 0)),
            ],
            out_specs=pl.BlockSpec((chunks, STATE, cols), lambda i, o: (0, 0, 0)),
        ),
        out_shape=jax.ShapeDtypeStruct((chunks, STATE, cols), jnp.bfloat16),
        compiler_params=pltpu.CompilerParams(vmem_limit_bytes=VMEM_LIMIT),
        name="state_combine",
    )(order, got, rates)


def run_flash(tables, q, kv_parts, rows=512):
    _, width = q.shape
    heads = width // HD
    steps = tables[0].shape[0]
    sources = len(kv_parts)

    def q_map(s, side, flip, half, diag, first, last):
        return (side[s], 0)

    def kv_map(s, side, flip, half, diag, first, last):
        return (half[s], 0)

    return pl.pallas_call(
        functools.partial(flash_kernel, heads=heads, rows=rows, sources=sources),
        grid_spec=pltpu.PrefetchScalarGridSpec(
            num_scalar_prefetch=6,
            grid=(steps,),
            in_specs=[pl.BlockSpec((SPAN, width), q_map)]
            + [pl.BlockSpec((SPAN, 2 * HD), kv_map)] * sources,
            out_specs=pl.BlockSpec((SPAN, width), q_map),
            scratch_shapes=[
                pltpu.VMEM((SPAN, 2 * width), jnp.bfloat16),
                pltpu.VMEM((SPAN, 2 * HD), jnp.bfloat16),
                pltpu.VMEM((HD + ONES, SPAN), jnp.bfloat16),
                pltpu.VMEM((heads, 8, SPAN), jnp.float32),
                pltpu.VMEM((heads, HD + ONES, SPAN), jnp.float32),
            ],
        ),
        out_shape=jax.ShapeDtypeStruct(q.shape, jnp.bfloat16),
        compiler_params=pltpu.CompilerParams(vmem_limit_bytes=VMEM_LIMIT),
        name="causal_attention",
    )(*tables, q, *kv_parts)


def flash_tables(span_order, my_blocks, blk):
    block_total = span_order.shape[0]
    places = jnp.arange(block_total, dtype=jnp.int32)
    holder = jnp.sum(jnp.where(span_order[None, :] == places[:, None], places[None, :], 0), axis=1)
    steps = jnp.arange(block_total + 1, dtype=jnp.int32)
    first_count = my_blocks[0] + 1
    side = (steps >= first_count).astype(jnp.int32)
    place = jnp.where(side == 1, steps - first_count, steps)
    limit = jnp.where(side == 1, my_blocks[1], my_blocks[0])
    block = jnp.sum(jnp.where(places[None, :] == place[:, None], holder[None, :], 0), axis=1)
    block = block.astype(jnp.int32)
    last = (place == limit).astype(jnp.int32)
    first = (place == 0).astype(jnp.int32)
    return (side, (block // 2) ^ blk.astype(jnp.int32), block % 2, last, first, last)


def local(
    mamba_input, gate_input, delta_low, state_mixers, conv_weight, conv_bias, delta_weight,
    delta_bias, decay_log, skip_gain, queries, key_rows, value_rows, span_order,
):
    blk = lax.axis_index("blk")
    chip = lax.axis_index("chip")
    core = lax.axis_index("core")
    blk_count = lax.axis_size("blk")
    chip_count = lax.axis_size("chip")
    ulys = ("chip", "core")
    chips = ("blk", "chip")
    ulys_count = chip_count * PAIR
    chunks = blk_count * chip_count
    block_total = span_order.shape[0]
    half, _ = mamba_input.shape
    tokens = PAIR * half
    shard_cols = delta_weight.shape[1]
    width = shard_cols // PIECES
    cols = chip_count * width
    swap = [(0, 1), (1, 0)]
    core_arr = jnp.stack([core, chip]).astype(jnp.int32)
    my_blocks = lax.dynamic_slice_in_dim(span_order, 2 * blk, 2, 0)

    depth = delta_weight.shape[0]
    part_rows = depth // blk_count
    part = lax.dynamic_slice_in_dim(delta_weight, blk * part_rows, part_rows, 0)
    far_moves = [
        [(i, (i + far) % chip_count) for i in range(chip_count)] for far in range(1, chip_count)
    ]
    flips = [[(i, i ^ flip) for i in range(blk_count)] for flip in range(1, blk_count)]
    part_first, part_later = part[:, :width], part[:, width:]
    shards_first = jnp.stack(
        [part_first] + [lax.ppermute(part_first, "chip", move) for move in far_moves]
    )

    def by_flip(low):
        return jnp.concatenate(
            [
                lax.dynamic_slice_in_dim(low, (blk ^ flip) * part_rows, part_rows, 1)
                for flip in range(blk_count)
            ],
            axis=1,
        )

    per_block = SPAN // tokens
    chunk_ids = jnp.arange(chunks, dtype=jnp.int32)
    stored = chunk_ids // per_block
    block_ids = jnp.arange(block_total, dtype=jnp.int32)
    block_pos = jnp.sum(
        jnp.where(stored[:, None] == block_ids[None, :], span_order[None, :], 0), axis=1
    )
    chunk_pos = block_pos * per_block + chunk_ids % per_block
    order = jnp.sum(
        jnp.where(chunk_pos[None, :] == chunk_ids[:, None], chunk_ids[None, :], 0), axis=1
    ).astype(jnp.int32)
    me = blk * chip_count + chip
    my_pos = jnp.sum(jnp.where(chunk_ids == me, chunk_pos, 0))
    last_rows = mamba_input[half - (CONV - 1) :].reshape(
        CONV - 1, chip_count, PAIR, PIECES, width
    )

    def columns_of(side):
        mine = lax.dynamic_index_in_dim(last_rows, side, 2, False)
        return mine.swapaxes(1, 2).reshape(CONV - 1, PIECES * cols)

    tail = jnp.where(
        core == 1, columns_of(core), lax.ppermute(columns_of(1 - core), "core", swap)
    )
    tails = lax.all_to_all(
        jnp.broadcast_to(tail[None], (chunks, CONV - 1, PIECES * cols)), chips,
        split_axis=0, concat_axis=0, tiled=True,
    )
    before = (chunk_pos == my_pos - 1).astype(jnp.bfloat16)
    halo = jnp.einsum("m,mkc->kc", before, tails, preferred_element_type=jnp.float32)
    halo = jnp.concatenate(
        [jnp.zeros((8 - (CONV - 1), PIECES * cols), jnp.bfloat16), halo.astype(jnp.bfloat16)],
        axis=0,
    )

    kv_heads = key_rows.shape[1] // HD
    repeat = ulys_count // kv_heads
    kv_rows = jnp.stack(
        [key_rows.reshape(half, kv_heads, HD), value_rows.reshape(half, kv_heads, HD)], axis=2
    )
    kv_rows = jnp.broadcast_to(
        kv_rows[:, :, None], (half, kv_heads, repeat, 2, HD)
    ).reshape(half, ulys_count * 2 * HD)
    kv_rows, halo = lax.optimization_barrier((kv_rows, halo))
    shards_first, part_later = lax.optimization_barrier((shards_first, part_later))
    weights_later = lax.all_gather(part_later, chips, axis=0, tiled=False)
    weights_first = [shards_first] + [
        lax.ppermute(shards_first, "blk", move) for move in flips
    ]
    weights_later = [weights_later.reshape(blk_count, chip_count, part_rows, width)]
    kv_local = lax.all_to_all(kv_rows, ulys, split_axis=1, concat_axis=0, tiled=True)

    packed = jnp.concatenate(
        [
            decay_log,
            conv_weight.astype(jnp.float32),
            conv_bias[None],
            delta_bias[None],
            skip_gain[None],
            jnp.zeros((1, shard_cols), jnp.float32),
        ],
        axis=0,
    )

    def picked(full, piece):
        return run_pick(core_arr, full, piece, width)

    x_other = [
        lax.ppermute(picked(mamba_input, piece), "core", swap)
        for piece in range(PIECES)
    ]
    low_other = lax.ppermute(delta_low, "core", swap)
    mixers_other = lax.ppermute(state_mixers, "core", swap)
    mixers = jnp.where(
        core == 0,
        jnp.concatenate([state_mixers, mixers_other], axis=0),
        jnp.concatenate([mixers_other, state_mixers], axis=0),
    )
    inject = jnp.broadcast_to(
        mixers[:, :STATE].astype(jnp.float32).reshape(tokens * STATE, 1), (tokens * STATE, LANES)
    )
    same = jnp.arange(tokens, dtype=jnp.int32)[:, None] % GROUP == jnp.arange(GROUP, dtype=jnp.int32)
    read = jnp.where(
        same[:, :, None], mixers[:, None, STATE:], jnp.zeros((), jnp.bfloat16)
    ).reshape(tokens, GROUP * STATE)

    gate_other = [
        lax.ppermute(picked(gate_input, piece), "core", swap)
        for piece in range(PIECES)
    ]

    params = jnp.stack([packed] + [lax.ppermute(packed, "chip", move) for move in far_moves])

    share = cols // chunks
    split = chip_count // 2

    def scan_part(piece, x_piece, lows, weights, first, blocks):
        return run_scan(
            core_arr, mamba_input, x_piece, halo, *lows, weights, params, inject, read, piece,
            width, share, first, blocks,
        )

    def rates_of(piece):
        at = me * share
        shard = at // width
        far = (chip + chip_count - shard) % chip_count
        mine = lax.dynamic_slice(
            params, (far, 0, piece * width + at % width), (1, STATE, share)
        )
        return -LOG2E * jnp.exp(mine[0])

    my_rates = [rates_of(piece) for piece in range(PIECES)]

    def to_owners(array):
        return lax.all_to_all(array, chips, split_axis=0, concat_axis=0, tiled=True)

    def correct_part(full, made, enter, piece, first, inside, blocks):
        delta, y = made[:2]
        return run_correct(
            core_arr, full, delta, y, enter, params, read, gate_input, gate_other[piece], piece,
            width, first, inside, blocks,
        )

    lows_first = (by_flip(delta_low), by_flip(low_other))
    lows_later = (delta_low, low_other)
    tables = flash_tables(span_order, my_blocks, blk)
    (
        queries, kv_local, gate_other, inject, read, params, my_rates, tables, order, lows_first,
        x_other,
    ) = lax.optimization_barrier(
        (
            queries, kv_local, gate_other, inject, read, params, my_rates, tables, order,
            lows_first, x_other,
        )
    )
    q_local = lax.all_to_all(queries, ulys, split_axis=1, concat_axis=0, tiled=True)
    kv_parts = [kv_local] + [lax.ppermute(kv_local, "blk", move) for move in flips]
    made_0 = scan_part(0, x_other[0], lows_first, weights_first, 0, chip_count)
    x_now, sent_0, q_local, kv_parts, my_rates = lax.optimization_barrier(
        (x_other[1], made_0[2], q_local, kv_parts, my_rates)
    )
    got_0 = to_owners(sent_0)
    made_1a = scan_part(1, x_now, lows_later, weights_later, 0, split)
    x_now, got_0, sent_1a = lax.optimization_barrier((x_now, got_0, made_1a[2]))
    enter_0 = to_owners(run_combine(order, got_0, my_rates[0]))
    made_1b = scan_part(1, x_now, lows_later, weights_later, split, chip_count - split)
    enter_0, sent_1, q_local = lax.optimization_barrier(
        (enter_0, jnp.concatenate([sent_1a, made_1b[2]], axis=0), q_local)
    )
    got_1 = to_owners(sent_1)
    attended = run_flash(tables, q_local, kv_parts)
    enter_0, got_1, attended = lax.optimization_barrier((enter_0, got_1, attended))
    enter_1 = to_owners(run_combine(order, got_1, my_rates[1]))
    full, theirs_0 = correct_part(None, made_0, enter_0, 0, 0, 0, chip_count)
    full, enter_1, attended = lax.optimization_barrier((full, enter_1, attended))
    back_0 = lax.ppermute(theirs_0, "core", swap)
    attention_output = lax.all_to_all(attended, ulys, split_axis=0, concat_axis=1, tiled=True)
    full, theirs_1a = correct_part(full, made_1a, enter_1, 1, 0, 0, split)
    back_1a = lax.ppermute(theirs_1a, "core", swap)
    full, theirs_1b = correct_part(full, made_1b, enter_1, 1, split, 0, chip_count - split)
    back_1b = lax.ppermute(theirs_1b, "core", swap)
    full = run_place(core_arr, full, back_0, 0, width, 0)
    full = run_place(core_arr, full, back_1a, 1, width, 0)
    mamba_output = run_place(core_arr, full, back_1b, 1, width, split)
    return (mamba_output, attention_output)


def solution(mesh):
    blk_count = mesh.shape["blk"]
    ulys_count = mesh.shape["ulys"]
    fine = Mesh(
        mesh.devices.reshape(blk_count, ulys_count // PAIR, PAIR), ("blk", "chip", "core")
    )
    rows = P(("blk", "chip", "core"), None)
    col = ("chip", "core")
    placed = (
        rows, rows, rows, rows,
        P(None, col), P(col), P(None, col), P(col), P(None, col), P(col),
        rows, rows, rows,
        P(),
    )

    return jax.shard_map(local, mesh=fine, in_specs=placed, out_specs=(rows, rows), check_vma=False)
```

```python
import functools

import jax
import jax.numpy as jnp
from jax import lax
from jax.experimental import pallas as pl
from jax.experimental.pallas import tpu as pltpu
from jax.sharding import Mesh
from jax.sharding import PartitionSpec as P


STATE = 16
CONV = 4
HD = 128
SPAN = 1024
LANES = 128
PAIR = 2
GROUP = 16
PIECES = 2
ONES = 16
NEG_LARGE = -1e30
LOG2E = 1.4426950408889634
PARAM_ROWS = 24
VMEM_LIMIT = 56 * 1024 * 1024


def softplus(x):
    return jnp.maximum(x, 0.0) + jnp.log1p(jnp.exp(-jnp.abs(x)))


def silu(x):
    half = 0.5 * x
    return half * jnp.tanh(half) + half


def lane_tiles(cols):
    size = min(LANES, cols)
    return [slice(at, at + size) for at in range(0, cols, size)]


def spread(ref, k, row, count):
    return jnp.broadcast_to(ref[k, pl.ds(row, 1), :], (count, ref.shape[2]))


def scan_kernel(
    core_ref, own_ref, other_ref, halo_ref, low_own_ref, low_other_ref, param_ref, inject_ref,
    read_ref, *refs, sources,
):
    weight_refs = refs[:sources]
    delta_ref, y_ref, sent_ref = refs[sources : sources + 3]
    x_scr, driven_scr, push_scr, hist_scr, rate_scr, param_scr = refs[sources + 3 :]
    core = core_ref[0]
    tokens, cols = y_ref.shape
    half = tokens // 2
    depth = low_own_ref.shape[1]
    tiles = lane_tiles(cols)
    mine = pl.multiple_of(core * half, 8)
    theirs = pl.multiple_of((1 - core) * half, 8)
    weight = jnp.concatenate(
        [ref[...].reshape(depth // sources, cols) for ref in weight_refs], axis=0
    )
    raw_mine = jnp.dot(low_own_ref[...], weight, preferred_element_type=jnp.float32)
    for k, tile in enumerate(tiles):
        delta_ref[k, pl.ds(mine, half), :] = raw_mine[:, tile]
    raw_theirs = jnp.dot(low_other_ref[...], weight, preferred_element_type=jnp.float32)
    for k, tile in enumerate(tiles):
        delta_ref[k, pl.ds(theirs, half), :] = raw_theirs[:, tile]
    for k, tile in enumerate(tiles):
        x_scr[k, 0:8, :] = halo_ref[:, tile].astype(jnp.float32)
        x_scr[k, pl.ds(8 + mine, half), :] = own_ref[:, tile].astype(jnp.float32)
        x_scr[k, pl.ds(8 + theirs, half), :] = other_ref[:, tile].astype(jnp.float32)
    rate_scr[...] = -LOG2E * jnp.exp(param_ref[0, :STATE, :])
    for k in range(CONV + 3):
        param_scr[8 * k : 8 * k + 8, :] = jnp.broadcast_to(
            param_ref[0, STATE + k : STATE + k + 1, :], (8, cols)
        )

    def prepare(step, total):
        first = pl.multiple_of(step * 8, 8)
        total = list(total)
        for k, tile in enumerate(tiles):
            mixed = param_scr[8 * CONV : 8 * CONV + 8, tile]
            for j in range(CONV):
                shifted = x_scr[k, pl.ds(first + 8 - (CONV - 1) + j, 8), :]
                mixed = mixed + param_scr[8 * j : 8 * j + 8, tile] * shifted
            driven = silu(mixed)
            delta = softplus(
                delta_ref[k, pl.ds(first, 8), :] + param_scr[8 * CONV + 8 : 8 * CONV + 16, tile]
            )
            delta_ref[k, pl.ds(first, 8), :] = delta
            driven_scr[pl.ds(first, 8), tile] = driven * param_scr[8 * CONV + 16 : 8 * CONV + 24, tile]
            push_scr[k, pl.ds(first, 8), :] = driven * delta
            total[k] = total[k] + delta
        return tuple(total)

    zero = jnp.zeros((8, tiles[0].stop), jnp.float32)
    total = lax.fori_loop(0, tokens // 8, prepare, (zero,) * len(tiles))
    total = jnp.sum(jnp.concatenate(total, axis=1), axis=0, keepdims=True)

    def step16(group, hidden):
        base = pl.multiple_of(group * GROUP, GROUP)
        hidden = list(hidden)
        for i in range(GROUP):
            inject = inject_ref[pl.ds(pl.multiple_of((base + i) * STATE, STATE), STATE), :]
            for k, tile in enumerate(tiles):
                decay = jnp.exp2(spread(delta_ref, k, base + i, STATE) * rate_scr[:, tile])
                push = spread(push_scr, k, base + i, STATE)
                hidden[k] = decay * hidden[k] + push * inject
            hist_scr[i * STATE : (i + 1) * STATE, :] = jnp.concatenate(hidden, axis=1).astype(
                jnp.bfloat16
            )
        read = read_ref[pl.ds(base, GROUP), :]
        out = jnp.dot(read, hist_scr[...], preferred_element_type=jnp.float32)
        y_ref[pl.ds(base, GROUP), :] = (out + driven_scr[pl.ds(base, GROUP), :]).astype(y_ref.dtype)
        return tuple(hidden)

    zero = jnp.zeros((STATE, tiles[0].stop), jnp.float32)
    end = lax.fori_loop(0, tokens // GROUP, step16, (zero,) * len(tiles))
    end = jnp.concatenate(end, axis=1)
    top = total.astype(jnp.bfloat16).astype(jnp.float32)
    mid = (total - top).astype(jnp.bfloat16).astype(jnp.float32)
    low = total - top - mid
    row = lax.broadcasted_iota(jnp.int32, (STATE, cols), 0)
    rows = jnp.where(row == 0, top, jnp.where(row == 1, mid, jnp.where(row == 2, low, 0.0)))
    share = sent_ref.shape[2]
    for k in range(sent_ref.shape[0]):
        at = slice(k * share, (k + 1) * share)
        sent_ref[k, :STATE, :] = end[:, at].astype(sent_ref.dtype)
        sent_ref[k, STATE:, :] = rows[:, at].astype(sent_ref.dtype)


def correct_body(
    core_ref, delta_ref, y_ref, enter_ref, param_ref, read_ref, own_gate_ref, other_gate_ref,
    mine_ref, theirs_ref, hist_scr, out_scr, rate_scr, enter_scr,
):
    core = core_ref[0]
    enter_scr[...] = jnp.concatenate([enter_ref[k] for k in range(enter_ref.shape[0])], axis=1)
    tokens, cols = y_ref.shape
    half = tokens // 2
    rate_scr[...] = -LOG2E * jnp.exp(param_ref[0, :STATE, :])

    tiles = lane_tiles(cols)

    def step16(group, elapsed):
        base = pl.multiple_of(group * GROUP, GROUP)
        elapsed = list(elapsed)
        for i in range(GROUP):
            carried = []
            for k, tile in enumerate(tiles):
                elapsed[k] = elapsed[k] + spread(delta_ref, k, base + i, 8)
                twice = jnp.concatenate([elapsed[k], elapsed[k]], axis=0)
                carried.append(jnp.exp2(twice * rate_scr[:, tile]))
            carried = jnp.concatenate(carried, axis=1).astype(jnp.bfloat16)
            hist_scr[i * STATE : (i + 1) * STATE, :] = carried * enter_scr[...]
        read = read_ref[pl.ds(base, GROUP), :]
        out = jnp.dot(read, hist_scr[...], preferred_element_type=jnp.float32)
        total = out + y_ref[pl.ds(base, GROUP), :].astype(jnp.float32)
        out_scr[pl.ds(base, GROUP), :] = total.astype(jnp.bfloat16).astype(jnp.float32)
        return tuple(elapsed)

    zero = jnp.zeros((8, tiles[0].stop), jnp.float32)
    lax.fori_loop(0, tokens // GROUP, step16, (zero,) * len(tiles))
    rows = 32

    def gated(gate_ref, dest_ref, offset):
        def body(step, carry):
            first = pl.multiple_of(step * rows, rows)
            gate = gate_ref[pl.ds(first, rows), :].astype(jnp.float32)
            value = out_scr[pl.ds(pl.multiple_of(offset + first, 8), rows), :]
            dest_ref[pl.ds(first, rows), :] = (value * silu(gate)).astype(dest_ref.dtype)
            return carry

        lax.fori_loop(0, half // rows, body, 0)

    gated(own_gate_ref, mine_ref, core * half)
    gated(other_gate_ref, theirs_ref, (1 - core) * half)


def correct_kernel(core_ref, *refs, resumed):
    correct_body(core_ref, *(refs[1:] if resumed else refs))


def combine_kernel(order_ref, got_ref, rate_ref, enter_ref):
    chunks = got_ref.shape[0]
    rates = rate_ref[...]

    def body(place, state):
        chunk = order_ref[place]
        enter_ref[chunk] = state.astype(enter_ref.dtype)
        got = got_ref[chunk].astype(jnp.float32)
        total = got[STATE : STATE + 1] + got[STATE + 1 : STATE + 2] + got[STATE + 2 : STATE + 3]
        return jnp.exp2(total * rates) * state + got[:STATE]

    lax.fori_loop(0, chunks, body, jnp.zeros(rates.shape, jnp.float32))


def copy_kernel(core_ref, in_ref, out_ref):
    out_ref[...] = in_ref[...]


def place_kernel(core_ref, buffer_ref, in_ref, out_ref):
    out_ref[...] = in_ref[...]


def flash_kernel(
    side_ref, flip_ref, half_ref, diag_ref, first_ref, last_ref, q_ref, *refs, heads, rows, sources,
):
    kv_refs = refs[:sources]
    out_ref, query_scr, key_scr, value_scr, max_scr, acc_scr = refs[sources:]
    step = pl.program_id(0)
    scale = LOG2E * HD ** (-0.5)
    wide = 2 * HD
    span = q_ref.shape[0]

    for source in range(sources):

        @pl.when(flip_ref[step] == source)
        def _(kv_ref=kv_refs[source]):
            key_scr[:, :HD] = kv_ref[:, :HD]
            key_scr[:, HD:] = kv_ref[:, :HD]
            value_scr[:HD, :] = kv_ref[:, HD:].T

    value_scr[HD:, :] = jnp.ones((ONES, span), jnp.bfloat16)

    @pl.when(first_ref[step] == 1)
    def _():
        max_scr[...] = jnp.full(max_scr.shape, NEG_LARGE, jnp.float32)
        acc_scr[...] = jnp.zeros(acc_scr.shape, jnp.float32)
        for head in range(heads):
            scaled = q_ref[:, head * HD : (head + 1) * HD].astype(jnp.float32) * scale
            coarse = scaled.astype(jnp.bfloat16)
            query_scr[:, head * wide : head * wide + HD] = coarse
            query_scr[:, head * wide + HD : (head + 1) * wide] = (
                scaled - coarse.astype(jnp.float32)
            ).astype(jnp.bfloat16)

    def score(head, row, key_count, masked):
        q = query_scr[row : row + rows, head * wide : (head + 1) * wide]
        scores = lax.dot_general(
            key_scr[:key_count, :], q, (((1,), (1,)), ((), ())),
            preferred_element_type=jnp.float32,
        )
        if masked:
            last = scores[row:, :]
            key_at = lax.broadcasted_iota(jnp.int32, last.shape, 0)
            query_at = lax.broadcasted_iota(jnp.int32, last.shape, 1)
            last = jnp.where(key_at <= query_at, last, NEG_LARGE)
            scores = jnp.concatenate([scores[:row, :], last], axis=0) if row else last
        return scores

    def absorb(head, row, key_count, scores):
        at = slice(row, row + rows)
        old_max = max_scr[head, 0:1, at]
        new_max = jnp.maximum(old_max, jnp.max(scores, axis=0, keepdims=True))
        weights = jnp.exp2(scores - new_max).astype(jnp.bfloat16)
        shrink = jnp.exp2(old_max - new_max)
        acc_scr[head, :, at] = acc_scr[head, :, at] * shrink + jnp.dot(
            value_scr[:, :key_count], weights, preferred_element_type=jnp.float32
        )
        max_scr[head, :, at] = jnp.broadcast_to(new_max, (8, rows))

    def sweep(masked):
        work = [(head, row) for head in range(heads) for row in range(0, span, rows)]
        count = [row + rows if masked else span for _, row in work]
        ahead = score(*work[0], count[0], masked)
        for i, (head, row) in enumerate(work):
            scores = ahead
            if i + 1 < len(work):
                ahead = score(*work[i + 1], count[i + 1], masked)
            absorb(head, row, count[i], scores)

    @pl.when(diag_ref[step] == 0)
    def _():
        sweep(False)

    @pl.when(diag_ref[step] == 1)
    def _():
        sweep(True)

    @pl.when(last_ref[step] == 1)
    def _():
        for head in range(heads):
            for row in range(0, span, rows):
                at = slice(row, row + rows)
                ratio = acc_scr[head, :HD, at] / acc_scr[head, HD : HD + 1, at]
                out_ref[at, head * HD : (head + 1) * HD] = ratio.T.astype(out_ref.dtype)


def whole(shape):
    return pl.BlockSpec(
        shape, lambda j, core_ref: (0,) * len(shape), pipeline_mode=pl.Buffered(1)
    )


def shard_map_of(side, piece, first=0):
    return lambda j, core_ref: (
        0, (PAIR * (j + first) + (core_ref[0] + side) % PAIR) * PIECES + piece,
    )


def param_spec(count, width, piece, first):
    return pl.BlockSpec(
        (1, PARAM_ROWS, width),
        lambda j, core_ref: (lax.rem(core_ref[1] + count - (j + first), count), 0, piece),
    )


def plain(j, core_ref):
    return (0, j)


def run_pick(core, full, piece, width):
    half, inner = full.shape
    blocks = inner // (width * PIECES * PAIR)
    return pl.pallas_call(
        copy_kernel,
        grid_spec=pltpu.PrefetchScalarGridSpec(
            num_scalar_prefetch=1,
            grid=(blocks,),
            in_specs=[pl.BlockSpec((half, width), shard_map_of(1, piece))],
            out_specs=pl.BlockSpec((half, width), plain),
        ),
        out_shape=jax.ShapeDtypeStruct((half, blocks * width), full.dtype),
        name="pick_channels",
    )(core, full)


def run_place(core, full, part, piece, width, first):
    half, _ = full.shape
    blocks = part.shape[1] // width
    return pl.pallas_call(
        place_kernel,
        grid_spec=pltpu.PrefetchScalarGridSpec(
            num_scalar_prefetch=1,
            grid=(blocks,),
            in_specs=[pl.BlockSpec(memory_space=pl.ANY), pl.BlockSpec((half, width), plain)],
            out_specs=pl.BlockSpec((half, width), shard_map_of(1, piece, first)),
        ),
        out_shape=jax.ShapeDtypeStruct(full.shape, full.dtype),
        input_output_aliases={1: 0},
        name="place_channels",
    )(core, full, part)


def weight_spec(weight, width, shards, first):
    if weight.ndim == 4:
        parts, _, rows, _ = weight.shape
        return pl.BlockSpec((parts, 1, rows, width), lambda j, core_ref: (0, j + first, 0, 0))
    return pl.BlockSpec(
        (1, weight.shape[1], width),
        lambda j, core_ref: (lax.rem(core_ref[1] + shards - (j + first), shards), 0, 0),
    )


def run_scan(
    core, x_own, x_other, halo, low_own, low_other, weights, params, inject, read, piece, width, share,
    first, blocks,
):
    half = x_other.shape[0]
    cols = blocks * width
    tokens = 2 * half
    shards = params.shape[0]
    sources = len(weights)

    def shifted(j, core_ref):
        return (0, j + first)

    lanes = min(LANES, width)
    tiles = width // lanes
    return pl.pallas_call(
        functools.partial(scan_kernel, sources=sources),
        grid_spec=pltpu.PrefetchScalarGridSpec(
            num_scalar_prefetch=1,
            grid=(blocks,),
            in_specs=[
                pl.BlockSpec((half, width), shard_map_of(0, piece, first)),
                pl.BlockSpec((half, width), shifted),
                pl.BlockSpec((8, width), lambda j, core_ref: (0, piece * shards + j + first)),
                whole(low_own.shape),
                whole(low_other.shape),
                param_spec(shards, width, piece, first),
                whole(inject.shape),
                whole(read.shape),
            ]
            + [weight_spec(weight, width, shards, first) for weight in weights],
            out_specs=[
                pl.BlockSpec((tiles, tokens, lanes), lambda j, core_ref: (j, 0, 0)),
                pl.BlockSpec((tokens, width), plain),
                pl.BlockSpec((width // share, 2 * STATE, share), lambda j, core_ref: (j, 0, 0)),
            ],
            scratch_shapes=[
                pltpu.VMEM((tiles, tokens + 8, lanes), jnp.float32),
                pltpu.VMEM((tokens, width), jnp.float32),
                pltpu.VMEM((tiles, tokens, lanes), jnp.float32),
                pltpu.VMEM((GROUP * STATE, width), jnp.bfloat16),
                pltpu.VMEM((STATE, width), jnp.float32),
                pltpu.VMEM((8 * (CONV + 3), width), jnp.float32),
            ],
        ),
        out_shape=[
            jax.ShapeDtypeStruct((cols // lanes, tokens, lanes), jnp.float32),
            jax.ShapeDtypeStruct((tokens, cols), jnp.bfloat16),
            jax.ShapeDtypeStruct((cols // share, 2 * STATE, share), jnp.bfloat16),
        ],
        compiler_params=pltpu.CompilerParams(vmem_limit_bytes=VMEM_LIMIT),
        name="token_scan",
    )(core, x_own, x_other, halo, low_own, low_other, params, inject, read, *weights)


def run_correct(
    core, full, delta, y, enter, params, read, gate_own, gate_other, piece, width, first, inside, blocks
):
    tokens = y.shape[0]
    half, inner = gate_own.shape
    cols = blocks * width
    lanes = delta.shape[2]
    tiles = width // lanes
    share = enter.shape[2]
    resumed = full is not None
    first_spec = [pl.BlockSpec(memory_space=pl.ANY)] if resumed else []
    first_arg = (full,) if resumed else ()
    return pl.pallas_call(
        functools.partial(correct_kernel, resumed=resumed),
        grid_spec=pltpu.PrefetchScalarGridSpec(
            num_scalar_prefetch=1,
            grid=(blocks,),
            in_specs=first_spec
            + [
                pl.BlockSpec((tiles, tokens, lanes), lambda j, core_ref: (j + inside, 0, 0)),
                pl.BlockSpec((tokens, width), lambda j, core_ref: (0, j + inside)),
                pl.BlockSpec((width // share, STATE, share), lambda j, core_ref: (j + first, 0, 0)),
                param_spec(params.shape[0], width, piece, first),
                whole(read.shape),
                pl.BlockSpec((half, width), shard_map_of(0, piece, first)),
                pl.BlockSpec((half, width), lambda j, core_ref: (0, j + first)),
            ],
            out_specs=[
                pl.BlockSpec((half, width), shard_map_of(0, piece, first)),
                pl.BlockSpec((half, width), plain),
            ],
            scratch_shapes=[
                pltpu.VMEM((GROUP * STATE, width), jnp.bfloat16),
                pltpu.VMEM((tokens, width), jnp.float32),
                pltpu.VMEM((STATE, width), jnp.float32),
                pltpu.VMEM((STATE, width), jnp.bfloat16),
            ],
        ),
        out_shape=[
            jax.ShapeDtypeStruct((half, inner), jnp.bfloat16),
            jax.ShapeDtypeStruct((half, cols), jnp.bfloat16),
        ],
        input_output_aliases={1: 0} if resumed else {},
        compiler_params=pltpu.CompilerParams(vmem_limit_bytes=VMEM_LIMIT),
        name="state_correction",
    )(core, *first_arg, delta, y, enter, params, read, gate_own, gate_other)


def run_combine(order, got, rates):
    chunks, _, cols = got.shape
    return pl.pallas_call(
        combine_kernel,
        grid_spec=pltpu.PrefetchScalarGridSpec(
            num_scalar_prefetch=1,
            grid=(1,),
            in_specs=[
                pl.BlockSpec(got.shape, lambda i, o: (0, 0, 0)),
                pl.BlockSpec(rates.shape, lambda i, o: (0, 0)),
            ],
            out_specs=pl.BlockSpec((chunks, STATE, cols), lambda i, o: (0, 0, 0)),
        ),
        out_shape=jax.ShapeDtypeStruct((chunks, STATE, cols), jnp.bfloat16),
        compiler_params=pltpu.CompilerParams(vmem_limit_bytes=VMEM_LIMIT),
        name="state_combine",
    )(order, got, rates)


def run_flash(tables, q, kv_parts, rows=512):
    _, width = q.shape
    heads = width // HD
    steps = tables[0].shape[0]
    sources = len(kv_parts)

    def q_map(s, side, flip, half, diag, first, last):
        return (side[s], 0)

    def kv_map(s, side, flip, half, diag, first, last):
        return (half[s], 0)

    return pl.pallas_call(
        functools.partial(flash_kernel, heads=heads, rows=rows, sources=sources),
        grid_spec=pltpu.PrefetchScalarGridSpec(
            num_scalar_prefetch=6,
            grid=(steps,),
            in_specs=[pl.BlockSpec((SPAN, width), q_map)]
            + [pl.BlockSpec((SPAN, 2 * HD), kv_map)] * sources,
            out_specs=pl.BlockSpec((SPAN, width), q_map),
            scratch_shapes=[
                pltpu.VMEM((SPAN, 2 * width), jnp.bfloat16),
                pltpu.VMEM((SPAN, 2 * HD), jnp.bfloat16),
                pltpu.VMEM((HD + ONES, SPAN), jnp.bfloat16),
                pltpu.VMEM((heads, 8, SPAN), jnp.float32),
                pltpu.VMEM((heads, HD + ONES, SPAN), jnp.float32),
            ],
        ),
        out_shape=jax.ShapeDtypeStruct(q.shape, jnp.bfloat16),
        compiler_params=pltpu.CompilerParams(vmem_limit_bytes=VMEM_LIMIT),
        name="causal_attention",
    )(*tables, q, *kv_parts)


def flash_tables(span_order, my_blocks, blk):
    block_total = span_order.shape[0]
    places = jnp.arange(block_total, dtype=jnp.int32)
    holder = jnp.sum(jnp.where(span_order[None, :] == places[:, None], places[None, :], 0), axis=1)
    steps = jnp.arange(block_total + 1, dtype=jnp.int32)
    first_count = my_blocks[0] + 1
    side = (steps >= first_count).astype(jnp.int32)
    place = jnp.where(side == 1, steps - first_count, steps)
    limit = jnp.where(side == 1, my_blocks[1], my_blocks[0])
    block = jnp.sum(jnp.where(places[None, :] == place[:, None], holder[None, :], 0), axis=1)
    block = block.astype(jnp.int32)
    last = (place == limit).astype(jnp.int32)
    first = (place == 0).astype(jnp.int32)
    return (side, (block // 2) ^ blk.astype(jnp.int32), block % 2, last, first, last)


def local(
    mamba_input, gate_input, delta_low, state_mixers, conv_weight, conv_bias, delta_weight,
    delta_bias, decay_log, skip_gain, queries, key_rows, value_rows, span_order,
):
    blk = lax.axis_index("blk")
    chip = lax.axis_index("chip")
    core = lax.axis_index("core")
    blk_count = lax.axis_size("blk")
    chip_count = lax.axis_size("chip")
    ulys = ("chip", "core")
    chips = ("blk", "chip")
    ulys_count = chip_count * PAIR
    chunks = blk_count * chip_count
    block_total = span_order.shape[0]
    half, _ = mamba_input.shape
    tokens = PAIR * half
    shard_cols = delta_weight.shape[1]
    width = shard_cols // PIECES
    cols = chip_count * width
    swap = [(0, 1), (1, 0)]
    core_arr = jnp.stack([core, chip]).astype(jnp.int32)
    my_blocks = lax.dynamic_slice_in_dim(span_order, 2 * blk, 2, 0)

    depth = delta_weight.shape[0]
    part_rows = depth // blk_count
    part = lax.dynamic_slice_in_dim(delta_weight, blk * part_rows, part_rows, 0)
    far_moves = [
        [(i, (i + far) % chip_count) for i in range(chip_count)] for far in range(1, chip_count)
    ]
    flips = [[(i, i ^ flip) for i in range(blk_count)] for flip in range(1, blk_count)]
    part_first, part_later = part[:, :width], part[:, width:]
    shards_first = jnp.stack(
        [part_first] + [lax.ppermute(part_first, "chip", move) for move in far_moves]
    )

    def by_flip(low):
        return jnp.concatenate(
            [
                lax.dynamic_slice_in_dim(low, (blk ^ flip) * part_rows, part_rows, 1)
                for flip in range(blk_count)
            ],
            axis=1,
        )

    per_block = SPAN // tokens
    chunk_ids = jnp.arange(chunks, dtype=jnp.int32)
    stored = chunk_ids // per_block
    block_ids = jnp.arange(block_total, dtype=jnp.int32)
    block_pos = jnp.sum(
        jnp.where(stored[:, None] == block_ids[None, :], span_order[None, :], 0), axis=1
    )
    chunk_pos = block_pos * per_block + chunk_ids % per_block
    order = jnp.sum(
        jnp.where(chunk_pos[None, :] == chunk_ids[:, None], chunk_ids[None, :], 0), axis=1
    ).astype(jnp.int32)
    me = blk * chip_count + chip
    my_pos = jnp.sum(jnp.where(chunk_ids == me, chunk_pos, 0))
    last_rows = mamba_input[half - (CONV - 1) :].reshape(
        CONV - 1, chip_count, PAIR, PIECES, width
    )

    def columns_of(side):
        mine = lax.dynamic_index_in_dim(last_rows, side, 2, False)
        return mine.swapaxes(1, 2).reshape(CONV - 1, PIECES * cols)

    tail = jnp.where(
        core == 1, columns_of(core), lax.ppermute(columns_of(1 - core), "core", swap)
    )
    tails = lax.all_to_all(
        jnp.broadcast_to(tail[None], (chunks, CONV - 1, PIECES * cols)), chips,
        split_axis=0, concat_axis=0, tiled=True,
    )
    before = (chunk_pos == my_pos - 1).astype(jnp.bfloat16)
    halo = jnp.einsum("m,mkc->kc", before, tails, preferred_element_type=jnp.float32)
    halo = jnp.concatenate(
        [jnp.zeros((8 - (CONV - 1), PIECES * cols), jnp.bfloat16), halo.astype(jnp.bfloat16)],
        axis=0,
    )

    kv_heads = key_rows.shape[1] // HD
    repeat = ulys_count // kv_heads
    kv_rows = jnp.stack(
        [key_rows.reshape(half, kv_heads, HD), value_rows.reshape(half, kv_heads, HD)], axis=2
    )
    kv_rows = jnp.broadcast_to(
        kv_rows[:, :, None], (half, kv_heads, repeat, 2, HD)
    ).reshape(half, ulys_count * 2 * HD)
    kv_rows, halo = lax.optimization_barrier((kv_rows, halo))
    shards_first, part_later = lax.optimization_barrier((shards_first, part_later))
    weights_later = lax.all_gather(part_later, chips, axis=0, tiled=False)
    weights_first = [shards_first] + [
        lax.ppermute(shards_first, "blk", move) for move in flips
    ]
    weights_later = [weights_later.reshape(blk_count, chip_count, part_rows, width)]
    kv_local = lax.all_to_all(kv_rows, ulys, split_axis=1, concat_axis=0, tiled=True)

    packed = jnp.concatenate(
        [
            decay_log,
            conv_weight.astype(jnp.float32),
            conv_bias[None],
            delta_bias[None],
            skip_gain[None],
            jnp.zeros((1, shard_cols), jnp.float32),
        ],
        axis=0,
    )

    def picked(full, piece):
        return run_pick(core_arr, full, piece, width)

    x_other = [
        lax.ppermute(picked(mamba_input, piece), "core", swap)
        for piece in range(PIECES)
    ]
    low_other = lax.ppermute(delta_low, "core", swap)
    mixers_other = lax.ppermute(state_mixers, "core", swap)
    mixers = jnp.where(
        core == 0,
        jnp.concatenate([state_mixers, mixers_other], axis=0),
        jnp.concatenate([mixers_other, state_mixers], axis=0),
    )
    inject = jnp.broadcast_to(
        mixers[:, :STATE].astype(jnp.float32).reshape(tokens * STATE, 1), (tokens * STATE, LANES)
    )
    same = jnp.arange(tokens, dtype=jnp.int32)[:, None] % GROUP == jnp.arange(GROUP, dtype=jnp.int32)
    read = jnp.where(
        same[:, :, None], mixers[:, None, STATE:], jnp.zeros((), jnp.bfloat16)
    ).reshape(tokens, GROUP * STATE)

    gate_other = [
        lax.ppermute(picked(gate_input, piece), "core", swap)
        for piece in range(PIECES)
    ]

    params = jnp.stack([packed] + [lax.ppermute(packed, "chip", move) for move in far_moves])

    share = cols // chunks

    def scan_part(piece, x_piece, lows, weights, first, blocks):
        return run_scan(
            core_arr, mamba_input, x_piece, halo, *lows, weights, params, inject, read, piece,
            width, share, first, blocks,
        )

    def rates_of(piece):
        at = me * share
        shard = at // width
        far = (chip + chip_count - shard) % chip_count
        mine = lax.dynamic_slice(
            params, (far, 0, piece * width + at % width), (1, STATE, share)
        )
        return -LOG2E * jnp.exp(mine[0])

    my_rates = [rates_of(piece) for piece in range(PIECES)]

    def to_owners(array):
        return lax.all_to_all(array, chips, split_axis=0, concat_axis=0, tiled=True)

    def correct_part(full, made, enter, piece, first, inside, blocks):
        delta, y = made[:2]
        return run_correct(
            core_arr, full, delta, y, enter, params, read, gate_input, gate_other[piece], piece,
            width, first, inside, blocks,
        )

    lows_first = (by_flip(delta_low), by_flip(low_other))
    lows_later = (delta_low, low_other)
    tables = flash_tables(span_order, my_blocks, blk)
    gate_other, inject, read, params, my_rates, tables, order, lows_first, x_other = (
        lax.optimization_barrier(
            (gate_other, inject, read, params, my_rates, tables, order, lows_first, x_other)
        )
    )
    made_0 = scan_part(0, x_other[0], lows_first, weights_first, 0, chip_count)
    x_now, sent_0, queries, kv_local = lax.optimization_barrier(
        (x_other[1], made_0[2], queries, kv_local)
    )
    q_local = lax.all_to_all(queries, ulys, split_axis=1, concat_axis=0, tiled=True)
    kv_parts = [kv_local] + [lax.ppermute(kv_local, "blk", move) for move in flips]
    made_1 = scan_part(1, x_now, lows_later, weights_later, 0, chip_count)
    sent, q_local = lax.optimization_barrier(
        (jnp.concatenate([sent_0, made_1[2]], axis=2), q_local)
    )
    got = to_owners(sent)
    attended = run_flash(tables, q_local, kv_parts)
    got, attended = lax.optimization_barrier((got, attended))
    enter = to_owners(run_combine(order, got, jnp.concatenate(my_rates, axis=1)))
    enter, attended = lax.optimization_barrier((enter, attended))
    attention_output = lax.all_to_all(attended, ulys, split_axis=0, concat_axis=1, tiled=True)
    full, theirs_0 = correct_part(None, made_0, enter[:, :, :share], 0, 0, 0, chip_count)
    back_0 = lax.ppermute(theirs_0, "core", swap)
    full, theirs_1 = correct_part(full, made_1, enter[:, :, share:], 1, 0, 0, chip_count)
    back_1 = lax.ppermute(theirs_1, "core", swap)
    full = run_place(core_arr, full, back_0, 0, width, 0)
    mamba_output = run_place(core_arr, full, back_1, 1, width, 0)
    return (mamba_output, attention_output)


def solution(mesh):
    blk_count = mesh.shape["blk"]
    ulys_count = mesh.shape["ulys"]
    fine = Mesh(
        mesh.devices.reshape(blk_count, ulys_count // PAIR, PAIR), ("blk", "chip", "core")
    )
    rows = P(("blk", "chip", "core"), None)
    col = ("chip", "core")
    placed = (
        rows, rows, rows, rows,
        P(None, col), P(col), P(None, col), P(col), P(None, col), P(col),
        rows, rows, rows,
        P(),
    )

    return jax.shard_map(local, mesh=fine, in_specs=placed, out_specs=(rows, rows), check_vma=False)
```
